32 devices in a mesh: row: 8 (over y, x, core), col: 4 (over z).
Axes of the slice: x: 2, y: 2, z: 4, core: 2. Of those that a mesh axis runs over, the one named last changes fastest.
Arguments:
- vector: float32 [4096, 4096], P('row', 'col'), may hold values from -6 to 6
- one_electron: float32 [16, 16], replicated, may hold values from -0.18 to 0.18
- links: int32 [32, 8], replicated, may hold values from 0 to 31, as said below
- counts: int32 [32], replicated, may hold values from 4 to 8, as said below
- pairs: int32 [32, 8], P('row'), may hold values from 0 to 255
- signs: int32 [32, 8, 128, 128], P('row'), may hold values from -1 to 1
Outputs:
- sigma_vector: float32 [4096, 4096], P('row', 'col')
The draws below stay inside these ranges and needn't reach their ends.
Inputs may be any that keep to these rules, and one draw needn't show every extreme that they name: `links`: entries name string blocks; only the first counts[I] entries of block I are used. Counting used entries only, the blocks I with I // 4 = d name blocks K with K // 4 = s at most 4 times for any d and s, and some pair d, s reaches 4. Block I has counts[I] used links; every block I with I % 4 = 0 has 8.
All inputs are finite; a program needn't handle non-finite values.
Results may differ from the reference program's by a relative error of at most 0.000051.
Values sent between devices are 32-bit elements; how exact they have to be, the bound alone decides.
A program may use at most 128 MiB of HBM per device.

```python
import jax
import jax.numpy as jnp
from jax import lax

BLK = 128
NORB = 16
LMAX = 8
A_DEV = 4
NPAIR = 256
NBLK_A = 32
NA = 4096


def link_tables(key, salt, blocks_all, blocks_dev, link_max):
    key = jax.random.fold_in(key, salt)
    count_key, order_key, local_key = jax.random.split(key, 3)
    devices = blocks_all // blocks_dev
    slot_width = blocks_dev * link_max
    capacity = (slot_width + devices - 1) // devices
    used = jax.random.randint(count_key, (blocks_all,), link_max // 2, link_max + 1)
    first_block = jnp.arange(blocks_all, dtype=jnp.int32) % blocks_dev == 0
    used = jnp.where(first_block, link_max, used).astype(jnp.int32)
    in_use = (jnp.arange(link_max, dtype=jnp.int32)[None, :] < used[:, None]).reshape(devices, slot_width)
    position = jnp.cumsum(in_use.astype(jnp.int32), axis=1) - 1
    position = jnp.clip(position, 0, slot_width - 1)

    def one_order(order_seed):
        return jax.random.permutation(order_seed, devices)
    orders = jax.vmap(one_order)(jax.random.split(order_key, devices)).astype(jnp.int32)
    sources = jnp.take_along_axis(orders, position // capacity, axis=1)
    local_block = jax.random.randint(local_key, (devices, slot_width), 0, blocks_dev)
    link_table = (sources * blocks_dev + local_block).reshape(blocks_all, link_max)
    return (link_table.astype(jnp.int32), used)


def draw_links(key, part):
    return link_tables(key, 11, NBLK_A, A_DEV, LMAX)[0]


def draw_counts(key, part):
    return link_tables(key, 11, NBLK_A, A_DEV, LMAX)[1]


def with_ends(result, key, low, largest):
    longest = result.shape.index(max(result.shape))
    spots = []
    for shift in (0, 1):
        where = [jax.random.randint(jax.random.fold_in(key, axis), (), 0, length) for axis, length in enumerate(result.shape)]
        where[longest] = (where[longest] + shift) % result.shape[longest]
        spots.append(tuple(where))
    return result.at[spots[0]].set(low).at[spots[1]].set(largest)


def steps_of(stream_key, dims, shards, least, largest):
    level, own = 1.0, jax.random.fold_in(stream_key, 6)
    for dim, blocks in shards:
        steps = jnp.exp(jax.random.uniform(jax.random.fold_in(own, dim), (blocks,), jnp.float32, least / len(shards), largest / len(shards)))
        level = level * jnp.repeat(steps, dims[dim] // blocks).reshape([-1 if axis == dim else 1 for axis in range(len(dims))])
    return level


def noise(stream_key, shape, scale, reach, shards=(), held_as=jnp.bfloat16):
    result = scale * jax.random.normal(stream_key, shape, jnp.float32)
    if shards:
        result = result * steps_of(stream_key, shape, shards, -0.22, 0.18)
    return jnp.clip(result, -reach, reach).astype(held_as)


def setup_inputs(seed: int = 0) -> dict:
    seeds = jax.random.split(jax.random.key(seed), 7)
    return {
        "vector": noise(seeds[0], (NA, NA), 1.0, 6.0, ((0, 8), (1, 4)), jnp.float32),
        "one_electron": noise(seeds[1], (NORB, NORB), 0.03, 0.18, (), jnp.float32),
        "links": draw_links(jax.random.fold_in(seeds[6], 71), 0),
        "counts": draw_counts(jax.random.fold_in(seeds[6], 71), 0),
        "pairs": with_ends(jax.random.randint(seeds[4], (NBLK_A, LMAX), 0, NPAIR), jax.random.fold_in(seeds[4], 1), 0, NPAIR - 1).astype(jnp.int32),
        "signs": with_ends(jax.random.randint(seeds[5], (NBLK_A, LMAX, BLK, BLK), -1, 2), jax.random.fold_in(seeds[5], 1), -1, 1).astype(jnp.int32),
    }


def pair_values(pair_ids, used, integrals):
    flat_table = integrals.reshape(-1)
    values = flat_table[pair_ids]
    in_use = jnp.arange(pair_ids.shape[1], dtype=jnp.int32)[None, :] < used[:, None]
    return jnp.where(in_use, values, jnp.zeros_like(values))


def reference(vector, one_electron, links, counts, pairs, signs):
    replace = pair_values(pairs, counts, one_electron)[:, :, None, None] * signs.astype(jnp.float32)
    row_tiles = vector.reshape(NBLK_A, BLK, NA)
    column_blocks = vector.reshape(NA, NBLK_A, BLK)

    def alpha_block(inputs):
        link_row, replace_row = inputs
        fetched = row_tiles[link_row]
        return jnp.einsum("lmk,lkb->mb", replace_row, fetched, precision=lax.Precision.HIGHEST)

    def beta_block(inputs):
        link_row, replace_row = inputs
        fetched = column_blocks[:, link_row, :]
        return jnp.einsum("alk,lmk->am", fetched, replace_row, precision=lax.Precision.HIGHEST)

    sigma_alpha = lax.map(alpha_block, (links, replace)).reshape(NA, NA)
    sigma_beta = lax.map(beta_block, (links, replace))
    sigma_beta = jnp.transpose(sigma_beta, (1, 0, 2)).reshape(NA, NA)
    return sigma_alpha + sigma_beta
```

```python
import functools

import jax
import jax.numpy as jnp
from jax import lax
from jax.experimental import pallas as pl
from jax.experimental.pallas import tpu as pltpu
from jax.sharding import PartitionSpec as P

MESH = pl.DeviceIdType.MESH
PARTS_A = 4
PIECES = 4
EARLY = 2
TILE = 45.0
HOP = 1.5
PIECE = 5.6


def split(value):
    high = value.astype(jnp.bfloat16)
    low = (value - high.astype(jnp.float32)).astype(jnp.bfloat16)
    return high, low


def row_parts(high, cols):
    helps = cols >= 4
    quarter, eighth, last = high // 4, high // 8, high // 16
    return [(quarter, False), (quarter, False), (quarter, helps), (eighth, helps), (last, helps), (last, helps)]


def row_chunks(high, cols):
    chunks, first = [], 0
    for part, (height, helped) in enumerate(row_parts(high, cols)):
        piece = min(height, high // 8)
        for offset in range(0, height, piece):
            chunks.append((part, offset, piece, first + offset, helped))
        first += height
    return chunks


def kernel(rows, cols, blocks, link_max, links, counts, integrals, pairs, v, tab, out, *scratch):
    size = tab.shape[1]
    high, width = out.shape
    parts = row_parts(high, cols)
    chunks = row_chunks(high, cols)
    firsts = [sum(p[0] for p in parts[:i]) for i in range(len(parts))]
    scratch = list(scratch)
    colbuf = [scratch.pop(0) for _ in range(PARTS_A)]
    rowbuf = [scratch.pop(0) for _ in parts]
    (own_tab, beta_tab, help_tab, alpha_signs, beta_signs, help_signs, shared,
     pairs_v, pairs_s, alpha_coef, beta_coef, help_coef, ssem, rsem, lsem) = scratch

    wide = width // PARTS_A
    spread = rows // cols
    blocks_b = blocks * spread
    tables = blocks * link_max
    chips = rows // 2
    reach = chips // 2
    across = chips // 2
    half = blocks // 2
    piece = tables // (2 * PIECES)
    helps = cols >= 4

    r = lax.axis_index("row")
    c = lax.axis_index("col")
    core = lax.rem(r, 2)
    chip = r // 2
    other = r + 1 - 2 * core
    place = jnp.where(chip < across, chip, chips - 1 - (chip - across))

    def chip_at(position):
        position = lax.rem(position + 2 * chips, chips)
        return jnp.where(position < across, position, across + (chips - 1 - position))

    def row_at(position, k):
        return 2 * chip_at(position) + k

    right = (row_at(place + 1, core), c)
    left = (row_at(place - 1, core), c)
    partner = (other, c)
    up = (r, jnp.minimum(c + 1, cols - 1))
    down = (r, jnp.maximum(c - 1, 0))
    has_up = c < cols - 1
    has_down = c > 0
    at_end = (c == 0) | (c == cols - 1)
    inner = jnp.logical_not(at_end)
    helper = (c == 1) | (c == cols - 2)
    aided = jnp.where(c == 1, 0, cols - 1)
    inward = (r, jnp.where(c == 0, 1, cols - 2))

    ids = {}

    def number(*key):
        return ids.setdefault(key, len(ids))

    pending = []

    def describe(src, dst, key, device):
        return pltpu.make_async_remote_copy(
            src_ref=src, dst_ref=dst, send_sem=ssem.at[number(*key)], recv_sem=rsem.at[number(*key)],
            device_id=device, device_id_type=MESH)

    def when(cond, action):
        if cond is None:
            action()
        else:
            pl.when(cond)(action)

    def send(src, dst, key, device, cond=None, drain=True):
        copy = describe(src, dst, key, device)
        if drain:
            pending.append((cond, copy))
        when(cond, copy.start)

    def arrive(ref, key, cond=None):
        when(cond, describe(ref, ref, key, partner).wait_recv)

    local = []

    def load(src, dst, cond=None):
        copy = pltpu.make_async_copy(src, dst, lsem.at[len(local)])
        local.append(copy)
        when(cond, copy.start)
        return lambda: when(cond, copy.wait)

    plan = []

    def at(time, action):
        plan.append((time, len(plan), action))

    barrier = pltpu.get_barrier_semaphore()
    for k in range(1, rows):
        pl.semaphore_signal(barrier, inc=1, device_id=(lax.rem(r + k, rows), c), device_id_type=MESH)

    @pl.when(has_up)
    def _():
        pl.semaphore_signal(barrier, inc=1, device_id=up, device_id_type=MESH)

    @pl.when(has_down)
    def _():
        pl.semaphore_signal(barrier, inc=1, device_id=down, device_id_type=MESH)

    wait_tab = load(tab, own_tab)
    wait_pairs = load(pairs, pairs_v.at[r])

    def load_rows(i):
        sem = lsem.at[len(local)]
        first = firsts[i]
        for k in range(blocks_b):
            pltpu.make_async_copy(
                v.at[first // size, pl.ds(first % size, parts[i][0]), pl.ds(k * size, size)],
                rowbuf[i].at[c * blocks_b + k], sem).start()
        ref = rowbuf[i].at[pl.ds(c * blocks_b, blocks_b)]
        local.append(pltpu.make_async_copy(ref, ref, sem))
        return local[-1].wait

    wait_rows = [load_rows(i) for i in range(len(parts))]
    wait_cols = [load(v.at[:, :, pl.ds(j * wide, wide)], colbuf[j].at[pl.ds(r * blocks, blocks)])
                 for j in range(PARTS_A)]

    pl.semaphore_wait(barrier, rows - 1 + has_up.astype(jnp.int32) + has_down.astype(jnp.int32))

    for k in range(1, rows):
        send(pairs, pairs_v.at[r], ("pairs", k), (lax.rem(r + k, rows), c))

    reach_up = {1: up, -1: down}

    def ends(k):
        return TILE * (chunks[k][3] + chunks[k][2]) / high

    def arrival(t, k, late):
        far = max(cols - 3, 1)
        tiles = max(1, min(t, far)) if late else min(t, far)
        return ends(k) + TILE * tiles + 3.0 * t + HOP * (t + 1)

    def row_chunk(k, tile):
        part, offset, count, _, _ = chunks[k]
        return rowbuf[part].at[pl.ds(tile * blocks_b, blocks_b), pl.ds(offset, count), :]

    def line_own(k, way, cond):
        helped = chunks[k][4]
        position = c if way == 1 else cols - 1 - c
        limit = cols - 2 if helped else cols - 1
        ref = row_chunk(k, c)
        send(ref, ref, ("line", way, k, 0), reach_up[way], cond & (position < limit))

    def line_arrive(k, way, t, edge):
        helped = chunks[k][4]
        last = cols - 2 if helped else cols - 1
        position = c if way == 1 else cols - 1 - c
        if edge:
            if t + 1 > last:
                return
            cond = position == t + 1
        else:
            if t + 2 > last:
                return
            cond = (position > t + 1) & (position <= last)
        ref = row_chunk(k, jnp.clip(c - way * (1 + t), 0, cols - 1))
        arrive(ref, ("line", way, k, t), cond)
        if edge:
            if t + 2 <= last:
                send(ref, ref, ("line", way, k, t + 1), reach_up[way], cond)
        elif t + 3 <= last:
            send(ref, ref, ("line", way, k, t + 1), reach_up[way], cond & (position < last))

    def table_places(s):
        source = c * spread + s
        source_chip = source // 2
        source_place = jnp.where(
            source_chip < across, source_chip, chips - 1 - (source_chip - across))
        distance = lax.rem(place - source_place + chips, chips)
        return lax.rem(source, 2), (distance, lax.rem(chips - distance, chips))

    ring = (right, left)

    def table_part(h, q):
        return pl.ds((h * PIECES + q) * piece, piece)

    def table_stage(s, h, q, d):
        source_core, hops = table_places(s)
        here = (core == source_core) & (hops[h] == d)
        part = table_part(h, q)
        ref = beta_tab.at[s, part]
        src = ref if d else tab.at[part]
        if d:
            arrive(ref, ("table", s, h, q), here)
        if d + 1 < chips:
            send(src, ref, ("table", s, h, q), ring[h], here, drain=False)
        send(src, ref, ("tableP", s, h, q), partner, here, drain=False)
        if helps:
            send(src, help_tab.at[s, part], ("help", s, h, q), inward, here & at_end, drain=False)

    def table_drain(s, h, q):
        source_core, hops = table_places(s)
        mine = core == source_core
        ref = beta_tab.at[s, table_part(h, q)]
        pending.append((mine & (hops[h] < chips - 1), describe(ref, ref, ("table", s, h, q), partner)))
        pending.append((mine, describe(ref, ref, ("tableP", s, h, q), partner)))
        if helps:
            pending.append((mine & at_end, describe(ref, ref, ("help", s, h, q), partner)))

    def table_finish():
        for s in range(spread):
            source_core, _ = table_places(s)
            for h in range(2):
                for q in range(PIECES):
                    arrive(beta_tab.at[s, table_part(h, q)], ("tableP", s, h, q), core != source_core)
            table_loads[s]()

    def help_arrive(s, h, q):
        source_core = table_places(s)[0]
        aided_core = lax.rem(aided * spread + s, 2)
        ref = help_tab.at[s, table_part(h, q)]
        arrive(ref, ("help", s, h, q), helper & (core == aided_core))
        send(ref, ref, ("helpP", s, h, q), partner, helper & (core == aided_core))

    def help_finish():
        for s in range(spread):
            aided_core = lax.rem(aided * spread + s, 2)
            for h in range(2):
                for q in range(PIECES):
                    arrive(help_tab.at[s, table_part(h, q)], ("helpP", s, h, q),
                           helper & (core != aided_core))

    def widen(source, base, target):
        @pl.loop(0, tables)
        def _(index):
            values = source[index].astype(jnp.float32).astype(jnp.bfloat16)
            target[base + index] = jnp.concatenate([values, values], axis=1)

    def widen_all(source, target):
        for s in range(spread):
            widen(source.at[s], s * tables, target)

    def tile_half(j, hb, position, k):
        return colbuf[j].at[pl.ds(row_at(position, k) * blocks + hb * half, half)]

    def ring_own(j, hb, way, cond, drain):
        ref = colbuf[j].at[pl.ds(r * blocks + hb * half, half)]
        src = v.at[pl.ds(hb * half, half), :, pl.ds(j * wide, wide)]
        send(src, ref, ("ring", way, j, hb, 0), ring[way], cond, drain=False)
        if drain:
            pending.append((None, describe(ref, ref, ("ring", way, j, hb, 0), partner)))

    def carried(way, hb, t):
        return t < reach - 1 or hb == way

    def ring_arrive(j, hb, way, t):
        ref = tile_half(j, hb, place - 1 - t if way == 0 else place + 1 + t, core)
        arrive(ref, ("ring", way, j, hb, t))
        if t + 1 < reach and carried(way, hb, t + 1):
            send(ref, ref, ("ring", way, j, hb, t + 1), ring[way])
        send(ref, ref, ("ringP", way, j, hb, t), partner)

    def ring_finish(j):
        wait_cols[j]()
        arrive(colbuf[j].at[pl.ds(other * blocks, blocks)], ("own", j))
        for t in range(reach):
            for way in range(2):
                for hb in range(2):
                    if carried(way, hb, t):
                        position = place - 1 - t if way == 0 else place + 1 + t
                        arrive(tile_half(j, hb, position, 1 - core), ("ringP", way, j, hb, t))

    def coefficients(target, first, count):
        @pl.loop(0, count)
        def _(b):
            block = first + b
            for l in range(link_max):
                pair = pairs_s[lax.div(block, blocks), lax.rem(block, blocks), l]
                norb = integrals.shape[0]
                value = integrals[lax.div(pair, norb), lax.rem(pair, norb)]
                target[b, l] = value * jnp.clip(counts[block] - l, 0, 1).astype(jnp.float32)

    def gather_pairs():
        wait_pairs()
        for k in range(1, rows):
            arrive(pairs_v.at[lax.rem(r - k + rows, rows)], ("pairs", k))
        copy = pltpu.make_async_copy(pairs_v, pairs_s, lsem.at[1])
        copy.start()
        copy.wait()
        coefficients(alpha_coef, r * blocks, blocks)
        coefficients(beta_coef, c * blocks_b, blocks_b)
        if helps:
            coefficients(help_coef, aided * blocks_b, blocks_b)

    def alpha_compute(j):
        @pl.loop(0, blocks)
        def _(block):
            total = jnp.zeros((size, wide), jnp.float32)
            for l in range(link_max):
                source = links[l, r * blocks + block]
                up_part, low_part = split(colbuf[j][source] * alpha_coef[block, l])
                total = total + jnp.dot(
                    alpha_signs[block * link_max + l], jnp.concatenate([up_part, low_part], axis=0),
                    preferred_element_type=jnp.float32)
            where = (pl.ds(pl.multiple_of(block * size, size), size), pl.ds(j * wide, wide))
            out[where] = out[where] + total

    def beta_compute(group, owner, coef, signs, target, start, add):
        count = sum(parts[i][0] for i in group)

        @pl.loop(0, blocks_b)
        def _(block):
            total = jnp.zeros((count, size), jnp.float32)
            for l in range(link_max):
                source = links[l, owner * blocks_b + block]
                value = jnp.concatenate([rowbuf[i][source] for i in group], axis=0)
                up_part, low_part = split(value * coef[block, l])
                total = total + lax.dot_general(
                    jnp.concatenate([up_part, low_part], axis=1), signs[block * link_max + l],
                    (((1,), (1,)), ((), ())), preferred_element_type=jnp.float32)
            where = (pl.ds(start, count), pl.ds(pl.multiple_of(block * size, size), size))
            if add:
                total = target[where] + total
            target[where] = total

    shared_first = sum(height for height, helped in parts if not helped)

    def own_beta(i, cond):
        def action():
            beta_compute([i], c, beta_coef, beta_signs, out, firsts[i], True)
        when(cond, action)

    def help_beta(i):
        @pl.when(helper)
        def _():
            beta_compute([i], aided, help_coef, help_signs, shared, firsts[i] - shared_first, False)

        ref = shared.at[pl.ds(firsts[i] - shared_first, parts[i][0])]
        send(ref, ref, ("sums", i), (r, aided), helper)

    def take_sums(i):
        ref = shared.at[pl.ds(firsts[i] - shared_first, parts[i][0])]
        arrive(ref, ("sums", i), at_end)

        @pl.when(at_end)
        def _():
            where = pl.ds(firsts[i], parts[i][0])
            out[where, :] = out[where, :] + ref[...]

    table_loads = []

    def begin():
        for s in range(spread):
            source_core, hops = table_places(s)
            table_loads.append(load(tab, beta_tab.at[s], (core == source_core) & (hops[0] == 0)))
        always = jnp.bool_(True)
        for k in range(len(chunks)):
            if chunks[k][1] == 0:
                wait_rows[chunks[k][0]]()
            early = always if k < EARLY or not helps else inner
            line_own(k, 1, early if k < EARLY or not helps else has_down)
            line_own(k, -1, early if k < EARLY or not helps else has_up)

    at(-2.0, begin)

    def rest():
        for k in range(EARLY, len(chunks)):
            line_own(k, 1, c == 0)
            line_own(k, -1, c == cols - 1)

    stage_last = PIECE * (PIECES - 1 + chips - 1) + HOP * (chips - 1)
    if helps:
        at(stage_last + 0.1, rest)

    for k in range(len(chunks)):
        for t in range(cols - 1):
            for edge in (False, True):
                late = edge and k >= EARLY and helps
                for way in (1, -1):
                    at(arrival(t, k, late), functools.partial(line_arrive, k, way, t, edge))

    for q in range(PIECES):
        for d in range(chips):
            for h in range(2):
                for s in range(spread):
                    time = -1.0 if d == 0 else PIECE * (q + d) + HOP * d
                    at(time, functools.partial(table_stage, s, h, q, d))
    at(stage_last + 3.5, table_finish)
    at(stage_last + 3.6, lambda: widen_all(beta_tab, beta_signs))

    if helps:
        helped_last = 0.0
        for q in range(PIECES):
            for h in range(2):
                time = 6.0 + max(TILE / 4 + PIECE * (2 * q + h + 1), PIECE * (q + chips) + HOP * (chips + 1))
                helped_last = max(helped_last, time)
                for s in range(spread):
                    at(time, functools.partial(help_arrive, s, h, q))
        at(helped_last + 1.5, help_finish)
        at(helped_last + 1.6, lambda: pl.when(helper)(lambda: widen_all(help_tab, help_signs)))

    order = []
    for j in range(PARTS_A):
        order.append((j, 0))
        if j:
            order.append((j - 1, 1))
    order.append((PARTS_A - 1, 1))
    step = TILE / (2 * PARTS_A)

    classes = []
    for h in range(2):
        kind = jnp.int32(chips - 1)
        for s in range(spread):
            source_core, hops = table_places(s)
            kind = jnp.where(core == source_core, hops[h], kind)
        classes.append(kind)

    begun = PIECE * PIECES
    for a, (j, second) in enumerate(order):
        for way in range(2):
            hb = (1 - way) if second else way
            for d in range(chips):
                if d == chips - 1:
                    time = max(0.0, 1.5 * step * a - 9.0)
                elif a < d:
                    time = 0.0
                else:
                    last = PIECE * (PIECES - 1 + d) + HOP * d if d else 0.0
                    time = max(last + 0.05, PIECE * (PIECES + d) + HOP * d + 1.5 * step * (a - d) - 9.0)
                at(time, functools.partial(ring_own, j, hb, way, classes[way] == d, d == 0))
            time = begun + 1.5 * step * a + step + HOP + 1.0
            for t in range(reach):
                if carried(way, hb, t):
                    at(time + 10.0 * t, functools.partial(ring_arrive, j, hb, way, t))

    def own_pass(j):
        ref = colbuf[j].at[pl.ds(r * blocks, blocks)]
        send(v.at[:, :, pl.ds(j * wide, wide)], ref, ("own", j), partner)

    for j in range(PARTS_A):
        at(0.5, functools.partial(own_pass, j))
        first = begun + 1.5 * step * order.index((j, 0)) + step + HOP + 1.0 + 10.0 * (reach - 1)
        second = begun + 1.5 * step * order.index((j, 1)) + step + HOP + 1.0 + 10.0 * max(reach - 2, 0)
        at(max(first, second) + 3.0, functools.partial(ring_finish, j))
        at(max(first, second) + 3.0, functools.partial(alpha_compute, j))

    def prepare():
        out[...] = jnp.zeros_like(out)
        gather_pairs()
        wait_tab()
        widen(own_tab, 0, alpha_signs)

    at(0.6, prepare)

    for i, (height, helped) in enumerate(parts):
        ks = [k for k, chunk in enumerate(chunks) if chunk[0] == i]
        late = helps and ks[-1] >= EARLY
        done = arrival(max(cols - 3, 0), ks[-1], late) + 0.1
        done_end = arrival(cols - 2, ks[-1], late) + 0.1
        if helped:
            at(done, functools.partial(help_beta, i))
            at(done, functools.partial(own_beta, i, inner))
            at(done_end + 12.0, functools.partial(take_sums, i))
        elif helps:
            at(done, functools.partial(own_beta, i, inner))
            at(done_end, functools.partial(own_beta, i, at_end))
        else:
            at(done_end, functools.partial(own_beta, i, None))

    for _, _, action in sorted(plan, key=lambda entry: entry[:2]):
        action()

    for s in range(spread):
        for h in range(2):
            for q in range(PIECES):
                table_drain(s, h, q)
    for cond, copy in pending:
        when(cond, copy.wait_send)


def local(vector, one_electron, links, counts, pairs, signs, rows, cols):
    blocks, link_max = pairs.shape
    size = signs.shape[2]
    high, width = vector.shape
    spread = rows // cols
    tables = blocks * link_max
    parts = row_parts(high, cols)
    helped = sum(height for height, aided in parts if aided)
    reach = rows // 4
    messages = rows - 1 + 2 * len(row_chunks(high, cols)) * (cols - 1)
    messages += PARTS_A * (1 + 8 * reach) + spread * 2 * PIECES * 4 + len(parts)
    scratch = [pltpu.VMEM((rows * blocks, size, width // PARTS_A), jnp.float32)] * PARTS_A
    scratch += [pltpu.VMEM((cols * blocks * spread, height, size), jnp.float32) for height, _ in parts]
    scratch += [
        pltpu.VMEM((tables, size, size), jnp.int32),
        pltpu.VMEM((spread, tables, size, size), jnp.int32),
        pltpu.VMEM((spread, tables, size, size), jnp.int32),
        pltpu.VMEM((tables, size, 2 * size), jnp.bfloat16),
        pltpu.VMEM((spread * tables, size, 2 * size), jnp.bfloat16),
        pltpu.VMEM((spread * tables, size, 2 * size), jnp.bfloat16),
        pltpu.VMEM((max(helped, 8), width), jnp.float32),
        pltpu.VMEM((rows, blocks, link_max), jnp.int32),
        pltpu.SMEM((rows, blocks, link_max), jnp.int32),
        pltpu.SMEM((blocks, link_max), jnp.float32),
        pltpu.SMEM((blocks * spread, link_max), jnp.float32),
        pltpu.SMEM((blocks * spread, link_max), jnp.float32),
        pltpu.SemaphoreType.DMA((messages,)),
        pltpu.SemaphoreType.DMA((messages,)),
        pltpu.SemaphoreType.DMA((2 + len(parts) + PARTS_A + spread,)),
    ]
    smem = pl.BlockSpec(memory_space=pltpu.SMEM)
    anywhere = pl.BlockSpec(memory_space=pl.ANY)
    return pl.pallas_call(
        functools.partial(kernel, rows, cols, blocks, link_max),
        out_shape=jax.ShapeDtypeStruct(vector.shape, jnp.float32),
        in_specs=[smem, smem, smem, anywhere, anywhere, anywhere],
        out_specs=pl.BlockSpec(memory_space=pltpu.VMEM),
        scratch_shapes=scratch,
        compiler_params=pltpu.CompilerParams(
            collective_id=0, has_side_effects=True, vmem_limit_bytes=60 << 20),
    )(links.T, counts, one_electron, pairs, vector.reshape(blocks, size, width),
      signs.reshape(tables, size, size))


def solution(mesh):
    in_specs = (P("row", "col"), P(), P(), P(), P("row", None), P("row", None, None, None))
    out_specs = P("row", "col")
    body = functools.partial(local, rows=mesh.shape["row"], cols=mesh.shape["col"])
    return jax.shard_map(body, mesh=mesh, in_specs=in_specs, out_specs=out_specs, check_vma=False)
```

```python
import functools

import jax
import jax.numpy as jnp
from jax import lax
from jax.experimental import pallas as pl
from jax.experimental.pallas import tpu as pltpu
from jax.sharding import PartitionSpec as P

MESH = pl.DeviceIdType.MESH
PARTS_A = 4
PIECES = 4
TILE = 45.0
HOP = 1.5
PIECE = 5.6


def split(value):
    high = value.astype(jnp.bfloat16)
    low = (value - high.astype(jnp.float32)).astype(jnp.bfloat16)
    return high, low


def row_parts(high, cols):
    helps = cols >= 4
    return [(high // 4, False)] + [(high // 8, helps)] * 5 + [(high // 16, helps)] * 2


def row_chunks(high, cols):
    chunks, first = [], 0
    for part, (height, helped) in enumerate(row_parts(high, cols)):
        piece = min(height, high // 16 if part else high // 8)
        for offset in range(0, height, piece):
            chunks.append((part, offset, piece, first + offset, helped))
        first += height
    return chunks


def kernel(rows, cols, blocks, link_max, links_in, counts_in, integrals_in, pairs, v, tab, out, *scratch):
    size = tab.shape[1]
    high, width = out.shape
    parts = row_parts(high, cols)
    chunks = row_chunks(high, cols)
    firsts = [sum(p[0] for p in parts[:i]) for i in range(len(parts))]
    scratch = list(scratch)
    colbuf = [scratch.pop(0) for _ in range(PARTS_A)]
    rowbuf = [scratch.pop(0) for _ in parts]
    (own_tab, beta_tab, help_tab, alpha_signs, beta_signs, help_signs, shared,
     pairs_v, pairs_s, links, counts, integrals, alpha_coef, beta_coef, help_coef,
     ssem, rsem, lsem) = scratch

    wide = width // PARTS_A
    spread = rows // cols
    blocks_b = blocks * spread
    tables = blocks * link_max
    chips = rows // 2
    reach = chips // 2
    across = chips // 2
    half = blocks // 2
    piece = tables // (2 * PIECES)
    helps = cols >= 4
    early = [k for k, chunk in enumerate(chunks) if chunk[0] < 2]

    r = lax.axis_index("row")
    c = lax.axis_index("col")
    core = lax.rem(r, 2)
    chip = r // 2
    other = r + 1 - 2 * core
    place = jnp.where(chip < across, chip, chips - 1 - (chip - across))

    def chip_at(position):
        position = lax.rem(position + 2 * chips, chips)
        return jnp.where(position < across, position, across + (chips - 1 - position))

    def row_at(position, k):
        return 2 * chip_at(position) + k

    right = (row_at(place + 1, core), c)
    left = (row_at(place - 1, core), c)
    partner = (other, c)
    up = (r, jnp.minimum(c + 1, cols - 1))
    down = (r, jnp.maximum(c - 1, 0))
    has_up = c < cols - 1
    has_down = c > 0
    at_end = (c == 0) | (c == cols - 1)
    inner = jnp.logical_not(at_end)
    helper = (c == 1) | (c == cols - 2)
    aided = jnp.where(c == 1, 0, cols - 1)
    inward = (r, jnp.where(c == 0, 1, cols - 2))

    ids = {}

    def number(*key):
        return ids.setdefault(key, len(ids))

    pending = []

    def describe(src, dst, key, device):
        return pltpu.make_async_remote_copy(
            src_ref=src, dst_ref=dst, send_sem=ssem.at[number(*key)], recv_sem=rsem.at[number(*key)],
            device_id=device, device_id_type=MESH)

    def when(cond, action):
        if cond is None:
            action()
        else:
            pl.when(cond)(action)

    def send(src, dst, key, device, cond=None, drain=True):
        copy = describe(src, dst, key, device)
        if drain:
            pending.append((cond, copy))
        when(cond, copy.start)

    def arrive(ref, key, cond=None):
        when(cond, describe(ref, ref, key, partner).wait_recv)

    local = []

    def load(src, dst, cond=None):
        copy = pltpu.make_async_copy(src, dst, lsem.at[len(local)])
        local.append(copy)
        when(cond, copy.start)
        return lambda: when(cond, copy.wait)

    plan = []

    def at(time, action):
        plan.append((time, len(plan), action))

    barrier = pltpu.get_barrier_semaphore()
    for k in range(1, rows):
        pl.semaphore_signal(barrier, inc=1, device_id=(lax.rem(r + k, rows), c), device_id_type=MESH)

    @pl.when(has_up)
    def _():
        pl.semaphore_signal(barrier, inc=1, device_id=up, device_id_type=MESH)

    @pl.when(has_down)
    def _():
        pl.semaphore_signal(barrier, inc=1, device_id=down, device_id_type=MESH)

    wait_small = [load(pairs, pairs_v.at[r]), load(links_in, links), load(counts_in, counts),
                  load(integrals_in, integrals)]

    def load_rows(i):
        sem = lsem.at[len(local)]
        first = firsts[i]
        for k in range(blocks_b):
            pltpu.make_async_copy(
                v.at[first // size, pl.ds(first % size, parts[i][0]), pl.ds(k * size, size)],
                rowbuf[i].at[c * blocks_b + k], sem).start()
        ref = rowbuf[i].at[pl.ds(c * blocks_b, blocks_b)]
        local.append(pltpu.make_async_copy(ref, ref, sem))
        return local[-1].wait

    wait_rows = [load_rows(i) for i in range(len(parts))]
    wait_tab = load(tab, own_tab)
    wait_cols = [load(v.at[:, :, pl.ds(j * wide, wide)], colbuf[j].at[pl.ds(r * blocks, blocks)])
                 for j in range(PARTS_A)]

    pl.semaphore_wait(barrier, rows - 1 + has_up.astype(jnp.int32) + has_down.astype(jnp.int32))

    for k in range(1, rows):
        send(pairs, pairs_v.at[r], ("pairs", k), (lax.rem(r + k, rows), c))

    reach_up = {1: up, -1: down}

    def ends(k):
        return TILE * (chunks[k][3] + chunks[k][2]) / high

    def arrival(t, k, late):
        far = max(cols - 3, 1)
        tiles = max(1, min(t, far)) if late else min(t, far)
        length = TILE * chunks[k][2] / high
        return ends(k) + TILE * tiles + HOP + (length + HOP) * (t if late else max(t - far, 0))

    def row_chunk(k, tile):
        part, offset, count, _, _ = chunks[k]
        return rowbuf[part].at[pl.ds(tile * blocks_b, blocks_b), pl.ds(offset, count), :]

    def line_own(k, way, cond):
        helped = chunks[k][4]
        position = c if way == 1 else cols - 1 - c
        limit = cols - 2 if helped else cols - 1
        ref = row_chunk(k, c)
        send(ref, ref, ("line", way, k, 0), reach_up[way], cond & (position < limit))

    def line_arrive(k, way, t, edge, forward):
        helped = chunks[k][4]
        last = cols - 2 if helped else cols - 1
        onward = t + 2 <= last if edge else t + 3 <= last
        if onward != forward or (t + 1 > last if edge else t + 2 > last):
            return
        position = c if way == 1 else cols - 1 - c
        cond = position == t + 1 if edge else (position > t + 1) & (position <= last)
        ref = row_chunk(k, jnp.clip(c - way * (1 + t), 0, cols - 1))
        arrive(ref, ("line", way, k, t), cond)
        if onward:
            send(ref, ref, ("line", way, k, t + 1), reach_up[way], cond if edge else cond & (position < last))

    def line_finish(i):
        for k, chunk in enumerate(chunks):
            if chunk[0] == i:
                for way in (1, -1):
                    for t in range(cols - 1):
                        for edge in (False, True):
                            line_arrive(k, way, t, edge, False)

    def table_places(s):
        source = c * spread + s
        source_chip = source // 2
        source_place = jnp.where(
            source_chip < across, source_chip, chips - 1 - (source_chip - across))
        distance = lax.rem(place - source_place + chips, chips)
        return lax.rem(source, 2), (distance, lax.rem(chips - distance, chips))

    ring = (right, left)

    def table_part(h, q):
        return pl.ds((h * PIECES + q) * piece, piece)

    def table_stage(s, h, q, d):
        source_core, hops = table_places(s)
        here = (core == source_core) & (hops[h] == d)
        part = table_part(h, q)
        ref = beta_tab.at[s, part]
        src = ref if d else tab.at[part]
        if d:
            arrive(ref, ("table", s, h, q), here)
        if d + 1 < chips:
            send(src, ref, ("table", s, h, q), ring[h], here, drain=False)
        send(src, ref, ("tableP", s, h, q), partner, here, drain=False)
        if helps:
            send(src, help_tab.at[s, part], ("help", s, h, q), inward, here & at_end, drain=False)

    def table_drain(s, h, q):
        source_core, hops = table_places(s)
        mine = core == source_core
        ref = beta_tab.at[s, table_part(h, q)]
        pending.append((mine & (hops[h] < chips - 1), describe(ref, ref, ("table", s, h, q), partner)))
        pending.append((mine, describe(ref, ref, ("tableP", s, h, q), partner)))
        if helps:
            pending.append((mine & at_end, describe(ref, ref, ("help", s, h, q), partner)))

    def table_finish():
        for s in range(spread):
            source_core, _ = table_places(s)
            for h in range(2):
                for q in range(PIECES):
                    arrive(beta_tab.at[s, table_part(h, q)], ("tableP", s, h, q), core != source_core)
            table_loads[s]()

    def help_arrive(s, h, q):
        source_core = table_places(s)[0]
        aided_core = lax.rem(aided * spread + s, 2)
        ref = help_tab.at[s, table_part(h, q)]
        arrive(ref, ("help", s, h, q), helper & (core == aided_core))
        send(ref, ref, ("helpP", s, h, q), partner, helper & (core == aided_core))

    def help_finish():
        for s in range(spread):
            aided_core = lax.rem(aided * spread + s, 2)
            for h in range(2):
                for q in range(PIECES):
                    arrive(help_tab.at[s, table_part(h, q)], ("helpP", s, h, q),
                           helper & (core != aided_core))

    def narrow(value):
        return value.astype(jnp.float32).astype(jnp.bfloat16)

    def widen(source, base, target):
        @pl.loop(0, tables)
        def _(index):
            values = narrow(source[index])
            target[base + index] = jnp.concatenate([values, values], axis=1)

    def couple(source, base, target):
        @pl.loop(0, tables // 2)
        def _(index):
            target[base + index] = jnp.concatenate(
                [narrow(source[2 * index]), narrow(source[2 * index + 1])], axis=1)

    def couple_all(source, target):
        for s in range(spread):
            couple(source.at[s], s * (tables // 2), target)

    def tile_half(j, hb, position, k):
        return colbuf[j].at[pl.ds(row_at(position, k) * blocks + hb * half, half)]

    def ring_own(j, hb, way, cond, drain):
        ref = colbuf[j].at[pl.ds(r * blocks + hb * half, half)]
        src = v.at[pl.ds(hb * half, half), :, pl.ds(j * wide, wide)]
        send(src, ref, ("ring", way, j, hb, 0), ring[way], cond, drain=False)
        if drain:
            pending.append((None, describe(ref, ref, ("ring", way, j, hb, 0), partner)))

    def carried(way, hb, t):
        return t < reach - 1 or hb == way

    def ring_arrive(j, hb, way, t):
        ref = tile_half(j, hb, place - 1 - t if way == 0 else place + 1 + t, core)
        arrive(ref, ("ring", way, j, hb, t))
        if t + 1 < reach and carried(way, hb, t + 1):
            send(ref, ref, ("ring", way, j, hb, t + 1), ring[way])
        send(ref, ref, ("ringP", way, j, hb, t), partner)

    def ring_finish(j):
        wait_cols[j]()
        arrive(colbuf[j].at[pl.ds(other * blocks, blocks)], ("own", j))
        for t in range(reach):
            for way in range(2):
                for hb in range(2):
                    if carried(way, hb, t):
                        position = place - 1 - t if way == 0 else place + 1 + t
                        arrive(tile_half(j, hb, position, 1 - core), ("ringP", way, j, hb, t))

    def coefficients(target, first, count):
        @pl.loop(0, count)
        def _(b):
            block = first + b
            for l in range(link_max):
                pair = pairs_s[lax.div(block, blocks), lax.rem(block, blocks), l]
                norb = integrals.shape[0]
                value = integrals[lax.div(pair, norb), lax.rem(pair, norb)]
                target[b, l] = value * jnp.clip(counts[block] - l, 0, 1).astype(jnp.float32)

    def gather_pairs():
        for wait in wait_small:
            wait()
        for k in range(1, rows):
            arrive(pairs_v.at[lax.rem(r - k + rows, rows)], ("pairs", k))
        copy = pltpu.make_async_copy(pairs_v, pairs_s, lsem.at[0])
        copy.start()
        copy.wait()
        coefficients(alpha_coef, r * blocks, blocks)
        coefficients(beta_coef, c * blocks_b, blocks_b)
        if helps:
            coefficients(help_coef, aided * blocks_b, blocks_b)

    def alpha_compute(j):
        @pl.loop(0, blocks)
        def _(block):
            total = jnp.zeros((size, wide), jnp.float32)
            for l in range(link_max):
                source = links[l, r * blocks + block]
                up_part, low_part = split(colbuf[j][source] * alpha_coef[block, l])
                total = total + jnp.dot(
                    alpha_signs[block * link_max + l], jnp.concatenate([up_part, low_part], axis=0),
                    preferred_element_type=jnp.float32)
            where = (pl.ds(pl.multiple_of(block * size, size), size), pl.ds(j * wide, wide))
            out[where] = out[where] + total

    def beta_compute(group, owner, coef, signs, target, start, add):
        count = sum(parts[i][0] for i in group)

        @pl.loop(0, blocks_b)
        def _(block):
            total = jnp.zeros((2 * count, size), jnp.float32)
            for l in range(0, link_max, 2):
                highs, lows = [], []
                for m in (l, l + 1):
                    source = links[m, owner * blocks_b + block]
                    value = jnp.concatenate([rowbuf[i][source] for i in group], axis=0)
                    up_part, low_part = split(value * coef[block, m])
                    highs.append(up_part)
                    lows.append(low_part)
                value = jnp.concatenate(
                    [jnp.concatenate(highs, axis=1), jnp.concatenate(lows, axis=1)], axis=0)
                total = total + lax.dot_general(
                    value, signs[block * (link_max // 2) + l // 2],
                    (((1,), (1,)), ((), ())), preferred_element_type=jnp.float32)
            total = total[:count] + total[count:]
            where = (pl.ds(start, count), pl.ds(pl.multiple_of(block * size, size), size))
            if add:
                total = target[where] + total
            target[where] = total

    shared_first = sum(height for height, helped in parts if not helped)

    def own_beta(group, cond):
        def action():
            beta_compute(group, c, beta_coef, beta_signs, out, firsts[group[0]], True)
        when(cond, action)

    def help_beta(i):
        @pl.when(helper)
        def _():
            beta_compute([i], aided, help_coef, help_signs, shared, firsts[i] - shared_first, False)

        ref = shared.at[pl.ds(firsts[i] - shared_first, parts[i][0])]
        send(ref, ref, ("sums", i), (r, aided), helper)

    def take_sums(i):
        ref = shared.at[pl.ds(firsts[i] - shared_first, parts[i][0])]
        arrive(ref, ("sums", i), at_end)

        @pl.when(at_end)
        def _():
            where = pl.ds(firsts[i], parts[i][0])
            out[where, :] = out[where, :] + ref[...]

    table_loads = []

    def begin():
        for s in range(spread):
            source_core, hops = table_places(s)
            table_loads.append(load(tab, beta_tab.at[s], (core == source_core) & (hops[0] == 0)))
        always = jnp.bool_(True)
        for k in range(len(chunks)):
            if chunks[k][1] == 0:
                wait_rows[chunks[k][0]]()
            first = k in early or not helps
            line_own(k, 1, always if first else has_down)
            line_own(k, -1, always if first else has_up)

    at(-2.0, begin)

    def rest():
        for k in range(len(early), len(chunks)):
            line_own(k, 1, c == 0)
            line_own(k, -1, c == cols - 1)

    stage_last = PIECE * (PIECES - 1 + chips - 1) + HOP * (chips - 1)
    if helps:
        at(stage_last + 0.1, rest)

    for k in range(len(chunks)):
        for t in range(cols - 1):
            for edge in (False, True):
                late = edge and k not in early and helps
                for way in (1, -1):
                    at(arrival(t, k, late), functools.partial(line_arrive, k, way, t, edge, True))

    for q in range(PIECES):
        for d in range(chips):
            for h in range(2):
                for s in range(spread):
                    time = -1.0 if d == 0 else PIECE * (q + d) + HOP * d
                    at(time, functools.partial(table_stage, s, h, q, d))
    at(stage_last + 3.5, table_finish)
    at(stage_last + 3.6, lambda: couple_all(beta_tab, beta_signs))

    help_ready = 0.0
    if helps:
        helped_last = 0.0
        for q in range(PIECES):
            for h in range(2):
                time = 6.0 + max(TILE / 4 + PIECE * (2 * q + h + 1), PIECE * (q + chips) + HOP * (chips + 1))
                helped_last = max(helped_last, time)
                for s in range(spread):
                    at(time, functools.partial(help_arrive, s, h, q))
        at(helped_last + 1.5, help_finish)
        at(helped_last + 1.6, lambda: pl.when(helper)(lambda: couple_all(help_tab, help_signs)))
        help_ready = helped_last + 1.7

    order = [(j, second) for second in range(2) for j in range(PARTS_A)]
    step = TILE / (2 * PARTS_A)

    classes = []
    for h in range(2):
        kind = jnp.int32(chips - 1)
        for s in range(spread):
            source_core, hops = table_places(s)
            kind = jnp.where(core == source_core, hops[h], kind)
        classes.append(kind)

    begun = PIECE * PIECES

    def ring_time(a, t):
        if t == 0:
            wait = PIECE * (PIECES + max(chips - 2, 0)) + HOP * chips + step * (a - 1)
            return wait if a else begun + step + HOP
        return begun + TILE + step * (a % PARTS_A + 1) + HOP + 1.0 + 30.0 * (t - 1) + 0.1 * (a // PARTS_A)

    for a, (j, second) in enumerate(order):
        for way in range(2):
            hb = (1 - way) if second else way
            for d in range(chips):
                time = 0.0
                if d < chips - 1 and a >= d:
                    time = PIECE * (PIECES - 1 + d) + HOP * d + 0.05 if d else 0.0
                at(time, functools.partial(ring_own, j, hb, way, classes[way] == d, d == 0))
            for t in range(reach):
                if carried(way, hb, t):
                    at(ring_time(a, t), functools.partial(ring_arrive, j, hb, way, t))

    def own_pass(j):
        ref = colbuf[j].at[pl.ds(r * blocks, blocks)]
        send(v.at[:, :, pl.ds(j * wide, wide)], ref, ("own", j), partner)

    for j in range(PARTS_A):
        at(0.5, functools.partial(own_pass, j))
        done = max(ring_time(j, reach - 1), ring_time(PARTS_A + j, max(reach - 2, 0))) + 2.5
        at(done, functools.partial(ring_finish, j))
        at(done, functools.partial(alpha_compute, j))

    def prepare():
        out[...] = jnp.zeros_like(out)
        gather_pairs()
        wait_tab()
        widen(own_tab, 0, alpha_signs)

    at(0.6, prepare)

    groups = [[0], [1, 2], [3, 4], [5, 6, 7]]

    def finish_time(i, t):
        k = max(k for k, chunk in enumerate(chunks) if chunk[0] == i)
        return arrival(t, k, helps and k not in early) + 0.1

    for i, (height, helped) in enumerate(parts):
        inside, outside = finish_time(i, max(cols - 3, 0)), finish_time(i, cols - 2)
        if helped:
            inside = max(inside, help_ready) if i == 1 else inside
            at(inside, functools.partial(line_finish, i))
            at(inside, functools.partial(help_beta, i))
            at(outside + 15.0 + i, functools.partial(take_sums, i))
        else:
            at(outside, functools.partial(line_finish, i))
    for group in groups:
        inside, outside = finish_time(group[-1], max(cols - 3, 0)), finish_time(group[-1], cols - 2)
        if parts[group[0]][1]:
            at(max(inside, help_ready) + 0.1, functools.partial(own_beta, group, inner))
        else:
            at(outside + 0.1, functools.partial(own_beta, group, None))

    for _, _, action in sorted(plan, key=lambda entry: entry[:2]):
        action()

    for s in range(spread):
        for h in range(2):
            for q in range(PIECES):
                table_drain(s, h, q)
    for cond, copy in pending:
        when(cond, copy.wait_send)


def local(vector, one_electron, links, counts, pairs, signs, rows, cols):
    blocks, link_max = pairs.shape
    size = signs.shape[2]
    high, width = vector.shape
    spread = rows // cols
    tables = blocks * link_max
    parts = row_parts(high, cols)
    helped = sum(height for height, aided in parts if aided)
    reach = rows // 4
    messages = rows - 1 + 2 * len(row_chunks(high, cols)) * (cols - 1)
    messages += PARTS_A * (1 + 8 * reach) + spread * 2 * PIECES * 4 + len(parts)
    scratch = [pltpu.VMEM((rows * blocks, size, width // PARTS_A), jnp.float32)] * PARTS_A
    scratch += [pltpu.VMEM((cols * blocks * spread, height, size), jnp.float32) for height, _ in parts]
    scratch += [
        pltpu.VMEM((tables, size, size), jnp.int32),
        pltpu.VMEM((spread, tables, size, size), jnp.int32),
        pltpu.VMEM((spread, tables, size, size), jnp.int32),
        pltpu.VMEM((tables, size, 2 * size), jnp.bfloat16),
        pltpu.VMEM((spread * tables // 2, size, 2 * size), jnp.bfloat16),
        pltpu.VMEM((spread * tables // 2, size, 2 * size), jnp.bfloat16),
        pltpu.VMEM((max(helped, 8), width), jnp.float32),
        pltpu.VMEM((rows, blocks, link_max), jnp.int32),
        pltpu.SMEM((rows, blocks, link_max), jnp.int32),
        pltpu.SMEM((link_max, links.shape[0]), jnp.int32),
        pltpu.SMEM(counts.shape, jnp.int32),
        pltpu.SMEM(one_electron.shape, jnp.float32),
        pltpu.SMEM((blocks, link_max), jnp.float32),
        pltpu.SMEM((blocks * spread, link_max), jnp.float32),
        pltpu.SMEM((blocks * spread, link_max), jnp.float32),
        pltpu.SemaphoreType.DMA((messages,)),
        pltpu.SemaphoreType.DMA((messages,)),
        pltpu.SemaphoreType.DMA((5 + len(parts) + PARTS_A + spread,)),
    ]
    far = pl.BlockSpec(memory_space=pltpu.HBM)
    operands = (links.T, counts, one_electron, pairs, vector.reshape(blocks, size, width),
                signs.reshape(tables, size, size))
    return pl.pallas_call(
        functools.partial(kernel, rows, cols, blocks, link_max),
        out_shape=jax.ShapeDtypeStruct(vector.shape, jnp.float32),
        in_specs=[far] * 6,
        out_specs=pl.BlockSpec(memory_space=pltpu.VMEM),
        scratch_shapes=scratch,
        compiler_params=pltpu.CompilerParams(
            collective_id=0, has_side_effects=True, vmem_limit_bytes=48 << 20),
    )(*[pltpu.with_memory_space_constraint(value, pltpu.HBM) for value in operands])


def solution(mesh):
    in_specs = (P("row", "col"), P(), P(), P(), P("row", None), P("row", None, None, None))
    out_specs = P("row", "col")
    body = functools.partial(local, rows=mesh.shape["row"], cols=mesh.shape["col"])
    return jax.shard_map(body, mesh=mesh, in_specs=in_specs, out_specs=out_specs, check_vma=False)
```

```python
import functools

import jax
import jax.numpy as jnp
from jax import lax
from jax.experimental import pallas as pl
from jax.experimental.pallas import tpu as pltpu
from jax.sharding import PartitionSpec as P

MESH = pl.DeviceIdType.MESH
PARTS_A = 4
PIECES = 4
START = 4.5
TILE = 45.0
HOP = 1.5
PIECE = 5.6


def split(value):
    high = value.astype(jnp.bfloat16)
    low = (value - high.astype(jnp.float32)).astype(jnp.bfloat16)
    return high, low


def row_parts(high, cols):
    helps = cols >= 4
    return [(high // 4, False)] + [(high // 8, helps)] * 5 + [(high // 16, helps)] * 2


def row_chunks(high, cols):
    chunks, first = [], 0
    for part, (height, helped) in enumerate(row_parts(high, cols)):
        piece = min(height, high // 16 if part else high // 8)
        for offset in range(0, height, piece):
            chunks.append((part, offset, piece, first + offset, helped))
        first += height
    return chunks


def in_order(plan):
    left = sorted(enumerate(plan), key=lambda entry: (entry[1][0], entry[0]))
    now, result = 0.0, []
    while left:
        ready = [entry for entry in left if entry[1][0] <= now] or [left[0]]
        chosen = min(ready, key=lambda entry: (entry[1][1], entry[1][0], entry[0]))
        left.remove(chosen)
        start, _, length, action = chosen[1]
        now = max(now, start) + length
        result.append(action)
    return result


def kernel(rows, cols, blocks, link_max, links_in, counts_in, integrals_in, pairs, v, tab, result, *scratch):
    size = tab.shape[1]
    high, width = result.shape
    parts = row_parts(high, cols)
    chunks = row_chunks(high, cols)
    firsts = [sum(p[0] for p in parts[:i]) for i in range(len(parts))]
    scratch = list(scratch)
    colbuf = [scratch.pop(0) for _ in range(PARTS_A)]
    rowbuf = [scratch.pop(0) for _ in parts]
    (own_tab, beta_tab, help_tab, alpha_signs, beta_signs, help_signs, shared,
     out, pairs_v, pairs_s, links, counts, integrals, alpha_coef, beta_coef, help_coef,
     ssem, rsem, lsem) = scratch

    wide = width // PARTS_A
    spread = rows // cols
    blocks_b = blocks * spread
    tables = blocks * link_max
    chips = rows // 2
    reach = chips // 2
    across = chips // 2
    half = blocks // 2
    piece = tables // (2 * PIECES)
    helps = cols >= 4
    early = [k for k, chunk in enumerate(chunks) if chunk[0] < 2]

    r = lax.axis_index("row")
    c = lax.axis_index("col")
    core = lax.rem(r, 2)
    chip = r // 2
    other = r + 1 - 2 * core
    place = jnp.where(chip < across, chip, chips - 1 - (chip - across))

    def chip_at(position):
        position = lax.rem(position + 2 * chips, chips)
        return jnp.where(position < across, position, across + (chips - 1 - position))

    def row_at(position, k):
        return 2 * chip_at(position) + k

    right = (row_at(place + 1, core), c)
    left = (row_at(place - 1, core), c)
    partner = (other, c)
    up = (r, jnp.minimum(c + 1, cols - 1))
    down = (r, jnp.maximum(c - 1, 0))
    has_up = c < cols - 1
    has_down = c > 0
    at_end = (c == 0) | (c == cols - 1)
    inner = jnp.logical_not(at_end)
    helper = (c == 1) | (c == cols - 2)
    aided = jnp.where(c == 1, 0, cols - 1)
    inward = (r, jnp.where(c == 0, 1, cols - 2))

    numbers = ({}, {})

    def number(side, key):
        return numbers[side].setdefault(key, len(numbers[side]))

    plan = []

    def at(time, action, rank=0, length=0.0):
        plan.append((time, rank, length, action))

    def describe(src, dst, group, key, device):
        return pltpu.make_async_remote_copy(
            src_ref=src, dst_ref=dst, send_sem=ssem.at[number(0, group)], recv_sem=rsem.at[number(1, key)],
            device_id=device, device_id_type=MESH)

    def when(cond, action):
        if cond is None:
            action()
        else:
            pl.when(cond)(action)

    def send(src, dst, group, key, device, cond=None):
        when(cond, describe(src, dst, group, key, device).start)

    def arrive(ref, key, cond=None):
        when(cond, pltpu.make_async_copy(ref, ref, rsem.at[number(1, key)]).wait)

    def drain(time, ref, group, cond=None):
        def action():
            wait = pltpu.make_async_copy(ref, ref, ssem.at[number(0, group)]).wait
            when(cond() if cond else None, wait)
        at(time, action, 9, 0.02)

    local = []

    def load(src, dst, cond=None):
        copy = pltpu.make_async_copy(src, dst, lsem.at[len(local)])
        local.append(copy)
        when(cond, copy.start)
        return lambda: when(cond, copy.wait)

    barrier = pltpu.get_barrier_semaphore()
    for k in range(1, rows):
        pl.semaphore_signal(barrier, inc=1, device_id=(lax.rem(r + k, rows), c), device_id_type=MESH)

    @pl.when(has_up)
    def _():
        pl.semaphore_signal(barrier, inc=1, device_id=up, device_id_type=MESH)

    @pl.when(has_down)
    def _():
        pl.semaphore_signal(barrier, inc=1, device_id=down, device_id_type=MESH)

    wait_small = [load(pairs, pairs_v.at[r]), load(links_in, links), load(counts_in, counts),
                  load(integrals_in, integrals)]

    def load_rows(i):
        sem = lsem.at[len(local)]
        first = firsts[i]
        for k in range(blocks_b):
            pltpu.make_async_copy(
                v.at[first // size, pl.ds(first % size, parts[i][0]), pl.ds(k * size, size)],
                rowbuf[i].at[c * blocks_b + k], sem).start()
        ref = rowbuf[i].at[pl.ds(c * blocks_b, blocks_b)]
        local.append(pltpu.make_async_copy(ref, ref, sem))
        return local[-1].wait

    wait_rows = [load_rows(i) for i in range(len(parts))]
    wait_tab = load(tab, own_tab)
    wait_cols = [load(v.at[:, :, pl.ds(j * wide, wide)], colbuf[j].at[pl.ds(r * blocks, blocks)])
                 for j in range(PARTS_A)]

    pl.semaphore_wait(barrier, rows - 1 + has_up.astype(jnp.int32) + has_down.astype(jnp.int32))

    for k in range(1, rows):
        send(pairs, pairs_v.at[r], ("pairs", k), ("pairs", k), (lax.rem(r + k, rows), c))
        drain(15.0, pairs_v.at[r], ("pairs", k))

    reach_up = {1: up, -1: down}

    def ends(k):
        return TILE * (chunks[k][3] + chunks[k][2]) / high

    def arrival(t, k, late):
        far = max(cols - 3, 1)
        tiles = max(1, min(t, far)) if late else min(t, far)
        length = TILE * chunks[k][2] / high
        return ends(k) + TILE * tiles + HOP + (length + HOP) * (t if late else max(t - far, 0))

    def row_chunk(k, tile):
        part, offset, count, _, _ = chunks[k]
        return rowbuf[part].at[pl.ds(tile * blocks_b, blocks_b), pl.ds(offset, count), :]

    def line_own(k, way, cond):
        helped = chunks[k][4]
        position = c if way == 1 else cols - 1 - c
        limit = cols - 2 if helped else cols - 1
        ref = row_chunk(k, c)
        send(ref, ref, ("line", way, 0, helped), ("line", way, k, 0), reach_up[way], cond & (position < limit))

    def line_arrive(k, way, t, edge, forward):
        helped = chunks[k][4]
        last = cols - 2 if helped else cols - 1
        onward = t + 2 <= last if edge else t + 3 <= last
        if onward != forward or (t + 1 > last if edge else t + 2 > last):
            return
        position = c if way == 1 else cols - 1 - c
        cond = position == t + 1 if edge else (position > t + 1) & (position <= last)
        ref = row_chunk(k, jnp.clip(c - way * (1 + t), 0, cols - 1))
        arrive(ref, ("line", way, k, t), cond)
        if onward:
            send(ref, ref, ("line", way, t + 1, helped), ("line", way, k, t + 1), reach_up[way],
                 cond if edge else cond & (position < last))

    def line_finish(i):
        for k, chunk in enumerate(chunks):
            if chunk[0] == i:
                for way in (1, -1):
                    for t in range(cols - 1):
                        for edge in (False, True):
                            line_arrive(k, way, t, edge, False)

    def table_places(s):
        source = c * spread + s
        source_chip = source // 2
        source_place = jnp.where(
            source_chip < across, source_chip, chips - 1 - (source_chip - across))
        distance = lax.rem(place - source_place + chips, chips)
        return lax.rem(source, 2), (distance, lax.rem(chips - distance, chips))

    ring = (right, left)

    def table_part(h, q):
        return pl.ds((h * PIECES + q) * piece, piece)

    def table_stage(s, h, q, d):
        source_core, hops = table_places(s)
        here = (core == source_core) & (hops[h] == d)
        part = table_part(h, q)
        ref = beta_tab.at[s, part]
        src = ref if d else own_tab.at[part]
        if d:
            arrive(ref, ("table", s, h, q), here)
        if d + 1 < chips:
            send(src, ref, ("table", s, h), ("table", s, h, q), ring[h], here)
        send(src, ref, ("tableP", s), ("tableP", s), partner, here)
        if helps:
            send(src, help_tab.at[s, part], ("help", s), ("help", s, h, q), inward, here & at_end)

    def table_finish():
        for s in range(spread):
            source_core, _ = table_places(s)
            arrive(beta_tab.at[s], ("tableP", s), core != source_core)
            table_loads[s]()

    def help_arrive(s, h, q):
        source_core = table_places(s)[0]
        aided_core = lax.rem(aided * spread + s, 2)
        ref = help_tab.at[s, table_part(h, q)]
        arrive(ref, ("help", s, h, q), helper & (core == aided_core))
        send(ref, ref, ("helpP", s), ("helpP", s), partner, helper & (core == aided_core))

    def help_finish():
        for s in range(spread):
            aided_core = lax.rem(aided * spread + s, 2)
            arrive(help_tab.at[s], ("helpP", s), helper & (core != aided_core))

    def narrow(value):
        return value.astype(jnp.float32).astype(jnp.bfloat16)

    def widen(source, base, target):
        @pl.loop(0, tables)
        def _(index):
            values = narrow(source[index])
            target[base + index] = jnp.concatenate([values, values], axis=1)

    def couple(source, base, target):
        @pl.loop(0, tables // 2)
        def _(index):
            target[base + index] = jnp.concatenate(
                [narrow(source[2 * index]), narrow(source[2 * index + 1])], axis=1)

    def couple_all(source, target):
        for s in range(spread):
            couple(source.at[s], s * (tables // 2), target)

    def tile_half(j, hb, position, k):
        return colbuf[j].at[pl.ds(row_at(position, k) * blocks + hb * half, half)]

    def ring_own(j, hb, way, cond):
        ref = colbuf[j].at[pl.ds(r * blocks + hb * half, half)]
        send(ref, ref, ("ring", way, 0), ("ring", way, j, hb, 0), ring[way], cond)

    def carried(way, hb, t):
        return t < reach - 1 or hb == way

    def ring_arrive(j, hb, way, t):
        ref = tile_half(j, hb, place - 1 - t if way == 0 else place + 1 + t, core)
        arrive(ref, ("ring", way, j, hb, t))
        if t + 1 < reach and carried(way, hb, t + 1):
            send(ref, ref, ("ring", way, t + 1), ("ring", way, j, hb, t + 1), ring[way])
        send(ref, ref, ("ringP", way, t), ("tiles", j), partner)

    def ring_finish(j):
        arrive(colbuf[j].at[pl.ds(0, chips * blocks)], ("tiles", j))

    def coefficients(target, first, count):
        @pl.loop(0, count)
        def _(b):
            block = first + b
            for l in range(link_max):
                pair = pairs_s[lax.div(block, blocks), lax.rem(block, blocks), l]
                norb = integrals.shape[0]
                value = integrals[lax.div(pair, norb), lax.rem(pair, norb)]
                target[b, l] = value * jnp.clip(counts[block] - l, 0, 1).astype(jnp.float32)

    def gather_pairs():
        for wait in wait_small:
            wait()
        for k in range(1, rows):
            arrive(pairs_v.at[lax.rem(r - k + rows, rows)], ("pairs", k))
        copy = pltpu.make_async_copy(pairs_v, pairs_s, lsem.at[0])
        copy.start()
        copy.wait()
        coefficients(alpha_coef, r * blocks, blocks)
        coefficients(beta_coef, c * blocks_b, blocks_b)
        if helps:
            coefficients(help_coef, aided * blocks_b, blocks_b)

    def alpha_compute(j):
        @pl.loop(0, blocks)
        def _(block):
            total = jnp.zeros((size, wide), jnp.float32)
            for l in range(link_max):
                source = links[l, r * blocks + block]
                up_part, low_part = split(colbuf[j][source] * alpha_coef[block, l])
                total = total + jnp.dot(
                    alpha_signs[block * link_max + l], jnp.concatenate([up_part, low_part], axis=0),
                    preferred_element_type=jnp.float32)
            where = (pl.ds(pl.multiple_of(block * size, size), size), pl.ds(j * wide, wide))
            out[where] = out[where] + total

    def beta_compute(group, owner, coef, signs, target, start, add):
        count = sum(parts[i][0] for i in group)

        @pl.loop(0, blocks_b)
        def _(block):
            total = jnp.zeros((2 * count, size), jnp.float32)
            for l in range(0, link_max, 2):
                highs, lows = [], []
                for m in (l, l + 1):
                    source = links[m, owner * blocks_b + block]
                    value = jnp.concatenate([rowbuf[i][source] for i in group], axis=0)
                    up_part, low_part = split(value * coef[block, m])
                    highs.append(up_part)
                    lows.append(low_part)
                value = jnp.concatenate(
                    [jnp.concatenate(highs, axis=1), jnp.concatenate(lows, axis=1)], axis=0)
                total = total + lax.dot_general(
                    value, signs[block * (link_max // 2) + l // 2],
                    (((1,), (1,)), ((), ())), preferred_element_type=jnp.float32)
            total = total[:count] + total[count:]
            where = (pl.ds(start, count), pl.ds(pl.multiple_of(block * size, size), size))
            if add:
                total = target[where] + total
            target[where] = total

    shared_first = sum(height for height, helped in parts if not helped)

    def own_beta(group, cond):
        def action():
            beta_compute(group, c, beta_coef, beta_signs, out, firsts[group[0]], True)
        when(cond, action)

    def help_beta(i):
        @pl.when(helper)
        def _():
            beta_compute([i], aided, help_coef, help_signs, shared, firsts[i] - shared_first, False)

        ref = shared.at[pl.ds(firsts[i] - shared_first, parts[i][0])]
        send(ref, ref, ("sums",), ("sums", i), (r, aided), helper)

    def take_sums(i):
        ref = shared.at[pl.ds(firsts[i] - shared_first, parts[i][0])]
        arrive(ref, ("sums", i), at_end)

        @pl.when(at_end)
        def _():
            where = pl.ds(firsts[i], parts[i][0])
            out[where, :] = out[where, :] + ref[...]

        flush(firsts[i], parts[i][0], at_end)

    flushes, held, alphas = [], [], []

    def flush(first, count, cond):
        if len(alphas) < PARTS_A:
            held.append((first, count, cond))
            return
        where = pl.ds(first, count)
        flushes.append(load(out.at[where], result.at[where], cond))

    table_loads = []

    def begin():
        always = jnp.bool_(True)
        for k in range(len(chunks)):
            if chunks[k][1] == 0:
                wait_rows[chunks[k][0]]()
            first = k in early or not helps
            line_own(k, 1, always if first else has_down)
            line_own(k, -1, always if first else has_up)
        wait_tab()

    def begin_tables():
        for s in range(spread):
            source_core, hops = table_places(s)
            table_loads.append(load(tab, beta_tab.at[s], (core == source_core) & (hops[0] == 0)))

    def begin_tiles():
        for j in range(PARTS_A):
            wait_cols[j]()

    at(-4.0, begin)
    at(-2.0, begin_tables)
    at(-1.5, begin_tiles)

    def rest():
        for k in range(len(early), len(chunks)):
            line_own(k, 1, c == 0)
            line_own(k, -1, c == cols - 1)

    stage_last = START + PIECE * (PIECES - 1 + chips - 1) + HOP * (chips - 1)
    if helps:
        at(stage_last + 0.1, rest)

    for k in range(len(chunks)):
        helped = chunks[k][4]
        late_k = helps and k not in early
        for way in (1, -1):
            for t in range(cols - 1):
                for edge in (False, True):
                    late = edge and late_k
                    at(START + arrival(t, k, late), functools.partial(line_arrive, k, way, t, edge, True))

    for helped in (False, True) if helps else (False,):
        count = sum(height for height, aided_part in parts if aided_part == helped)
        last_k = max(k for k, chunk in enumerate(chunks) if chunk[4] == helped)
        last = cols - 2 if helped else cols - 1
        for way in (1, -1):
            for t in range(last):
                def cond(t=t, way=way, last=last):
                    position = c if way == 1 else cols - 1 - c
                    return (position >= t) & (position < last)

                sent = START + arrival(t, last_k, helps and last_k not in early) + (TILE if t == 0 else 0.0)
                drain(sent + 6.0, out.at[pl.ds(0, count)], ("line", way, t, helped), cond)

    for q in range(PIECES):
        for h in range(2):
            for s in range(spread):
                for d in range(chips):
                    time = -1.0 if d == 0 else START + PIECE * (q + d) + HOP * d
                    at(time, functools.partial(table_stage, s, h, q, d))
    for s in range(spread):
        def mine(s=s):
            return core == table_places(s)[0]

        for h in range(2):
            drain(stage_last + 12.0, beta_tab.at[s, pl.ds(0, tables // 2)], ("table", s, h),
                  lambda s=s, h=h: mine(s) & (table_places(s)[1][h] < chips - 1))
        drain(stage_last + 12.0, beta_tab.at[s], ("tableP", s), mine)
        if helps:
            drain(START + 1.8 * TILE, beta_tab.at[s], ("help", s), lambda s=s: mine(s) & at_end)
            drain(START + 1.8 * TILE, beta_tab.at[s], ("helpP", s),
                  lambda s=s: helper & (core == lax.rem(aided * spread + s, 2)))
    at(stage_last + 4.0, table_finish, 1, 0.1)
    at(stage_last + 4.1, lambda: couple_all(beta_tab, beta_signs), 2, 1.0)

    help_ready = 0.0
    if helps:
        for q in range(PIECES):
            for h in range(2):
                time = START + max(
                    ends(len(early) - 1) + PIECE * (q + PIECES + 1) + HOP, PIECE * (q + chips) + HOP * (chips + 1))
                help_ready = max(help_ready, time + 1.5)
                for s in range(spread):
                    at(time + 0.5, functools.partial(help_arrive, s, h, q))
        at(help_ready, help_finish, 1, 0.1)
        at(help_ready + 0.1, lambda: pl.when(helper)(lambda: couple_all(help_tab, help_signs)), 1, 1.0)
        help_ready += 0.2

    order = [(j, second) for second in range(2) for j in range(PARTS_A)]
    step = TILE / (2 * PARTS_A)

    classes = []
    for h in range(2):
        kind = jnp.int32(chips - 1)
        for s in range(spread):
            source_core, hops = table_places(s)
            kind = jnp.where(core == source_core, hops[h], kind)
        classes.append(kind)

    held_back = PARTS_A + 1

    def ring_time(a, t):
        if t == 0 and a < PARTS_A:
            wait = PIECE * (PIECES + max(chips - 2, 0)) + HOP * (chips - 1) + step * (a - 1) + HOP
            return max(stage_last - PIECE - HOP + 0.2, START + (wait if a else 0.0))
        j = a % PARTS_A
        place = PARTS_A + 1 + 2 * j + (1 if t else 0)
        return START + PIECE * PIECES + step * place + 3.0 * HOP + 30.0 * max(t - 1, 0)

    for a, (j, second) in enumerate(order):
        for way in range(2):
            hb = (1 - way) if second else way
            for d in range(chips):
                time = 0.0
                if d < chips - 1 and a >= d:
                    time = START + PIECE * (PIECES - 1 + d) + HOP * d + 0.05 if d else 0.0
                if a >= held_back:
                    time = ring_time(a - held_back, 0) + 0.1
                at(time, functools.partial(ring_own, j, hb, way, classes[way] == d))
            for t in range(reach):
                if carried(way, hb, t):
                    forwards = t + 1 < reach and carried(way, hb, t + 1)
                    at(ring_time(a, t) + (0.0 if forwards else 1.0),
                       functools.partial(ring_arrive, j, hb, way, t), 0 if forwards else 1, 0.03)
    for t in range(reach):
        count = high if t < reach - 1 else high // 2
        for way in range(2):
            drain(ring_time(2 * PARTS_A - 1, t) + 4.0, out.at[pl.ds(0, count)], ("ring", way, t))
            drain(ring_time(2 * PARTS_A - 1, t) + 8.0, out.at[pl.ds(0, count)], ("ringP", way, t))

    def own_pass(j):
        ref = colbuf[j].at[pl.ds(r * blocks, blocks)]
        send(ref, ref, ("own",), ("tiles", j), partner)

    def alpha_step(j):
        ring_finish(j)
        alpha_compute(j)
        alphas.append(j)
        if len(alphas) == PARTS_A:
            for entry in held:
                flush(*entry)

    for j in range(PARTS_A):
        at(0.5, functools.partial(own_pass, j))
        done = max(ring_time(j, reach - 1), ring_time(PARTS_A + j, max(reach - 2, 0))) + 3.0
        at(done, functools.partial(alpha_step, j), 4, 1.4)

    drain(25.0, out, ("own",))

    def prepare():
        out[...] = jnp.zeros_like(out)
        gather_pairs()
        widen(own_tab, 0, alpha_signs)

    at(0.6, prepare, 0, 4.0)

    groups = [[0], [1, 2, 3, 4], [5, 6, 7]]

    def finish_time(i, t):
        k = max(k for k, chunk in enumerate(chunks) if chunk[0] == i)
        return START + arrival(t, k, helps and k not in early) + 0.1

    def help_step(i):
        line_finish(i)
        help_beta(i)

    def own_step(group, finish, cond):
        if finish:
            for i in group:
                line_finish(i)
        own_beta(group, cond)
        flush(firsts[group[0]], sum(parts[i][0] for i in group), cond)

    for i, (height, helped) in enumerate(parts):
        if helped:
            ready = max(finish_time(i, max(cols - 3, 0)), help_ready)
            at(ready, functools.partial(help_step, i), 2, 1.9)
            at(ready + 11.0, functools.partial(take_sums, i), 5, 0.0)
    if helps:
        drain(help_ready + TILE, shared, ("sums",), lambda: helper)
    for group in groups:
        inside, outside = finish_time(group[-1], max(cols - 3, 0)), finish_time(group[-1], cols - 2)
        if parts[group[0]][1]:
            at(max(inside, help_ready) + 0.1, functools.partial(own_step, group, False, inner), 6, 2.6)
        elif helps:
            at(inside + 0.1, functools.partial(own_step, group, False, inner), 6, 2.6)
            at(outside + 0.1, functools.partial(own_step, group, True, at_end), 6, 0.0)
        else:
            at(outside + 0.1, functools.partial(own_step, group, True, None), 6, 2.6)

    for action in in_order(plan):
        action()
    for wait in flushes:
        wait()
    assert len(numbers[0]) == ssem.shape[0] and len(numbers[1]) == rsem.shape[0]
    assert len(local) <= lsem.shape[0]


def local(vector, one_electron, links, counts, pairs, signs, rows, cols):
    blocks, link_max = pairs.shape
    size = signs.shape[2]
    high, width = vector.shape
    spread = rows // cols
    tables = blocks * link_max
    parts = row_parts(high, cols)
    helped = sum(height for height, aided in parts if aided)
    reach = rows // 4
    sends = rows - 1 + 2 * (cols - 1) + 4 * reach + 2 + spread * 3
    arrivals = rows - 1 + PARTS_A * (4 * reach - 1) + spread * (2 * PIECES + 1)
    arrivals += sum(2 * (cols - 2 if chunk[4] else cols - 1) for chunk in row_chunks(high, cols))
    if cols >= 4:
        sends += 2 * (cols - 2) + spread * 2
        arrivals += len(parts) - 1 + spread * (2 * PIECES + 1)
    scratch = [pltpu.VMEM((rows * blocks, size, width // PARTS_A), jnp.float32)] * PARTS_A
    scratch += [pltpu.VMEM((cols * blocks * spread, height, size), jnp.float32) for height, _ in parts]
    scratch += [
        pltpu.VMEM((tables, size, size), jnp.int32),
        pltpu.VMEM((spread, tables, size, size), jnp.int32),
        pltpu.VMEM((spread, tables, size, size), jnp.int32),
        pltpu.VMEM((tables, size, 2 * size), jnp.bfloat16),
        pltpu.VMEM((spread * tables // 2, size, 2 * size), jnp.bfloat16),
        pltpu.VMEM((spread * tables // 2, size, 2 * size), jnp.bfloat16),
        pltpu.VMEM((max(helped, 8), width), jnp.float32),
        pltpu.VMEM((high, width), jnp.float32),
        pltpu.VMEM((rows, blocks, link_max), jnp.int32),
        pltpu.SMEM((rows, blocks, link_max), jnp.int32),
        pltpu.SMEM((link_max, links.shape[0]), jnp.int32),
        pltpu.SMEM(counts.shape, jnp.int32),
        pltpu.SMEM(one_electron.shape, jnp.float32),
        pltpu.SMEM((blocks, link_max), jnp.float32),
        pltpu.SMEM((blocks * spread, link_max), jnp.float32),
        pltpu.SMEM((blocks * spread, link_max), jnp.float32),
        pltpu.SemaphoreType.DMA((sends,)),
        pltpu.SemaphoreType.DMA((arrivals,)),
        pltpu.SemaphoreType.DMA((8 + 2 * len(parts) + PARTS_A + spread,)),
    ]
    far = pl.BlockSpec(memory_space=pltpu.HBM)
    operands = (links.T, counts, one_electron, pairs, vector.reshape(blocks, size, width),
                signs.reshape(tables, size, size))
    return pl.pallas_call(
        functools.partial(kernel, rows, cols, blocks, link_max),
        out_shape=jax.ShapeDtypeStruct(vector.shape, jnp.float32),
        in_specs=[far] * 6,
        out_specs=pl.BlockSpec(memory_space=pl.ANY),
        scratch_shapes=scratch,
        compiler_params=pltpu.CompilerParams(
            collective_id=0, has_side_effects=True, vmem_limit_bytes=48 << 20),
    )(*[pltpu.with_memory_space_constraint(value, pltpu.HBM) for value in operands])


def solution(mesh):
    in_specs = (P("row", "col"), P(), P(), P(), P("row", None), P("row", None, None, None))
    out_specs = P("row", "col")
    body = functools.partial(local, rows=mesh.shape["row"], cols=mesh.shape["col"])
    return jax.shard_map(body, mesh=mesh, in_specs=in_specs, out_specs=out_specs, check_vma=False)
```

```python
import functools

import jax
import jax.numpy as jnp
from jax import lax
from jax.experimental import pallas as pl
from jax.experimental.pallas import tpu as pltpu
from jax.sharding import PartitionSpec as P

MESH = pl.DeviceIdType.MESH
PARTS_A = 4
PIECES = 4
START = 4.5
LEAD = 2.5
SLACK = 0.7
TILE = 45.0
HOP = 1.5
PIECE = 5.6


def split(value):
    high = value.astype(jnp.bfloat16)
    low = (value - high.astype(jnp.float32)).astype(jnp.bfloat16)
    return high, low


def row_parts(high, cols):
    helps = cols >= 4
    return [(high // 4, False)] + [(high // 8, helps)] * 5 + [(high // 16, helps)] * 2


def row_chunks(high, cols):
    chunks, first = [], 0
    for part, (height, helped) in enumerate(row_parts(high, cols)):
        piece = min(height, high // 16 if part else high // 8)
        for offset in range(0, height, piece):
            chunks.append((part, offset, piece, first + offset, helped))
        first += height
    return chunks


def in_order(plan):
    left = sorted(enumerate(plan), key=lambda entry: (entry[1][0], entry[0]))
    urgent = [entry for entry in left if entry[1][1] <= 2]
    now, result = 0.0, []
    while left:
        ready = [entry for entry in left if entry[1][0] <= now]
        soon = [entry for entry in urgent if entry[1][0] > now][:1]
        if soon:
            room = soon[0][1][0] - now + SLACK
            ready = [entry for entry in ready if entry[1][1] <= 2 or entry[1][2] <= room]
        if not ready:
            now = min(entry[1][0] for entry in (soon or left))
            ready = [entry for entry in left if entry[1][0] <= now and entry[1][1] <= 2] or left[:1]
        chosen = min(ready, key=lambda entry: (entry[1][1], entry[1][0], entry[0]))
        left.remove(chosen)
        if chosen[1][1] <= 2:
            urgent.remove(chosen)
        start, _, length, action = chosen[1]
        now = max(now, start) + length
        result.append(action)
    return result


def kernel(rows, cols, blocks, link_max, links_in, counts_in, integrals_in, pairs, v, tab, result, *scratch):
    size = tab.shape[1]
    high, width = result.shape
    parts = row_parts(high, cols)
    chunks = row_chunks(high, cols)
    firsts = [sum(p[0] for p in parts[:i]) for i in range(len(parts))]
    scratch = list(scratch)
    colbuf = [scratch.pop(0) for _ in range(PARTS_A)]
    rowbuf = [scratch.pop(0) for _ in parts]
    (own_tab, beta_tab, help_tab, alpha_signs, beta_signs, help_signs, shared,
     out, pairs_v, pairs_s, links, counts, integrals, alpha_coef, beta_coef, help_coef,
     ssem, rsem, lsem) = scratch

    wide = width // PARTS_A
    spread = rows // cols
    blocks_b = blocks * spread
    tables = blocks * link_max
    chips = rows // 2
    reach = chips // 2
    across = chips // 2
    half = blocks // 2
    piece = tables // (2 * PIECES)
    helps = cols >= 4
    early = [k for k, chunk in enumerate(chunks) if chunk[0] < 2]

    r = lax.axis_index("row")
    c = lax.axis_index("col")
    core = lax.rem(r, 2)
    chip = r // 2
    other = r + 1 - 2 * core
    place = jnp.where(chip < across, chip, chips - 1 - (chip - across))

    def chip_at(position):
        position = lax.rem(position + 2 * chips, chips)
        return jnp.where(position < across, position, across + (chips - 1 - position))

    def row_at(position, k):
        return 2 * chip_at(position) + k

    right = (row_at(place + 1, core), c)
    left = (row_at(place - 1, core), c)
    partner = (other, c)
    up = (r, jnp.minimum(c + 1, cols - 1))
    down = (r, jnp.maximum(c - 1, 0))
    has_up = c < cols - 1
    has_down = c > 0
    at_end = (c == 0) | (c == cols - 1)
    inner = jnp.logical_not(at_end)
    helper = (c == 1) | (c == cols - 2)
    aided = jnp.where(c == 1, 0, cols - 1)
    inward = (r, jnp.where(c == 0, 1, cols - 2))

    numbers = ({}, {})

    def number(side, key):
        return numbers[side].setdefault(key, len(numbers[side]))

    plan = []

    def at(time, action, rank=0, length=0.0):
        plan.append((time, rank, length, action))

    def describe(src, dst, group, key, device):
        return pltpu.make_async_remote_copy(
            src_ref=src, dst_ref=dst, send_sem=ssem.at[number(0, group)], recv_sem=rsem.at[number(1, key)],
            device_id=device, device_id_type=MESH)

    def when(cond, action):
        if cond is None:
            action()
        else:
            pl.when(cond)(action)

    def send(src, dst, group, key, device, cond=None):
        when(cond, describe(src, dst, group, key, device).start)

    def arrive(ref, key, cond=None):
        when(cond, pltpu.make_async_copy(ref, ref, rsem.at[number(1, key)]).wait)

    def drain(time, ref, group, cond=None):
        def action():
            wait = pltpu.make_async_copy(ref, ref, ssem.at[number(0, group)]).wait
            when(cond() if cond else None, wait)
        at(time, action, 9, 0.02)

    local = []

    def load(src, dst, cond=None):
        copy = pltpu.make_async_copy(src, dst, lsem.at[len(local)])
        local.append(copy)
        when(cond, copy.start)
        return lambda: when(cond, copy.wait)

    barrier = pltpu.get_barrier_semaphore()
    for k in range(1, rows):
        pl.semaphore_signal(barrier, inc=1, device_id=(lax.rem(r + k, rows), c), device_id_type=MESH)

    @pl.when(has_up)
    def _():
        pl.semaphore_signal(barrier, inc=1, device_id=up, device_id_type=MESH)

    @pl.when(has_down)
    def _():
        pl.semaphore_signal(barrier, inc=1, device_id=down, device_id_type=MESH)

    wait_small = [load(pairs, pairs_v.at[r]), load(links_in, links), load(counts_in, counts),
                  load(integrals_in, integrals)]

    def load_rows(i):
        sem = lsem.at[len(local)]
        first = firsts[i]
        for k in range(blocks_b):
            pltpu.make_async_copy(
                v.at[first // size, pl.ds(first % size, parts[i][0]), pl.ds(k * size, size)],
                rowbuf[i].at[c * blocks_b + k], sem).start()
        ref = rowbuf[i].at[pl.ds(c * blocks_b, blocks_b)]
        local.append(pltpu.make_async_copy(ref, ref, sem))
        return local[-1].wait

    wait_rows = [load_rows(i) for i in range(len(parts))]
    wait_tab = load(tab, own_tab)
    wait_cols = [load(v.at[:, :, pl.ds(j * wide, wide)], colbuf[j].at[pl.ds(r * blocks, blocks)])
                 for j in range(PARTS_A)]

    pl.semaphore_wait(barrier, rows - 1 + has_up.astype(jnp.int32) + has_down.astype(jnp.int32))

    for k in range(1, rows):
        send(pairs, pairs_v.at[r], ("pairs", k), ("pairs", k), (lax.rem(r + k, rows), c))
        drain(15.0, pairs_v.at[r], ("pairs", k))

    reach_up = {1: up, -1: down}

    def ends(k):
        return TILE * (chunks[k][3] + chunks[k][2]) / high

    def arrival(t, k, late):
        far = max(cols - 3, 1)
        tiles = max(1, min(t, far)) if late else min(t, far)
        length = TILE * chunks[k][2] / high
        return ends(k) + TILE * tiles + HOP + (length + HOP) * (t if late else max(t - far, 0))

    def row_chunk(k, tile):
        part, offset, count, _, _ = chunks[k]
        return rowbuf[part].at[pl.ds(tile * blocks_b, blocks_b), pl.ds(offset, count), :]

    def line_own(k, way, cond):
        helped = chunks[k][4]
        position = c if way == 1 else cols - 1 - c
        limit = cols - 2 if helped else cols - 1
        ref = row_chunk(k, c)
        send(ref, ref, ("line", way, 0, helped), ("line", way, k, 0), reach_up[way], cond & (position < limit))

    def line_arrive(k, way, t, edge, forward):
        helped = chunks[k][4]
        last = cols - 2 if helped else cols - 1
        onward = t + 2 <= last if edge else t + 3 <= last
        if onward != forward or (t + 1 > last if edge else t + 2 > last):
            return
        position = c if way == 1 else cols - 1 - c
        cond = position == t + 1 if edge else (position > t + 1) & (position <= last)
        ref = row_chunk(k, jnp.clip(c - way * (1 + t), 0, cols - 1))
        arrive(ref, ("line", way, k, t), cond)
        if onward:
            send(ref, ref, ("line", way, t + 1, helped), ("line", way, k, t + 1), reach_up[way],
                 cond if edge else cond & (position < last))

    def line_finish(i):
        for k, chunk in enumerate(chunks):
            if chunk[0] == i:
                for way in (1, -1):
                    for t in range(cols - 1):
                        for edge in (False, True):
                            line_arrive(k, way, t, edge, False)

    def table_places(s):
        source = c * spread + s
        source_chip = source // 2
        source_place = jnp.where(
            source_chip < across, source_chip, chips - 1 - (source_chip - across))
        distance = lax.rem(place - source_place + chips, chips)
        return lax.rem(source, 2), (distance, lax.rem(chips - distance, chips))

    ring = (right, left)

    def table_part(h, q):
        return pl.ds((h * PIECES + q) * piece, piece)

    def table_stage(s, h, q, d):
        source_core, hops = table_places(s)
        here = (core == source_core) & (hops[h] == d)
        part = table_part(h, q)
        ref = beta_tab.at[s, part]
        src = ref if d else own_tab.at[part]
        if d:
            arrive(ref, ("table", s, h, q), here)
        if d + 1 < chips:
            send(src, ref, ("table", s, h), ("table", s, h, q), ring[h], here)
        send(src, ref, ("tableP", s), ("tableP", s), partner, here)
        if helps:
            send(src, help_tab.at[s, part], ("help", s), ("help", s, h, q), inward, here & at_end)

    def table_finish():
        for s in range(spread):
            source_core, _ = table_places(s)
            arrive(beta_tab.at[s], ("tableP", s), core != source_core)
            table_loads[s]()

    def help_arrive(s, h, q):
        source_core = table_places(s)[0]
        aided_core = lax.rem(aided * spread + s, 2)
        ref = help_tab.at[s, table_part(h, q)]
        arrive(ref, ("help", s, h, q), helper & (core == aided_core))
        send(ref, ref, ("helpP", s), ("helpP", s), partner, helper & (core == aided_core))

    def help_finish():
        for s in range(spread):
            aided_core = lax.rem(aided * spread + s, 2)
            arrive(help_tab.at[s], ("helpP", s), helper & (core != aided_core))

    def narrow(value):
        return value.astype(jnp.float32).astype(jnp.bfloat16)

    def widen(source, base, target):
        @pl.loop(0, tables)
        def _(index):
            values = narrow(source[index])
            target[base + index] = jnp.concatenate([values, values], axis=1)

    def couple(source, base, target):
        @pl.loop(0, tables // 2)
        def _(index):
            target[base + index] = jnp.concatenate(
                [narrow(source[2 * index]), narrow(source[2 * index + 1])], axis=1)

    def couple_all(source, target):
        for s in range(spread):
            couple(source.at[s], s * (tables // 2), target)

    def tile_half(j, hb, position, k):
        return colbuf[j].at[pl.ds(row_at(position, k) * blocks + hb * half, half)]

    def ring_own(j, hb, way, cond):
        ref = colbuf[j].at[pl.ds(r * blocks + hb * half, half)]
        send(ref, ref, ("ring", way, 0), ("ring", way, j, hb, 0), ring[way], cond)

    def carried(way, hb, t):
        return t < reach - 1 or hb == way

    def ring_arrive(j, hb, way, t):
        ref = tile_half(j, hb, place - 1 - t if way == 0 else place + 1 + t, core)
        arrive(ref, ("ring", way, j, hb, t))
        if t + 1 < reach and carried(way, hb, t + 1):
            send(ref, ref, ("ring", way, t + 1), ("ring", way, j, hb, t + 1), ring[way])
        send(ref, ref, ("ringP", way, t), ("tiles", j), partner)

    def ring_finish(j):
        arrive(colbuf[j].at[pl.ds(0, chips * blocks)], ("tiles", j))

    def coefficients(target, first, count):
        @pl.loop(0, count)
        def _(b):
            block = first + b
            for l in range(link_max):
                pair = pairs_s[lax.div(block, blocks), lax.rem(block, blocks), l]
                norb = integrals.shape[0]
                value = integrals[lax.div(pair, norb), lax.rem(pair, norb)]
                target[b, l] = value * jnp.clip(counts[block] - l, 0, 1).astype(jnp.float32)

    def gather_pairs():
        for wait in wait_small:
            wait()
        for k in range(1, rows):
            arrive(pairs_v.at[lax.rem(r - k + rows, rows)], ("pairs", k))
        copy = pltpu.make_async_copy(pairs_v, pairs_s, lsem.at[0])
        copy.start()
        copy.wait()
        coefficients(alpha_coef, r * blocks, blocks)
        coefficients(beta_coef, c * blocks_b, blocks_b)
        if helps:
            coefficients(help_coef, aided * blocks_b, blocks_b)

    def alpha_compute(j):
        @pl.loop(0, blocks)
        def _(block):
            total = jnp.zeros((size, wide), jnp.float32)
            for l in range(link_max):
                source = links[l, r * blocks + block]
                up_part, low_part = split(colbuf[j][source] * alpha_coef[block, l])
                total = total + jnp.dot(
                    alpha_signs[block * link_max + l], jnp.concatenate([up_part, low_part], axis=0),
                    preferred_element_type=jnp.float32)
            where = (pl.ds(pl.multiple_of(block * size, size), size), pl.ds(j * wide, wide))
            out[where] = out[where] + total

    def beta_compute(group, owner, coef, signs, target, start, add):
        count = sum(parts[i][0] for i in group)

        @pl.loop(0, blocks_b)
        def _(block):
            total = jnp.zeros((2 * count, size), jnp.float32)
            for l in range(0, link_max, 2):
                highs, lows = [], []
                for m in (l, l + 1):
                    source = links[m, owner * blocks_b + block]
                    value = jnp.concatenate([rowbuf[i][source] for i in group], axis=0)
                    up_part, low_part = split(value * coef[block, m])
                    highs.append(up_part)
                    lows.append(low_part)
                value = jnp.concatenate(
                    [jnp.concatenate(highs, axis=1), jnp.concatenate(lows, axis=1)], axis=0)
                total = total + lax.dot_general(
                    value, signs[block * (link_max // 2) + l // 2],
                    (((1,), (1,)), ((), ())), preferred_element_type=jnp.float32)
            total = total[:count] + total[count:]
            where = (pl.ds(start, count), pl.ds(pl.multiple_of(block * size, size), size))
            if add:
                total = target[where] + total
            target[where] = total

    shared_first = sum(height for height, helped in parts if not helped)

    def own_beta(group, cond):
        def action():
            beta_compute(group, c, beta_coef, beta_signs, out, firsts[group[0]], True)
        when(cond, action)

    def help_beta(i):
        @pl.when(helper)
        def _():
            beta_compute([i], aided, help_coef, help_signs, shared, firsts[i] - shared_first, False)

        ref = shared.at[pl.ds(firsts[i] - shared_first, parts[i][0])]
        send(ref, ref, ("sums",), ("sums", i), (r, aided), helper)

    def take_sums(i):
        ref = shared.at[pl.ds(firsts[i] - shared_first, parts[i][0])]
        arrive(ref, ("sums", i), at_end)

        @pl.when(at_end)
        def _():
            where = pl.ds(firsts[i], parts[i][0])
            out[where, :] = out[where, :] + ref[...]

        flush(firsts[i], parts[i][0], at_end)

    flushes, held, alphas = [], [], []

    def flush(first, count, cond):
        if len(alphas) < PARTS_A:
            held.append((first, count, cond))
            return
        where = pl.ds(first, count)
        flushes.append(load(out.at[where], result.at[where], cond))

    table_loads = []

    def begin():
        always = jnp.bool_(True)
        for k in range(len(chunks)):
            if chunks[k][1] == 0:
                wait_rows[chunks[k][0]]()
            first = k in early or not helps
            line_own(k, 1, always if first else has_down)
            line_own(k, -1, always if first else has_up)
        wait_tab()

    def begin_tables():
        for s in range(spread):
            source_core, hops = table_places(s)
            table_loads.append(load(tab, beta_tab.at[s], (core == source_core) & (hops[0] == 0)))

    def begin_tiles():
        for j in range(PARTS_A):
            wait_cols[j]()

    at(-4.0, begin)
    at(-2.0, begin_tables)
    at(-1.5, begin_tiles)

    def rest():
        for k in range(len(early), len(chunks)):
            line_own(k, 1, c == 0)
            line_own(k, -1, c == cols - 1)

    stage_last = START + PIECE * (PIECES - 1 + chips - 1) + HOP * (chips - 1)
    if helps:
        at(stage_last + 0.1, rest)

    for k in range(len(chunks)):
        helped = chunks[k][4]
        late_k = helps and k not in early
        for way in (1, -1):
            for t in range(cols - 1):
                for edge in (False, True):
                    late = edge and late_k
                    at(START - LEAD + arrival(t, k, late) + (1.5 if t else 0.0),
                       functools.partial(line_arrive, k, way, t, edge, True))

    for helped in (False, True) if helps else (False,):
        count = sum(height for height, aided_part in parts if aided_part == helped)
        last_k = max(k for k, chunk in enumerate(chunks) if chunk[4] == helped)
        last = cols - 2 if helped else cols - 1
        for way in (1, -1):
            for t in range(last):
                def cond(t=t, way=way, last=last):
                    position = c if way == 1 else cols - 1 - c
                    return (position >= t) & (position < last)

                sent = START + arrival(t, last_k, helps and last_k not in early) + (TILE if t == 0 else 0.0)
                drain(sent + 6.0, out.at[pl.ds(0, count)], ("line", way, t, helped), cond)

    for q in range(PIECES):
        for h in range(2):
            for s in range(spread):
                for d in range(chips):
                    time = -1.0 if d == 0 else START + PIECE * (q + d) + HOP * d
                    at(time, functools.partial(table_stage, s, h, q, d))
    for s in range(spread):
        def mine(s=s):
            return core == table_places(s)[0]

        for h in range(2):
            drain(stage_last + 12.0, beta_tab.at[s, pl.ds(0, tables // 2)], ("table", s, h),
                  lambda s=s, h=h: mine(s) & (table_places(s)[1][h] < chips - 1))
        drain(stage_last + 12.0, beta_tab.at[s], ("tableP", s), mine)
        if helps:
            drain(START + 1.8 * TILE, beta_tab.at[s], ("help", s), lambda s=s: mine(s) & at_end)
            drain(START + 1.8 * TILE, beta_tab.at[s], ("helpP", s),
                  lambda s=s: helper & (core == lax.rem(aided * spread + s, 2)))
    at(stage_last + 4.0, table_finish, 1, 0.1)
    at(stage_last + 4.1, lambda: couple_all(beta_tab, beta_signs), 2, 1.0)

    help_ready = 0.0
    if helps:
        for q in range(PIECES):
            for h in range(2):
                time = START + max(
                    ends(len(early) - 1) + PIECE * (q + PIECES + 1) + HOP, PIECE * (q + chips) + HOP * (chips + 1))
                help_ready = max(help_ready, time + 1.5)
                for s in range(spread):
                    at(time + 0.5, functools.partial(help_arrive, s, h, q))
        at(help_ready, help_finish, 1, 0.1)
        at(help_ready + 0.1, lambda: pl.when(helper)(lambda: couple_all(help_tab, help_signs)), 1, 1.0)
        help_ready += 0.2

    order = [(j, second) for second in range(2) for j in range(PARTS_A)]
    step = TILE / (2 * PARTS_A)

    classes = []
    for h in range(2):
        kind = jnp.int32(chips - 1)
        for s in range(spread):
            source_core, hops = table_places(s)
            kind = jnp.where(core == source_core, hops[h], kind)
        classes.append(kind)

    held_back = PARTS_A + 1

    def ring_time(a, t):
        if t == 0 and a < PARTS_A:
            wait = PIECE * (PIECES + max(chips - 2, 0)) + HOP * (chips - 1) + step * (a - 1) + HOP
            return max(stage_last - PIECE - HOP + 0.2, START + (wait if a else 0.0))
        j = a % PARTS_A
        place = PARTS_A + 1 + 2 * j + (1 if t else 0)
        return START + PIECE * PIECES + step * place + 3.0 * HOP + 30.0 * max(t - 1, 0)

    for a, (j, second) in enumerate(order):
        for way in range(2):
            hb = (1 - way) if second else way
            for d in range(chips):
                time = 0.0
                if d < chips - 1 and a >= d:
                    time = START + PIECE * (PIECES - 1 + d) + HOP * d + 0.05 if d else 0.0
                if a >= held_back:
                    time = ring_time(a - held_back, 0) + 0.1
                at(time, functools.partial(ring_own, j, hb, way, classes[way] == d))
            for t in range(reach):
                if carried(way, hb, t):
                    forwards = t + 1 < reach and carried(way, hb, t + 1)
                    at(ring_time(a, t) + (0.0 if forwards else 1.0),
                       functools.partial(ring_arrive, j, hb, way, t), 0 if forwards else 1, 0.03)
    for t in range(reach):
        count = high if t < reach - 1 else high // 2
        for way in range(2):
            drain(ring_time(2 * PARTS_A - 1, t) + 4.0, out.at[pl.ds(0, count)], ("ring", way, t))
            drain(ring_time(2 * PARTS_A - 1, t) + 8.0, out.at[pl.ds(0, count)], ("ringP", way, t))

    def own_pass(j):
        ref = colbuf[j].at[pl.ds(r * blocks, blocks)]
        send(ref, ref, ("own",), ("tiles", j), partner)

    def alpha_step(j):
        ring_finish(j)
        alpha_compute(j)
        alphas.append(j)
        if len(alphas) == PARTS_A:
            for entry in held:
                flush(*entry)

    for j in range(PARTS_A):
        at(0.5, functools.partial(own_pass, j))
        done = max(ring_time(j, reach - 1), ring_time(PARTS_A + j, max(reach - 2, 0))) + 3.0
        at(done, functools.partial(alpha_step, j), 4, 1.4)

    drain(25.0, out, ("own",))

    def prepare():
        out[...] = jnp.zeros_like(out)
        gather_pairs()
        widen(own_tab, 0, alpha_signs)

    at(0.6, prepare, 0, 4.0)

    groups = [[0], [1, 2], [3, 4], [5, 6, 7]]

    def finish_time(i, t):
        k = max(k for k, chunk in enumerate(chunks) if chunk[0] == i)
        return START + arrival(t, k, helps and k not in early) + 0.1

    def help_step(i):
        line_finish(i)
        help_beta(i)

    def own_step(group, finish, cond):
        if finish:
            for i in group:
                line_finish(i)
        own_beta(group, cond)
        flush(firsts[group[0]], sum(parts[i][0] for i in group), cond)

    for i, (height, helped) in enumerate(parts):
        if helped:
            ready = max(finish_time(i, max(cols - 3, 0)), help_ready)
            at(ready, functools.partial(help_step, i), 2, 1.9)
            at(ready + 11.0, functools.partial(take_sums, i), 5, 0.0)
    if helps:
        drain(help_ready + TILE, shared, ("sums",), lambda: helper)
    for group in groups:
        inside, outside = finish_time(group[-1], max(cols - 3, 0)), finish_time(group[-1], cols - 2)
        if parts[group[0]][1]:
            at(max(inside, help_ready) + 0.1, functools.partial(own_step, group, False, inner), 6, 2.6)
        elif helps:
            at(inside + 0.1, functools.partial(own_step, group, False, inner), 6, 2.6)
            at(outside + 0.1, functools.partial(own_step, group, True, at_end), 6, 0.0)
        else:
            at(outside + 0.1, functools.partial(own_step, group, True, None), 6, 2.6)

    for action in in_order(plan):
        action()
    for wait in flushes:
        wait()
    assert len(numbers[0]) == ssem.shape[0] and len(numbers[1]) == rsem.shape[0]
    assert len(local) <= lsem.shape[0]


def local(vector, one_electron, links, counts, pairs, signs, rows, cols):
    blocks, link_max = pairs.shape
    size = signs.shape[2]
    high, width = vector.shape
    spread = rows // cols
    tables = blocks * link_max
    parts = row_parts(high, cols)
    helped = sum(height for height, aided in parts if aided)
    reach = rows // 4
    sends = rows - 1 + 2 * (cols - 1) + 4 * reach + 2 + spread * 3
    arrivals = rows - 1 + PARTS_A * (4 * reach - 1) + spread * (2 * PIECES + 1)
    arrivals += sum(2 * (cols - 2 if chunk[4] else cols - 1) for chunk in row_chunks(high, cols))
    if cols >= 4:
        sends += 2 * (cols - 2) + spread * 2
        arrivals += len(parts) - 1 + spread * (2 * PIECES + 1)
    scratch = [pltpu.VMEM((rows * blocks, size, width // PARTS_A), jnp.float32)] * PARTS_A
    scratch += [pltpu.VMEM((cols * blocks * spread, height, size), jnp.float32) for height, _ in parts]
    scratch += [
        pltpu.VMEM((tables, size, size), jnp.int32),
        pltpu.VMEM((spread, tables, size, size), jnp.int32),
        pltpu.VMEM((spread, tables, size, size), jnp.int32),
        pltpu.VMEM((tables, size, 2 * size), jnp.bfloat16),
        pltpu.VMEM((spread * tables // 2, size, 2 * size), jnp.bfloat16),
        pltpu.VMEM((spread * tables // 2, size, 2 * size), jnp.bfloat16),
        pltpu.VMEM((max(helped, 8), width), jnp.float32),
        pltpu.VMEM((high, width), jnp.float32),
        pltpu.VMEM((rows, blocks, link_max), jnp.int32),
        pltpu.SMEM((rows, blocks, link_max), jnp.int32),
        pltpu.SMEM((link_max, links.shape[0]), jnp.int32),
        pltpu.SMEM(counts.shape, jnp.int32),
        pltpu.SMEM(one_electron.shape, jnp.float32),
        pltpu.SMEM((blocks, link_max), jnp.float32),
        pltpu.SMEM((blocks * spread, link_max), jnp.float32),
        pltpu.SMEM((blocks * spread, link_max), jnp.float32),
        pltpu.SemaphoreType.DMA((sends,)),
        pltpu.SemaphoreType.DMA((arrivals,)),
        pltpu.SemaphoreType.DMA((8 + 3 * len(parts) + PARTS_A + spread,)),
    ]
    far = pl.BlockSpec(memory_space=pltpu.HBM)
    operands = (links.T, counts, one_electron, pairs, vector.reshape(blocks, size, width),
                signs.reshape(tables, size, size))
    return pl.pallas_call(
        functools.partial(kernel, rows, cols, blocks, link_max),
        out_shape=jax.ShapeDtypeStruct(vector.shape, jnp.float32),
        in_specs=[far] * 6,
        out_specs=pl.BlockSpec(memory_space=pl.ANY),
        scratch_shapes=scratch,
        compiler_params=pltpu.CompilerParams(
            collective_id=0, has_side_effects=True, vmem_limit_bytes=48 << 20),
    )(*[pltpu.with_memory_space_constraint(value, pltpu.HBM) for value in operands])


def solution(mesh):
    in_specs = (P("row", "col"), P(), P(), P(), P("row", None), P("row", None, None, None))
    out_specs = P("row", "col")
    body = functools.partial(local, rows=mesh.shape["row"], cols=mesh.shape["col"])
    return jax.shard_map(body, mesh=mesh, in_specs=in_specs, out_specs=out_specs, check_vma=False)
```

```python
import functools

import jax
import jax.numpy as jnp
from jax import lax
from jax.experimental import pallas as pl
from jax.experimental.pallas import tpu as pltpu
from jax.sharding import PartitionSpec as P

MESH = pl.DeviceIdType.MESH
PARTS_A = 4
PIECES = 4
START = 4.5
LEAD = 2.5
SLACK = 0.7
TILE = 45.0
HOP = 1.5
PIECE = 5.6


def split(value):
    high = value.astype(jnp.bfloat16)
    low = (value - high.astype(jnp.float32)).astype(jnp.bfloat16)
    return high, low


def row_parts(high, cols):
    helps = cols >= 4
    return [(high // 4, False)] * 2 + [(high // 16, helps)] * 7 + [(high // 32, helps)] * 2


def row_chunks(high, cols):
    chunks, first = [], 0
    for part, (height, helped) in enumerate(row_parts(high, cols)):
        piece = min(height, high // 16 if part else high // 8)
        for offset in range(0, height, piece):
            chunks.append((part, offset, piece, first + offset, helped))
        first += height
    return chunks


def in_order(plan):
    left = sorted(enumerate(plan), key=lambda entry: (entry[1][0], entry[0]))
    urgent = [entry for entry in left if entry[1][1] <= 2]
    now, result = 0.0, []
    while left:
        ready = [entry for entry in left if entry[1][0] <= now]
        soon = [entry for entry in urgent if entry[1][0] > now][:1]
        if soon:
            room = soon[0][1][0] - now + SLACK
            ready = [entry for entry in ready if entry[1][1] <= 2 or entry[1][2] <= room]
        if not ready:
            now = min(entry[1][0] for entry in (soon or left))
            ready = [entry for entry in left if entry[1][0] <= now and entry[1][1] <= 2] or left[:1]
        chosen = min(ready, key=lambda entry: (entry[1][1], entry[1][0], entry[0]))
        left.remove(chosen)
        if chosen[1][1] <= 2:
            urgent.remove(chosen)
        start, _, length, action = chosen[1]
        now = max(now, start) + length
        result.append(action)
    return result


def kernel(rows, cols, blocks, link_max, links_in, counts_in, integrals_in, pairs, v, tab, result, *scratch):
    size = tab.shape[1]
    high, width = result.shape
    parts = row_parts(high, cols)
    chunks = row_chunks(high, cols)
    firsts = [sum(p[0] for p in parts[:i]) for i in range(len(parts))]
    scratch = list(scratch)
    colbuf = [scratch.pop(0) for _ in range(PARTS_A)]
    rowbuf = [scratch.pop(0) for _ in parts]
    (own_tab, beta_tab, help_tab, alpha_signs, beta_signs, help_signs, shared,
     out, pairs_v, pairs_s, links, counts, integrals, alpha_coef, beta_coef, help_coef,
     ssem, rsem, lsem) = scratch

    wide = width // PARTS_A
    spread = rows // cols
    blocks_b = blocks * spread
    tables = blocks * link_max
    chips = rows // 2
    reach = chips // 2
    across = chips // 2
    half = blocks // 2
    piece = tables // (2 * PIECES)
    helps = cols >= 4
    early = [k for k, chunk in enumerate(chunks) if chunk[0] < 2]

    r = lax.axis_index("row")
    c = lax.axis_index("col")
    core = lax.rem(r, 2)
    chip = r // 2
    other = r + 1 - 2 * core
    place = jnp.where(chip < across, chip, chips - 1 - (chip - across))

    def chip_at(position):
        position = lax.rem(position + 2 * chips, chips)
        return jnp.where(position < across, position, across + (chips - 1 - position))

    def row_at(position, k):
        return 2 * chip_at(position) + k

    right = (row_at(place + 1, core), c)
    left = (row_at(place - 1, core), c)
    partner = (other, c)
    up = (r, jnp.minimum(c + 1, cols - 1))
    down = (r, jnp.maximum(c - 1, 0))
    has_up = c < cols - 1
    has_down = c > 0
    at_end = (c == 0) | (c == cols - 1)
    inner = jnp.logical_not(at_end)
    helper = (c == 1) | (c == cols - 2)
    aided = jnp.where(c == 1, 0, cols - 1)
    inward = (r, jnp.where(c == 0, 1, cols - 2))

    numbers = ({}, {})

    def number(side, key):
        return numbers[side].setdefault(key, len(numbers[side]))

    plan = []

    def at(time, action, rank=0, length=0.0):
        plan.append((time, rank, length, action))

    def describe(src, dst, group, key, device):
        return pltpu.make_async_remote_copy(
            src_ref=src, dst_ref=dst, send_sem=ssem.at[number(0, group)], recv_sem=rsem.at[number(1, key)],
            device_id=device, device_id_type=MESH)

    def when(cond, action):
        if cond is None:
            action()
        else:
            pl.when(cond)(action)

    def send(src, dst, group, key, device, cond=None):
        when(cond, describe(src, dst, group, key, device).start)

    def arrive(ref, key, cond=None):
        when(cond, pltpu.make_async_copy(ref, ref, rsem.at[number(1, key)]).wait)

    def drain(time, ref, group, cond=None):
        def action():
            wait = pltpu.make_async_copy(ref, ref, ssem.at[number(0, group)]).wait
            when(cond() if cond else None, wait)
        at(time, action, 9, 0.02)

    local = []

    def load(src, dst, cond=None):
        copy = pltpu.make_async_copy(src, dst, lsem.at[len(local)])
        local.append(copy)
        when(cond, copy.start)
        return lambda: when(cond, copy.wait)

    barrier = pltpu.get_barrier_semaphore()
    for k in range(1, rows):
        pl.semaphore_signal(barrier, inc=1, device_id=(lax.rem(r + k, rows), c), device_id_type=MESH)

    @pl.when(has_up)
    def _():
        pl.semaphore_signal(barrier, inc=1, device_id=up, device_id_type=MESH)

    @pl.when(has_down)
    def _():
        pl.semaphore_signal(barrier, inc=1, device_id=down, device_id_type=MESH)

    wait_small = [load(pairs, pairs_v.at[r]), load(links_in, links), load(counts_in, counts),
                  load(integrals_in, integrals)]

    def load_rows(i):
        sem = lsem.at[len(local)]
        first = firsts[i]
        for k in range(blocks_b):
            pltpu.make_async_copy(
                v.at[first // size, pl.ds(first % size, parts[i][0]), pl.ds(k * size, size)],
                rowbuf[i].at[c * blocks_b + k], sem).start()
        ref = rowbuf[i].at[pl.ds(c * blocks_b, blocks_b)]
        local.append(pltpu.make_async_copy(ref, ref, sem))
        return local[-1].wait

    wait_rows = [load_rows(i) for i in range(len(parts))]
    wait_tab = load(tab, own_tab)
    wait_cols = [load(v.at[:, :, pl.ds(j * wide, wide)], colbuf[j].at[pl.ds(r * blocks, blocks)])
                 for j in range(PARTS_A)]

    pl.semaphore_wait(barrier, rows - 1 + has_up.astype(jnp.int32) + has_down.astype(jnp.int32))

    for k in range(1, rows):
        send(pairs, pairs_v.at[r], ("pairs", k), ("pairs", k), (lax.rem(r + k, rows), c))
        drain(15.0, pairs_v.at[r], ("pairs", k))

    reach_up = {1: up, -1: down}

    def ends(k):
        return TILE * (chunks[k][3] + chunks[k][2]) / high

    def arrival(t, k, late):
        far = max(cols - 3, 1)
        tiles = max(1, min(t, far)) if late else min(t, far)
        length = TILE * chunks[k][2] / high
        return ends(k) + TILE * tiles + HOP + (length + HOP) * (t if late else max(t - far, 0))

    def row_chunk(k, tile):
        part, offset, count, _, _ = chunks[k]
        return rowbuf[part].at[pl.ds(tile * blocks_b, blocks_b), pl.ds(offset, count), :]

    def line_own(k, way, cond):
        helped = chunks[k][4]
        position = c if way == 1 else cols - 1 - c
        limit = cols - 2 if helped else cols - 1
        ref = row_chunk(k, c)
        send(ref, ref, ("line", way, 0, helped), ("line", way, k, 0), reach_up[way], cond & (position < limit))

    def line_arrive(k, way, t, edge, forward):
        helped = chunks[k][4]
        last = cols - 2 if helped else cols - 1
        onward = t + 2 <= last if edge else t + 3 <= last
        if onward != forward or (t + 1 > last if edge else t + 2 > last):
            return
        position = c if way == 1 else cols - 1 - c
        cond = position == t + 1 if edge else (position > t + 1) & (position <= last)
        ref = row_chunk(k, jnp.clip(c - way * (1 + t), 0, cols - 1))
        arrive(ref, ("line", way, k, t), cond)
        if onward:
            send(ref, ref, ("line", way, t + 1, helped), ("line", way, k, t + 1), reach_up[way],
                 cond if edge else cond & (position < last))

    def line_finish(i):
        for k, chunk in enumerate(chunks):
            if chunk[0] == i:
                for way in (1, -1):
                    for t in range(cols - 1):
                        for edge in (False, True):
                            line_arrive(k, way, t, edge, False)

    def table_places(s):
        source = c * spread + s
        source_chip = source // 2
        source_place = jnp.where(
            source_chip < across, source_chip, chips - 1 - (source_chip - across))
        distance = lax.rem(place - source_place + chips, chips)
        return lax.rem(source, 2), (distance, lax.rem(chips - distance, chips))

    ring = (right, left)

    def table_part(h, q):
        return pl.ds((h * PIECES + q) * piece, piece)

    def table_stage(s, h, q, d):
        source_core, hops = table_places(s)
        here = (core == source_core) & (hops[h] == d)
        part = table_part(h, q)
        ref = beta_tab.at[s, part]
        src = ref if d else own_tab.at[part]
        if d:
            arrive(ref, ("table", s, h, q), here)
        if d + 1 < chips:
            send(src, ref, ("table", s, h), ("table", s, h, q), ring[h], here)
        send(src, ref, ("tableP", s), ("tableP", s), partner, here)
        if helps:
            send(src, help_tab.at[s, part], ("help", s), ("help", s, h, q), inward, here & at_end)

    def table_finish():
        for s in range(spread):
            source_core, _ = table_places(s)
            arrive(beta_tab.at[s], ("tableP", s), core != source_core)
            table_loads[s]()

    def help_arrive(s, h, q):
        source_core = table_places(s)[0]
        aided_core = lax.rem(aided * spread + s, 2)
        ref = help_tab.at[s, table_part(h, q)]
        arrive(ref, ("help", s, h, q), helper & (core == aided_core))
        send(ref, ref, ("helpP", s), ("helpP", s), partner, helper & (core == aided_core))

    def help_finish():
        for s in range(spread):
            aided_core = lax.rem(aided * spread + s, 2)
            arrive(help_tab.at[s], ("helpP", s), helper & (core != aided_core))

    def narrow(value):
        return value.astype(jnp.float32).astype(jnp.bfloat16)

    def widen(source, base, target):
        @pl.loop(0, tables)
        def _(index):
            values = narrow(source[index])
            target[base + index] = jnp.concatenate([values, values], axis=1)

    def couple(source, base, target):
        @pl.loop(0, tables // 2)
        def _(index):
            target[base + index] = jnp.concatenate(
                [narrow(source[2 * index]), narrow(source[2 * index + 1])], axis=1)

    def couple_all(source, target):
        for s in range(spread):
            couple(source.at[s], s * (tables // 2), target)

    def tile_half(j, hb, position, k):
        return colbuf[j].at[pl.ds(row_at(position, k) * blocks + hb * half, half)]

    def ring_own(j, hb, way, cond):
        ref = colbuf[j].at[pl.ds(r * blocks + hb * half, half)]
        send(ref, ref, ("ring", way, 0), ("ring", way, j, hb, 0), ring[way], cond)

    def carried(way, hb, t):
        return t < reach - 1 or hb == way

    def ring_arrive(j, hb, way, t):
        ref = tile_half(j, hb, place - 1 - t if way == 0 else place + 1 + t, core)
        arrive(ref, ("ring", way, j, hb, t))
        if t + 1 < reach and carried(way, hb, t + 1):
            send(ref, ref, ("ring", way, t + 1), ("ring", way, j, hb, t + 1), ring[way])
        send(ref, ref, ("ringP", way, t), ("tiles", j), partner)

    def ring_finish(j):
        arrive(colbuf[j].at[pl.ds(0, chips * blocks)], ("tiles", j))

    def coefficients(target, first, count):
        @pl.loop(0, count)
        def _(b):
            block = first + b
            for l in range(link_max):
                pair = pairs_s[lax.div(block, blocks), lax.rem(block, blocks), l]
                norb = integrals.shape[0]
                value = integrals[lax.div(pair, norb), lax.rem(pair, norb)]
                target[b, l] = value * jnp.clip(counts[block] - l, 0, 1).astype(jnp.float32)

    def gather_pairs():
        for wait in wait_small:
            wait()
        for k in range(1, rows):
            arrive(pairs_v.at[lax.rem(r - k + rows, rows)], ("pairs", k))
        copy = pltpu.make_async_copy(pairs_v, pairs_s, lsem.at[0])
        copy.start()
        copy.wait()
        coefficients(alpha_coef, r * blocks, blocks)
        coefficients(beta_coef, c * blocks_b, blocks_b)
        if helps:
            coefficients(help_coef, aided * blocks_b, blocks_b)

    def trips(first, last, body):
        together = max(u for u in (4, 2, 1) if (last - first) % u == 0)

        @pl.loop(0, (last - first) // together)
        def _(trip):
            for turn in range(together):
                body(first + trip * together + turn)

    def alpha_compute(j):
        def body(block):
            total = None
            for l in range(link_max):
                source = links[l, r * blocks + block]
                up_part, low_part = split(colbuf[j][source] * alpha_coef[block, l])
                term = jnp.dot(
                    alpha_signs[block * link_max + l], jnp.concatenate([up_part, low_part], axis=0),
                    preferred_element_type=jnp.float32)
                total = term if total is None else total + term
            where = (pl.ds(pl.multiple_of(block * size, size), size), pl.ds(j * wide, wide))
            out[where] = out[where] + total

        trips(0, blocks, body)

    def beta_compute(group, owner, coef, signs, target, start, add, span=None):
        count = sum(parts[i][0] for i in group)

        def body(block):
            total = None
            for l in range(0, link_max, 2):
                highs, lows = [], []
                for m in (l, l + 1):
                    source = links[m, owner * blocks_b + block]
                    value = jnp.concatenate([rowbuf[i][source] for i in group], axis=0)
                    up_part, low_part = split(value * coef[block, m])
                    highs.append(up_part)
                    lows.append(low_part)
                value = jnp.concatenate(
                    [jnp.concatenate(highs, axis=1), jnp.concatenate(lows, axis=1)], axis=0)
                term = lax.dot_general(
                    value, signs[block * (link_max // 2) + l // 2],
                    (((1,), (1,)), ((), ())), preferred_element_type=jnp.float32)
                total = term if total is None else total + term
            total = total[:count] + total[count:]
            where = (pl.ds(start, count), pl.ds(pl.multiple_of(block * size, size), size))
            if add:
                total = target[where] + total
            target[where] = total

        trips(*(span or (0, blocks_b)), body)

    shared_first = sum(height for height, helped in parts if not helped)

    def own_beta(group, cond, span):
        def action():
            beta_compute(group, c, beta_coef, beta_signs, out, firsts[group[0]], True, span)
        when(cond, action)

    def help_beta(i):
        @pl.when(helper)
        def _():
            beta_compute([i], aided, help_coef, help_signs, shared, firsts[i] - shared_first, False)

        ref = shared.at[pl.ds(firsts[i] - shared_first, parts[i][0])]
        send(ref, ref, ("sums",), ("sums", i), (r, aided), helper)

    def take_sums(i):
        ref = shared.at[pl.ds(firsts[i] - shared_first, parts[i][0])]
        arrive(ref, ("sums", i), at_end)

        @pl.when(at_end)
        def _():
            where = pl.ds(firsts[i], parts[i][0])
            out[where, :] = out[where, :] + ref[...]

        flush(firsts[i], parts[i][0], at_end)

    flushes, held, alphas = [], [], []

    def flush(first, count, cond):
        if len(alphas) < PARTS_A:
            held.append((first, count, cond))
            return
        where = pl.ds(first, count)
        flushes.append(load(out.at[where], result.at[where], cond))

    table_loads = []

    def begin():
        always = jnp.bool_(True)
        for k in range(len(chunks)):
            if chunks[k][1] == 0:
                wait_rows[chunks[k][0]]()
            first = k in early or not helps
            line_own(k, 1, always if first else has_down)
            line_own(k, -1, always if first else has_up)
        wait_tab()

    def begin_tables():
        for s in range(spread):
            source_core, hops = table_places(s)
            table_loads.append(load(tab, beta_tab.at[s], (core == source_core) & (hops[0] == 0)))

    def begin_tiles():
        for j in range(PARTS_A):
            wait_cols[j]()

    at(-4.0, begin)
    at(-2.0, begin_tables)
    at(-1.5, begin_tiles)

    def rest():
        for k in range(len(early), len(chunks)):
            line_own(k, 1, c == 0)
            line_own(k, -1, c == cols - 1)

    stage_last = START + PIECE * (PIECES - 1 + chips - 1) + HOP * (chips - 1)
    if helps:
        at(stage_last + 0.1, rest)

    for k in range(len(chunks)):
        helped = chunks[k][4]
        late_k = helps and k not in early
        for way in (1, -1):
            for t in range(cols - 1):
                for edge in (False, True):
                    late = edge and late_k
                    at(START - LEAD + arrival(t, k, late) + (1.5 if t else 0.0),
                       functools.partial(line_arrive, k, way, t, edge, True))

    for helped in (False, True) if helps else (False,):
        count = sum(height for height, aided_part in parts if aided_part == helped)
        last_k = max(k for k, chunk in enumerate(chunks) if chunk[4] == helped)
        last = cols - 2 if helped else cols - 1
        for way in (1, -1):
            for t in range(last):
                def cond(t=t, way=way, last=last):
                    position = c if way == 1 else cols - 1 - c
                    return (position >= t) & (position < last)

                sent = START + arrival(t, last_k, helps and last_k not in early) + (TILE if t == 0 else 0.0)
                drain(sent + 6.0, out.at[pl.ds(0, count)], ("line", way, t, helped), cond)

    for q in range(PIECES):
        for h in range(2):
            for s in range(spread):
                for d in range(chips):
                    time = -1.0 if d == 0 else START + PIECE * (q + d) + HOP * d
                    at(time, functools.partial(table_stage, s, h, q, d))
    for s in range(spread):
        def mine(s=s):
            return core == table_places(s)[0]

        for h in range(2):
            drain(stage_last + 12.0, beta_tab.at[s, pl.ds(0, tables // 2)], ("table", s, h),
                  lambda s=s, h=h: mine(s) & (table_places(s)[1][h] < chips - 1))
        drain(stage_last + 12.0, beta_tab.at[s], ("tableP", s), mine)
        if helps:
            drain(START + 1.8 * TILE, beta_tab.at[s], ("help", s), lambda s=s: mine(s) & at_end)
            drain(START + 1.8 * TILE, beta_tab.at[s], ("helpP", s),
                  lambda s=s: helper & (core == lax.rem(aided * spread + s, 2)))
    at(stage_last + 4.0, table_finish, 1, 0.1)
    at(stage_last + 4.1, lambda: couple_all(beta_tab, beta_signs), 2, 1.0)

    help_ready = 0.0
    if helps:
        for q in range(PIECES):
            for h in range(2):
                time = START + max(
                    ends(len(early) - 1) + PIECE * (q + PIECES + 1) + HOP, PIECE * (q + chips) + HOP * (chips + 1))
                help_ready = max(help_ready, time + 1.5)
                for s in range(spread):
                    at(time + 0.5, functools.partial(help_arrive, s, h, q))
        at(help_ready, help_finish, 1, 0.1)
        at(help_ready + 0.1, lambda: pl.when(helper)(lambda: couple_all(help_tab, help_signs)), 1, 1.0)
        help_ready += 0.2

    order = [(j, second) for second in range(2) for j in range(PARTS_A)]
    step = TILE / (2 * PARTS_A)

    classes = []
    for h in range(2):
        kind = jnp.int32(chips - 1)
        for s in range(spread):
            source_core, hops = table_places(s)
            kind = jnp.where(core == source_core, hops[h], kind)
        classes.append(kind)

    held_back = PARTS_A + 1

    def ring_time(a, t):
        if t == 0 and a < PARTS_A:
            wait = PIECE * (PIECES + max(chips - 2, 0)) + HOP * (chips - 1) + step * (a - 1) + HOP
            return max(stage_last - PIECE - HOP + 0.2, START + (wait if a else 0.0))
        j = a % PARTS_A
        place = PARTS_A + 1 + 2 * j + (1 if t else 0)
        return START + PIECE * PIECES + step * place + 3.0 * HOP + 30.0 * max(t - 1, 0)

    for a, (j, second) in enumerate(order):
        for way in range(2):
            hb = (1 - way) if second else way
            for d in range(chips):
                time = 0.0
                if d < chips - 1 and a >= d:
                    time = START + PIECE * (PIECES - 1 + d) + HOP * d + 0.05 if d else 0.0
                if a >= held_back:
                    time = ring_time(a - held_back, 0) + 0.1
                at(time, functools.partial(ring_own, j, hb, way, classes[way] == d))
            for t in range(reach):
                if carried(way, hb, t):
                    forwards = t + 1 < reach and carried(way, hb, t + 1)
                    at(ring_time(a, t) + (0.0 if forwards else 1.0),
                       functools.partial(ring_arrive, j, hb, way, t), 0 if forwards else 1, 0.03)
    for t in range(reach):
        count = high if t < reach - 1 else high // 2
        for way in range(2):
            drain(ring_time(2 * PARTS_A - 1, t) + 4.0, out.at[pl.ds(0, count)], ("ring", way, t))
            drain(ring_time(2 * PARTS_A - 1, t) + 8.0, out.at[pl.ds(0, count)], ("ringP", way, t))

    def own_pass(j):
        ref = colbuf[j].at[pl.ds(r * blocks, blocks)]
        send(ref, ref, ("own",), ("tiles", j), partner)

    def alpha_step(j):
        ring_finish(j)
        alpha_compute(j)
        alphas.append(j)
        if len(alphas) == PARTS_A:
            for entry in held:
                flush(*entry)

    for j in range(PARTS_A):
        at(0.5, functools.partial(own_pass, j))
        done = max(ring_time(j, reach - 1), ring_time(PARTS_A + j, max(reach - 2, 0))) + 4.5
        at(done, functools.partial(alpha_step, j), 4, 0.9)

    drain(25.0, out, ("own",))

    def prepare():
        out[...] = jnp.zeros_like(out)
        gather_pairs()
        widen(own_tab, 0, alpha_signs)

    at(0.6, prepare, 0, 4.0)

    groups = [[0, 1], [2, 3, 4, 5], [6, 7, 8, 9, 10]]

    def finish_time(i, t):
        k = max(k for k, chunk in enumerate(chunks) if chunk[0] == i)
        return START - LEAD + 1.0 + arrival(t, k, helps and k not in early)

    def help_step(i):
        line_finish(i)
        help_beta(i)

    def own_step(group, finish, cond, turn=0, turns=1):
        if finish and not turn:
            for i in group:
                line_finish(i)
        span = (blocks_b * turn // turns, blocks_b * (turn + 1) // turns)
        own_beta(group, cond, span)
        if turn == turns - 1:
            flush(firsts[group[0]], sum(parts[i][0] for i in group), cond)

    for i, (height, helped) in enumerate(parts):
        if helped:
            ready = max(finish_time(i, max(cols - 3, 0)), help_ready)
            at(ready, functools.partial(help_step, i), 2, 1.0)
            at(ready + 11.0, functools.partial(take_sums, i), 5, 0.0)
    if helps:
        drain(help_ready + TILE, shared, ("sums",), lambda: helper)
    for group in groups:
        inside, outside = finish_time(group[-1], max(cols - 3, 0)), finish_time(group[-1], cols - 2)
        if not helps:
            at(outside + 0.1, functools.partial(own_step, group, True, None), 6, 2.6)
            continue
        for turn in range(2):
            at(max(inside, help_ready if parts[group[0]][1] else 0.0) + 0.1 + 0.01 * turn,
               functools.partial(own_step, group, False, inner, turn, 2), 6, 0.9)
        if not parts[group[0]][1]:
            at(outside + 0.1, functools.partial(own_step, group, True, at_end), 6, 0.0)

    for action in in_order(plan):
        action()
    for wait in flushes:
        wait()
    assert len(numbers[0]) == ssem.shape[0] and len(numbers[1]) == rsem.shape[0]
    assert len(local) <= lsem.shape[0]


def local(vector, one_electron, links, counts, pairs, signs, rows, cols):
    blocks, link_max = pairs.shape
    size = signs.shape[2]
    high, width = vector.shape
    spread = rows // cols
    tables = blocks * link_max
    parts = row_parts(high, cols)
    helped = sum(height for height, aided in parts if aided)
    reach = rows // 4
    sends = rows - 1 + 2 * (cols - 1) + 4 * reach + 2 + spread * 3
    arrivals = rows - 1 + PARTS_A * (4 * reach - 1) + spread * (2 * PIECES + 1)
    arrivals += sum(2 * (cols - 2 if chunk[4] else cols - 1) for chunk in row_chunks(high, cols))
    if cols >= 4:
        sends += 2 * (cols - 2) + spread * 2
        arrivals += sum(1 for _, aided in parts if aided) + spread * (2 * PIECES + 1)
    scratch = [pltpu.VMEM((rows * blocks, size, width // PARTS_A), jnp.float32)] * PARTS_A
    scratch += [pltpu.VMEM((cols * blocks * spread, height, size), jnp.float32) for height, _ in parts]
    scratch += [
        pltpu.VMEM((tables, size, size), jnp.int32),
        pltpu.VMEM((spread, tables, size, size), jnp.int32),
        pltpu.VMEM((spread, tables, size, size), jnp.int32),
        pltpu.VMEM((tables, size, 2 * size), jnp.bfloat16),
        pltpu.VMEM((spread * tables // 2, size, 2 * size), jnp.bfloat16),
        pltpu.VMEM((spread * tables // 2, size, 2 * size), jnp.bfloat16),
        pltpu.VMEM((max(helped, 8), width), jnp.float32),
        pltpu.VMEM((high, width), jnp.float32),
        pltpu.VMEM((rows, blocks, link_max), jnp.int32),
        pltpu.SMEM((rows, blocks, link_max), jnp.int32),
        pltpu.SMEM((link_max, links.shape[0]), jnp.int32),
        pltpu.SMEM(counts.shape, jnp.int32),
        pltpu.SMEM(one_electron.shape, jnp.float32),
        pltpu.SMEM((blocks, link_max), jnp.float32),
        pltpu.SMEM((blocks * spread, link_max), jnp.float32),
        pltpu.SMEM((blocks * spread, link_max), jnp.float32),
        pltpu.SemaphoreType.DMA((sends,)),
        pltpu.SemaphoreType.DMA((arrivals,)),
        pltpu.SemaphoreType.DMA((8 + 3 * len(parts) + PARTS_A + spread,)),
    ]
    far = pl.BlockSpec(memory_space=pltpu.HBM)
    operands = (links.T, counts, one_electron, pairs, vector.reshape(blocks, size, width),
                signs.reshape(tables, size, size))
    return pl.pallas_call(
        functools.partial(kernel, rows, cols, blocks, link_max),
        out_shape=jax.ShapeDtypeStruct(vector.shape, jnp.float32),
        in_specs=[far] * 6,
        out_specs=pl.BlockSpec(memory_space=pl.ANY),
        scratch_shapes=scratch,
        compiler_params=pltpu.CompilerParams(
            collective_id=0, has_side_effects=True, vmem_limit_bytes=48 << 20),
    )(*[pltpu.with_memory_space_constraint(value, pltpu.HBM) for value in operands])


def solution(mesh):
    in_specs = (P("row", "col"), P(), P(), P(), P("row", None), P("row", None, None, None))
    out_specs = P("row", "col")
    body = functools.partial(local, rows=mesh.shape["row"], cols=mesh.shape["col"])
    return jax.shard_map(body, mesh=mesh, in_specs=in_specs, out_specs=out_specs, check_vma=False)
```

```python
import functools

import jax
import jax.numpy as jnp
from jax import lax
from jax.experimental import pallas as pl
from jax.experimental.pallas import tpu as pltpu
from jax.sharding import PartitionSpec as P

MESH = pl.DeviceIdType.MESH
PARTS_A = 4
PIECES = 4
START = 4.5
LEAD = 2.5
SLACK = 0.3
TILE = 45.0
HOP = 1.5
PIECE = 5.6


def split(value):
    high = value.astype(jnp.bfloat16)
    low = (value - high.astype(jnp.float32)).astype(jnp.bfloat16)
    return high, low


def row_parts(high, cols):
    helps = cols >= 4
    return [(high // 4, False)] * 2 + [(high // 32, helps)] * 16


def row_chunks(high, cols):
    chunks, first = [], 0
    for part, (height, helped) in enumerate(row_parts(high, cols)):
        piece = min(height, high // 16 if part else high // 8)
        for offset in range(0, height, piece):
            chunks.append((part, offset, piece, first + offset, helped))
        first += height
    return chunks


def in_order(plan):
    left = sorted(enumerate(plan), key=lambda entry: (entry[1][0], entry[0]))
    urgent = [entry for entry in left if entry[1][1] <= 2]
    now, result = 0.0, []
    while left:
        ready = [entry for entry in left if entry[1][0] <= now]
        soon = [entry for entry in urgent if entry[1][0] > now][:1]
        if soon:
            room = soon[0][1][0] - now + SLACK
            ready = [entry for entry in ready if entry[1][1] <= 2 or entry[1][2] <= room]
        if not ready:
            now = min(entry[1][0] for entry in (soon or left))
            ready = [entry for entry in left if entry[1][0] <= now and entry[1][1] <= 2] or left[:1]
        chosen = min(ready, key=lambda entry: (entry[1][1], entry[1][0], entry[0]))
        left.remove(chosen)
        if chosen[1][1] <= 2:
            urgent.remove(chosen)
        start, _, length, action = chosen[1]
        now = max(now, start) + length
        result.append(action)
    return result


def kernel(rows, cols, blocks, link_max, links_in, counts_in, integrals_in, pairs, v, tab, result, *scratch):
    size = tab.shape[1]
    high, width = result.shape
    parts = row_parts(high, cols)
    chunks = row_chunks(high, cols)
    firsts = [sum(p[0] for p in parts[:i]) for i in range(len(parts))]
    scratch = list(scratch)
    colbuf = [scratch.pop(0) for _ in range(PARTS_A)]
    rowbuf = [scratch.pop(0) for _ in parts]
    (own_tab, beta_tab, help_tab, alpha_signs, beta_signs, help_signs, shared,
     out, pairs_v, pairs_s, links, counts, integrals, alpha_coef, beta_coef, help_coef,
     ssem, rsem, lsem) = scratch

    wide = width // PARTS_A
    spread = rows // cols
    blocks_b = blocks * spread
    tables = blocks * link_max
    chips = rows // 2
    reach = chips // 2
    across = chips // 2
    half = blocks // 2
    piece = tables // (2 * PIECES)
    helps = cols >= 4
    early = [k for k, chunk in enumerate(chunks) if chunk[0] < 2]

    r = lax.axis_index("row")
    c = lax.axis_index("col")
    core = lax.rem(r, 2)
    chip = r // 2
    other = r + 1 - 2 * core
    place = jnp.where(chip < across, chip, chips - 1 - (chip - across))

    def chip_at(position):
        position = lax.rem(position + 2 * chips, chips)
        return jnp.where(position < across, position, across + (chips - 1 - position))

    def row_at(position, k):
        return 2 * chip_at(position) + k

    right = (row_at(place + 1, core), c)
    left = (row_at(place - 1, core), c)
    partner = (other, c)
    up = (r, jnp.minimum(c + 1, cols - 1))
    down = (r, jnp.maximum(c - 1, 0))
    has_up = c < cols - 1
    has_down = c > 0
    at_end = (c == 0) | (c == cols - 1)
    inner = jnp.logical_not(at_end)
    helper = (c == 1) | (c == cols - 2)
    aided = jnp.where(c == 1, 0, cols - 1)
    inward = (r, jnp.where(c == 0, 1, cols - 2))

    numbers = ({}, {})

    def number(side, key):
        return numbers[side].setdefault(key, len(numbers[side]))

    plan = []

    def at(time, action, rank=0, length=0.0):
        plan.append((time, rank, length, action))

    def describe(src, dst, group, key, device):
        return pltpu.make_async_remote_copy(
            src_ref=src, dst_ref=dst, send_sem=ssem.at[number(0, group)], recv_sem=rsem.at[number(1, key)],
            device_id=device, device_id_type=MESH)

    def when(cond, action):
        if cond is None:
            action()
        else:
            pl.when(cond)(action)

    def send(src, dst, group, key, device, cond=None):
        when(cond, describe(src, dst, group, key, device).start)

    def arrive(ref, key, cond=None):
        when(cond, pltpu.make_async_copy(ref, ref, rsem.at[number(1, key)]).wait)

    def drain(time, ref, group, cond=None):
        def action():
            wait = pltpu.make_async_copy(ref, ref, ssem.at[number(0, group)]).wait
            when(cond() if cond else None, wait)
        at(time, action, 9, 0.02)

    local = []

    def load(src, dst, cond=None):
        copy = pltpu.make_async_copy(src, dst, lsem.at[len(local)])
        local.append(copy)
        when(cond, copy.start)
        return lambda: when(cond, copy.wait)

    barrier = pltpu.get_barrier_semaphore()
    for k in range(1, rows):
        pl.semaphore_signal(barrier, inc=1, device_id=(lax.rem(r + k, rows), c), device_id_type=MESH)

    @pl.when(has_up)
    def _():
        pl.semaphore_signal(barrier, inc=1, device_id=up, device_id_type=MESH)

    @pl.when(has_down)
    def _():
        pl.semaphore_signal(barrier, inc=1, device_id=down, device_id_type=MESH)

    wait_small = [load(pairs, pairs_v.at[r]), load(links_in, links), load(counts_in, counts),
                  load(integrals_in, integrals)]

    def load_rows(group):
        sem = lsem.at[len(local)]
        for i in group:
            first = firsts[i]
            for k in range(blocks_b):
                pltpu.make_async_copy(
                    v.at[first // size, pl.ds(first % size, parts[i][0]), pl.ds(k * size, size)],
                    rowbuf[i].at[c * blocks_b + k], sem).start()
        ref = out.at[pl.ds(0, sum(parts[i][0] for i in group))]
        local.append(pltpu.make_async_copy(ref, ref, sem))
        return local[-1].wait

    wait_rows = {group[0]: load_rows(group) for group in ([0], [1], range(2, len(parts)))}
    wait_tab = load(tab, own_tab)
    for j in range(PARTS_A):
        pltpu.make_async_copy(v.at[:, :, pl.ds(j * wide, wide)], colbuf[j].at[pl.ds(r * blocks, blocks)],
                              lsem.at[len(local)]).start()
    local.append(pltpu.make_async_copy(out, out, lsem.at[len(local)]))
    wait_cols = local[-1].wait

    pl.semaphore_wait(barrier, rows - 1 + has_up.astype(jnp.int32) + has_down.astype(jnp.int32))

    for k in range(1, rows):
        send(pairs, pairs_v.at[r], ("pairs", k), ("pairs", k), (lax.rem(r + k, rows), c))
        drain(15.0, pairs_v.at[r], ("pairs", k))

    reach_up = {1: up, -1: down}

    def ends(k):
        return TILE * (chunks[k][3] + chunks[k][2]) / high

    def arrival(t, k, late):
        far = max(cols - 3, 1)
        tiles = max(1, min(t, far)) if late else min(t, far)
        length = TILE * chunks[k][2] / high
        return ends(k) + TILE * tiles + HOP + (length + HOP) * (t if late else max(t - far, 0))

    def line_key(k, way, t):
        return "line", k, way * (1 + t) % cols

    def row_chunk(k, tile):
        part, offset, count, _, _ = chunks[k]
        return rowbuf[part].at[pl.ds(tile * blocks_b, blocks_b), pl.ds(offset, count), :]

    def line_own(k, way, cond):
        helped = chunks[k][4]
        position = c if way == 1 else cols - 1 - c
        limit = cols - 2 if helped else cols - 1
        ref = row_chunk(k, c)
        send(ref, ref, ("line", way, 0, helped), line_key(k, way, 0), reach_up[way], cond & (position < limit))

    def line_arrive(k, way, t, edge, forward):
        helped = chunks[k][4]
        last = cols - 2 if helped else cols - 1
        onward = t + 2 <= last if edge else t + 3 <= last
        if onward != forward or (t + 1 > last if edge else t + 2 > last):
            return
        position = c if way == 1 else cols - 1 - c
        cond = position == t + 1 if edge else (position > t + 1) & (position <= last)
        ref = row_chunk(k, jnp.clip(c - way * (1 + t), 0, cols - 1))
        arrive(ref, line_key(k, way, t), cond)
        if onward:
            send(ref, ref, ("line", way, t + 1, helped), line_key(k, way, t + 1), reach_up[way],
                 cond if edge else cond & (position < last))

    def line_finish(i):
        for k, chunk in enumerate(chunks):
            if chunk[0] == i:
                for way in (1, -1):
                    for t in range(cols - 1):
                        for edge in (False, True):
                            line_arrive(k, way, t, edge, False)

    def table_places(s):
        source = c * spread + s
        source_chip = source // 2
        source_place = jnp.where(
            source_chip < across, source_chip, chips - 1 - (source_chip - across))
        distance = lax.rem(place - source_place + chips, chips)
        return lax.rem(source, 2), (distance, lax.rem(chips - distance, chips))

    ring = (right, left)

    def table_part(h, q):
        return pl.ds((h * PIECES + q) * piece, piece)

    def table_stage(s, h, q, d):
        source_core, hops = table_places(s)
        here = (core == source_core) & (hops[h] == d)
        part = table_part(h, q)
        ref = beta_tab.at[s, part]
        src = ref if d else own_tab.at[part]
        if d:
            arrive(ref, ("table", s // 2, h, q), here)
        if d + 1 < chips:
            send(src, ref, ("table", s, h), ("table", s // 2, h, q), ring[h], here)
        send(src, ref, ("tableP", s), ("tableP", s), partner, here)
        if helps:
            send(src, help_tab.at[s, part], ("help", s), ("help", s // 2, h, q), inward, here & at_end)

    def table_finish():
        for s in range(spread):
            source_core, _ = table_places(s)
            arrive(beta_tab.at[s], ("tableP", s), core != source_core)
            table_loads[s]()

    def help_arrive(s, h, q):
        source_core = table_places(s)[0]
        aided_core = lax.rem(aided * spread + s, 2)
        ref = help_tab.at[s, table_part(h, q)]
        arrive(ref, ("help", s // 2, h, q), helper & (core == aided_core))
        send(ref, ref, ("helpP", s), ("helpP", s), partner, helper & (core == aided_core))

    def help_finish():
        for s in range(spread):
            aided_core = lax.rem(aided * spread + s, 2)
            arrive(help_tab.at[s], ("helpP", s), helper & (core != aided_core))

    def narrow(value):
        return value.astype(jnp.float32).astype(jnp.bfloat16)

    def widen(source, base, target):
        @pl.loop(0, tables)
        def _(index):
            values = narrow(source[index])
            target[base + index] = jnp.concatenate([values, values], axis=1)

    def couple(source, base, target):
        @pl.loop(0, tables // 2)
        def _(index):
            target[base + index] = jnp.concatenate(
                [narrow(source[2 * index]), narrow(source[2 * index + 1])], axis=1)

    def couple_all(source, target):
        for s in range(spread):
            couple(source.at[s], s * (tables // 2), target)

    def tile_half(j, hb, position, k):
        return colbuf[j].at[pl.ds(row_at(position, k) * blocks + hb * half, half)]

    def ring_own(j, hb, way, cond):
        ref = colbuf[j].at[pl.ds(r * blocks + hb * half, half)]
        send(ref, ref, ("ring", way, 0), ("ring", way, j, hb, 0), ring[way], cond)

    def carried(way, hb, t):
        return t < reach - 1 or hb == way

    def ring_arrive(j, hb, way, t):
        ref = tile_half(j, hb, place - 1 - t if way == 0 else place + 1 + t, core)
        arrive(ref, ("ring", way, j, hb, t))
        if t + 1 < reach and carried(way, hb, t + 1):
            send(ref, ref, ("ring", way, t + 1), ("ring", way, j, hb, t + 1), ring[way])
        send(ref, ref, ("ringP", way, t), ("tiles", j), partner)

    def ring_finish(j):
        arrive(colbuf[j].at[pl.ds(0, chips * blocks)], ("tiles", j))

    def coefficients(target, first, count):
        @pl.loop(0, count)
        def _(b):
            block = first + b
            for l in range(link_max):
                pair = pairs_s[lax.div(block, blocks), lax.rem(block, blocks), l]
                norb = integrals.shape[0]
                value = integrals[lax.div(pair, norb), lax.rem(pair, norb)]
                target[b, l] = value * jnp.clip(counts[block] - l, 0, 1).astype(jnp.float32)

    def gather_pairs():
        for wait in wait_small:
            wait()
        for k in range(1, rows):
            arrive(pairs_v.at[lax.rem(r - k + rows, rows)], ("pairs", k))
        copy = pltpu.make_async_copy(pairs_v, pairs_s, lsem.at[0])
        copy.start()
        copy.wait()
        coefficients(alpha_coef, r * blocks, blocks)
        coefficients(beta_coef, c * blocks_b, blocks_b)
        if helps:
            coefficients(help_coef, aided * blocks_b, blocks_b)

    def trips(first, last, body):
        together = max(u for u in (4, 2, 1) if (last - first) % u == 0)

        @pl.loop(0, (last - first) // together)
        def _(trip):
            for turn in range(together):
                body(first + trip * together + turn)

    def alpha_compute(j):
        def body(block):
            total = None
            for l in range(link_max):
                source = links[l, r * blocks + block]
                up_part, low_part = split(colbuf[j][source] * alpha_coef[block, l])
                term = jnp.dot(
                    alpha_signs[block * link_max + l], jnp.concatenate([up_part, low_part], axis=0),
                    preferred_element_type=jnp.float32)
                total = term if total is None else total + term
            where = (pl.ds(pl.multiple_of(block * size, size), size), pl.ds(j * wide, wide))
            out[where] = out[where] + total

        trips(0, blocks, body)

    def beta_compute(group, owner, coef, signs, target, start, add, span=None):
        count = sum(parts[i][0] for i in group)

        def body(block):
            total = None
            for l in range(0, link_max, 2):
                highs, lows = [], []
                for m in (l, l + 1):
                    source = links[m, owner * blocks_b + block]
                    value = jnp.concatenate([rowbuf[i][source] for i in group], axis=0)
                    up_part, low_part = split(value * coef[block, m])
                    highs.append(up_part)
                    lows.append(low_part)
                value = jnp.concatenate(
                    [jnp.concatenate(highs, axis=1), jnp.concatenate(lows, axis=1)], axis=0)
                term = lax.dot_general(
                    value, signs[block * (link_max // 2) + l // 2],
                    (((1,), (1,)), ((), ())), preferred_element_type=jnp.float32)
                total = term if total is None else total + term
            total = total[:count] + total[count:]
            where = (pl.ds(start, count), pl.ds(pl.multiple_of(block * size, size), size))
            if add:
                total = target[where] + total
            target[where] = total

        trips(*(span or (0, blocks_b)), body)

    shared_first = sum(height for height, helped in parts if not helped)

    def own_beta(group, cond, span):
        def action():
            beta_compute(group, c, beta_coef, beta_signs, out, firsts[group[0]], True, span)
        when(cond, action)

    def sums_key(i):
        return line_key(next(k for k, chunk in enumerate(chunks) if chunk[0] == i), 1, 0)

    def help_beta(i):
        @pl.when(helper)
        def _():
            beta_compute([i], aided, help_coef, help_signs, shared, firsts[i] - shared_first, False)

        ref = shared.at[pl.ds(firsts[i] - shared_first, parts[i][0])]
        send(ref, ref, ("sums",), sums_key(i), (r, aided), helper)

    def take_sums(i):
        ref = shared.at[pl.ds(firsts[i] - shared_first, parts[i][0])]
        arrive(ref, sums_key(i), at_end)

        @pl.when(at_end)
        def _():
            where = pl.ds(firsts[i], parts[i][0])
            out[where, :] = out[where, :] + ref[...]

        flush(firsts[i], parts[i][0], at_end)

    held, alphas = [], []

    def flush(first, count, cond):
        if len(alphas) < PARTS_A:
            held.append((first, count, cond))
            return
        where = pl.ds(first, count)
        when(cond, pltpu.make_async_copy(out.at[where], result.at[where], lsem.at[lsem.shape[0] - 1]).start)

    table_loads = []

    def begin():
        always = jnp.bool_(True)
        for k in range(len(chunks)):
            if chunks[k][1] == 0 and chunks[k][0] in wait_rows:
                wait_rows[chunks[k][0]]()
            first = k in early or not helps
            line_own(k, 1, always if first else has_down)
            line_own(k, -1, always if first else has_up)
        wait_tab()

    def begin_tables():
        for s in range(spread):
            source_core, hops = table_places(s)
            table_loads.append(load(tab, beta_tab.at[s], (core == source_core) & (hops[0] == 0)))

    def begin_tiles():
        wait_cols()

    at(-4.0, begin)
    at(-2.0, begin_tables)
    at(-1.5, begin_tiles)

    def rest():
        for k in range(len(early), len(chunks)):
            line_own(k, 1, c == 0)
            line_own(k, -1, c == cols - 1)

    stage_last = START + PIECE * (PIECES - 1 + chips - 1) + HOP * (chips - 1)
    if helps:
        at(stage_last + 0.1, rest)

    for k in range(len(chunks)):
        helped = chunks[k][4]
        late_k = helps and k not in early
        for way in (1, -1):
            for t in range(cols - 1):
                for edge in (False, True):
                    late = edge and late_k
                    at(START - LEAD + arrival(t, k, late) + (1.5 if t else 0.0),
                       functools.partial(line_arrive, k, way, t, edge, True))

    for helped in (False, True) if helps else (False,):
        count = sum(height for height, aided_part in parts if aided_part == helped)
        last_k = max(k for k, chunk in enumerate(chunks) if chunk[4] == helped)
        last = cols - 2 if helped else cols - 1
        for way in (1, -1):
            for t in range(last):
                def cond(t=t, way=way, last=last):
                    position = c if way == 1 else cols - 1 - c
                    return (position >= t) & (position < last)

                sent = START + arrival(t, last_k, helps and last_k not in early) + (TILE if t == 0 else 0.0)
                drain(sent + 6.0, out.at[pl.ds(0, count)], ("line", way, t, helped), cond)

    for q in range(PIECES):
        for h in range(2):
            for s in range(spread):
                for d in range(chips):
                    time = -1.0 if d == 0 else START + PIECE * (q + d) + HOP * d
                    at(time, functools.partial(table_stage, s, h, q, d))
    for s in range(spread):
        def mine(s=s):
            return core == table_places(s)[0]

        for h in range(2):
            drain(stage_last + 12.0, beta_tab.at[s, pl.ds(0, tables // 2)], ("table", s, h),
                  lambda s=s, h=h: mine(s) & (table_places(s)[1][h] < chips - 1))
        drain(stage_last + 12.0, beta_tab.at[s], ("tableP", s), mine)
        if helps:
            drain(START + 1.8 * TILE, beta_tab.at[s], ("help", s), lambda s=s: mine(s) & at_end)
            drain(START + 1.8 * TILE, beta_tab.at[s], ("helpP", s),
                  lambda s=s: helper & (core == lax.rem(aided * spread + s, 2)))
    at(stage_last + 4.0, table_finish, 1, 0.1)
    at(stage_last + 4.1, lambda: couple_all(beta_tab, beta_signs), 2, 1.0)

    help_ready = 0.0
    if helps:
        for q in range(PIECES):
            for h in range(2):
                time = START + max(
                    ends(len(early) - 1) + PIECE * (q + PIECES + 1) + HOP, PIECE * (q + chips) + HOP * (chips + 1))
                help_ready = max(help_ready, time + 1.5)
                for s in range(spread):
                    at(time + 0.5, functools.partial(help_arrive, s, h, q))
        at(help_ready, help_finish, 1, 0.1)
        at(help_ready + 0.1, lambda: pl.when(helper)(lambda: couple_all(help_tab, help_signs)), 1, 1.0)
        help_ready += 0.2

    order = [(j, second) for second in range(2) for j in range(PARTS_A)]
    step = TILE / (2 * PARTS_A)

    classes = []
    for h in range(2):
        kind = jnp.int32(chips - 1)
        for s in range(spread):
            source_core, hops = table_places(s)
            kind = jnp.where(core == source_core, hops[h], kind)
        classes.append(kind)

    held_back = PARTS_A + 1

    def ring_time(a, t):
        if t == 0 and a < PARTS_A:
            wait = PIECE * (PIECES + max(chips - 2, 0)) + HOP * (chips - 1) + step * (a - 1) + HOP
            return max(stage_last - PIECE - HOP + 0.2, START + (wait if a else 0.0))
        j = a % PARTS_A
        place = PARTS_A + 1 + 2 * j + (1 if t else 0)
        return START + PIECE * PIECES + step * place + 3.0 * HOP + 30.0 * max(t - 1, 0)

    for a, (j, second) in enumerate(order):
        for way in range(2):
            hb = (1 - way) if second else way
            for d in range(chips):
                time = 0.0
                if d < chips - 1 and a >= d:
                    time = START + PIECE * (PIECES - 1 + d) + HOP * d + 0.05 if d else 0.0
                if a >= held_back:
                    time = ring_time(a - held_back, 0) + 0.1
                at(time, functools.partial(ring_own, j, hb, way, classes[way] == d))
            for t in range(reach):
                if carried(way, hb, t):
                    forwards = t + 1 < reach and carried(way, hb, t + 1)
                    at(ring_time(a, t) + (0.0 if forwards else 1.0),
                       functools.partial(ring_arrive, j, hb, way, t), 0 if forwards else 1, 0.03)
    for t in range(reach):
        count = high if t < reach - 1 else high // 2
        for way in range(2):
            drain(ring_time(2 * PARTS_A - 1, t) + 4.0, out.at[pl.ds(0, count)], ("ring", way, t))
            drain(ring_time(2 * PARTS_A - 1, t) + 8.0, out.at[pl.ds(0, count)], ("ringP", way, t))

    def own_pass(j):
        ref = colbuf[j].at[pl.ds(r * blocks, blocks)]
        send(ref, ref, ("own",), ("tiles", j), partner)

    def alpha_step(j):
        ring_finish(j)
        alpha_compute(j)
        alphas.append(j)
        if len(alphas) == PARTS_A:
            for entry in held:
                flush(*entry)

    for j in range(PARTS_A):
        at(0.5, functools.partial(own_pass, j))
        done = max(ring_time(j, reach - 1), ring_time(PARTS_A + j, max(reach - 2, 0))) + 4.5
        at(done, functools.partial(alpha_step, j), 4, 0.9)

    drain(25.0, out, ("own",))

    def prepare():
        out[...] = jnp.zeros_like(out)
        gather_pairs()
        widen(own_tab, 0, alpha_signs)

    at(0.6, prepare, 0, 4.0)

    groups = [[0], [1], list(range(2, 10)), list(range(10, 18))]

    def finish_time(i, t):
        k = max(k for k, chunk in enumerate(chunks) if chunk[0] == i)
        return START - LEAD + 1.0 + arrival(t, k, helps and k not in early)

    def help_step(i):
        line_finish(i)
        help_beta(i)

    def own_step(group, finish, cond, turn=0, turns=1):
        if finish and not turn:
            for i in group:
                line_finish(i)
        span = (blocks_b * turn // turns, blocks_b * (turn + 1) // turns)
        own_beta(group, cond, span)
        if turn == turns - 1:
            flush(firsts[group[0]], sum(parts[i][0] for i in group), cond)

    for i, (height, helped) in enumerate(parts):
        if helped:
            ready = max(finish_time(i, max(cols - 3, 0)), help_ready)
            at(ready + 1.5, functools.partial(help_step, i), 2, 0.85)
            at(ready + 11.0, functools.partial(take_sums, i), 5, 0.0)
    if helps:
        drain(help_ready + TILE, shared, ("sums",), lambda: helper)
    for group in groups:
        inside, outside = finish_time(group[-1], max(cols - 3, 0)), finish_time(group[-1], cols - 2)
        if not helps:
            at(outside + 0.1, functools.partial(own_step, group, True, None), 6, 2.6)
            continue
        for turn in range(2):
            at((max(inside, help_ready) + 1.6 if parts[group[0]][1] else inside + 0.1) + 0.01 * turn,
               functools.partial(own_step, group, False, inner, turn, 2), 6, 0.8)
        if not parts[group[0]][1]:
            at(outside + 0.1, functools.partial(own_step, group, True, at_end), 6, 0.0)

    for action in in_order(plan):
        action()
    pltpu.make_async_copy(out, result, lsem.at[lsem.shape[0] - 1]).wait()
    assert len(numbers[0]) == ssem.shape[0] and len(numbers[1]) == rsem.shape[0]
    assert len(local) == lsem.shape[0] - 1


def local(vector, one_electron, links, counts, pairs, signs, rows, cols):
    blocks, link_max = pairs.shape
    size = signs.shape[2]
    high, width = vector.shape
    spread = rows // cols
    tables = blocks * link_max
    parts = row_parts(high, cols)
    helped = sum(height for height, aided in parts if aided)
    reach = rows // 4
    sends = rows - 1 + 2 * (cols - 1) + 4 * reach + 2 + spread * 3
    pieces = 2 * PIECES * ((spread + 1) // 2) + spread
    arrivals = rows - 1 + PARTS_A * (4 * reach - 1) + pieces + len(row_chunks(high, cols)) * (cols - 1)
    if cols >= 4:
        sends += 2 * (cols - 2) + spread * 2
        arrivals += pieces
    scratch = [pltpu.VMEM((rows * blocks, size, width // PARTS_A), jnp.float32)] * PARTS_A
    scratch += [pltpu.VMEM((cols * blocks * spread, height, size), jnp.float32) for height, _ in parts]
    scratch += [
        pltpu.VMEM((tables, size, size), jnp.int32),
        pltpu.VMEM((spread, tables, size, size), jnp.int32),
        pltpu.VMEM((spread, tables, size, size), jnp.int32),
        pltpu.VMEM((tables, size, 2 * size), jnp.bfloat16),
        pltpu.VMEM((spread * tables // 2, size, 2 * size), jnp.bfloat16),
        pltpu.VMEM((spread * tables // 2, size, 2 * size), jnp.bfloat16),
        pltpu.VMEM((max(helped, 8), width), jnp.float32),
        pltpu.VMEM((high, width), jnp.float32),
        pltpu.VMEM((rows, blocks, link_max), jnp.int32),
        pltpu.SMEM((rows, blocks, link_max), jnp.int32),
        pltpu.SMEM((link_max, links.shape[0]), jnp.int32),
        pltpu.SMEM(counts.shape, jnp.int32),
        pltpu.SMEM(one_electron.shape, jnp.float32),
        pltpu.SMEM((blocks, link_max), jnp.float32),
        pltpu.SMEM((blocks * spread, link_max), jnp.float32),
        pltpu.SMEM((blocks * spread, link_max), jnp.float32),
        pltpu.SemaphoreType.DMA((sends,)),
        pltpu.SemaphoreType.DMA((arrivals,)),
        pltpu.SemaphoreType.DMA((10 + spread,)),
    ]
    far = pl.BlockSpec(memory_space=pltpu.HBM)
    operands = (links.T, counts, one_electron, pairs, vector.reshape(blocks, size, width),
                signs.reshape(tables, size, size))
    return pl.pallas_call(
        functools.partial(kernel, rows, cols, blocks, link_max),
        out_shape=jax.ShapeDtypeStruct(vector.shape, jnp.float32),
        in_specs=[far] * 6,
        out_specs=pl.BlockSpec(memory_space=pl.ANY),
        scratch_shapes=scratch,
        compiler_params=pltpu.CompilerParams(
            collective_id=0, has_side_effects=True, vmem_limit_bytes=48 << 20),
    )(*[pltpu.with_memory_space_constraint(value, pltpu.HBM) for value in operands])


def solution(mesh):
    in_specs = (P("row", "col"), P(), P(), P(), P("row", None), P("row", None, None, None))
    out_specs = P("row", "col")
    body = functools.partial(local, rows=mesh.shape["row"], cols=mesh.shape["col"])
    return jax.shard_map(body, mesh=mesh, in_specs=in_specs, out_specs=out_specs, check_vma=False)
```

```python
import functools

import jax
import jax.numpy as jnp
from jax import lax
from jax.experimental import pallas as pl
from jax.experimental.pallas import tpu as pltpu
from jax.sharding import PartitionSpec as P

MESH = pl.DeviceIdType.MESH
PARTS_A = 4
PIECES = 4
START = 4.5
LEAD = 2.5
SLACK = 0.1
TILE = 45.0
HOP = 1.5
PIECE = 5.6


def split(value):
    high = value.astype(jnp.bfloat16)
    low = (value - high.astype(jnp.float32)).astype(jnp.bfloat16)
    return high, low


def row_parts(high, cols):
    helps = cols >= 4
    return [(high // 4, False)] * 2 + [(high // 16, False)] + [(high // 32, helps)] * 14


def row_chunks(high, cols):
    chunks, first = [], 0
    for part, (height, helped) in enumerate(row_parts(high, cols)):
        piece = min(height, high // 16 if part else high // 8)
        for offset in range(0, height, piece):
            chunks.append((part, offset, piece, first + offset, helped))
        first += height
    return chunks


def in_order(plan):
    left = sorted(enumerate(plan), key=lambda entry: (entry[1][0], entry[0]))
    urgent = [entry for entry in left if entry[1][1] <= 2]
    now, result = 0.0, []
    while left:
        ready = [entry for entry in left if entry[1][0] <= now]
        soon = [entry for entry in urgent if entry[1][0] > now][:1]
        if soon:
            room = soon[0][1][0] - now + SLACK
            ready = [entry for entry in ready if entry[1][1] <= 2 or entry[1][2] <= room]
        if not ready:
            now = min(entry[1][0] for entry in (soon or left))
            ready = [entry for entry in left if entry[1][0] <= now and entry[1][1] <= 2] or left[:1]
        chosen = min(ready, key=lambda entry: (entry[1][1], entry[1][0], entry[0]))
        left.remove(chosen)
        if chosen[1][1] <= 2:
            urgent.remove(chosen)
        start, _, length, action = chosen[1]
        now = max(now, start) + length
        result.append(action)
    return result


def kernel(rows, cols, blocks, link_max, links_in, counts_in, integrals_in, pairs, v, tab, result, *scratch):
    size = tab.shape[1]
    high, width = result.shape
    parts = row_parts(high, cols)
    chunks = row_chunks(high, cols)
    firsts = [sum(p[0] for p in parts[:i]) for i in range(len(parts))]
    scratch = list(scratch)
    colbuf = [scratch.pop(0) for _ in range(PARTS_A)]
    rowbuf = [scratch.pop(0) for _ in parts]
    (own_tab, beta_tab, help_tab, alpha_signs, beta_signs, help_signs, shared,
     out, pairs_v, pairs_s, links, counts, integrals, alpha_coef, beta_coef, help_coef,
     ssem, rsem, lsem) = scratch

    wide = width // PARTS_A
    spread = rows // cols
    blocks_b = blocks * spread
    tables = blocks * link_max
    chips = rows // 2
    reach = chips // 2
    across = chips // 2
    half = blocks // 2
    piece = tables // (2 * PIECES)
    helps = cols >= 4
    early = [k for k, chunk in enumerate(chunks) if chunk[0] < 3]

    r = lax.axis_index("row")
    c = lax.axis_index("col")
    core = lax.rem(r, 2)
    chip = r // 2
    other = r + 1 - 2 * core
    place = jnp.where(chip < across, chip, chips - 1 - (chip - across))

    def chip_at(position):
        position = lax.rem(position + 2 * chips, chips)
        return jnp.where(position < across, position, across + (chips - 1 - position))

    def row_at(position, k):
        return 2 * chip_at(position) + k

    right = (row_at(place + 1, core), c)
    left = (row_at(place - 1, core), c)
    partner = (other, c)
    up = (r, jnp.minimum(c + 1, cols - 1))
    down = (r, jnp.maximum(c - 1, 0))
    has_up = c < cols - 1
    has_down = c > 0
    at_end = (c == 0) | (c == cols - 1)
    inner = jnp.logical_not(at_end)
    helper = (c == 1) | (c == cols - 2)
    aided = jnp.where(c == 1, 0, cols - 1)
    inward = (r, jnp.where(c == 0, 1, cols - 2))

    numbers = ({}, {})

    def number(side, key):
        return numbers[side].setdefault(key, len(numbers[side]))

    plan = []

    def at(time, action, rank=0, length=0.0):
        plan.append((time, rank, length, action))

    def describe(src, dst, group, key, device):
        return pltpu.make_async_remote_copy(
            src_ref=src, dst_ref=dst, send_sem=ssem.at[number(0, group)], recv_sem=rsem.at[number(1, key)],
            device_id=device, device_id_type=MESH)

    def when(cond, action):
        if cond is None:
            action()
        else:
            pl.when(cond)(action)

    def send(src, dst, group, key, device, cond=None):
        when(cond, describe(src, dst, group, key, device).start)

    def arrive(ref, key, cond=None):
        when(cond, pltpu.make_async_copy(ref, ref, rsem.at[number(1, key)]).wait)

    def drain(time, ref, group, cond=None):
        def action():
            wait = pltpu.make_async_copy(ref, ref, ssem.at[number(0, group)]).wait
            when(cond() if cond else None, wait)
        at(time, action, 9, 0.02)

    local = []

    def load(src, dst, cond=None):
        copy = pltpu.make_async_copy(src, dst, lsem.at[len(local)])
        local.append(copy)
        when(cond, copy.start)
        return lambda: when(cond, copy.wait)

    barrier = pltpu.get_barrier_semaphore()
    for k in range(1, rows):
        pl.semaphore_signal(barrier, inc=1, device_id=(lax.rem(r + k, rows), c), device_id_type=MESH)

    @pl.when(has_up)
    def _():
        pl.semaphore_signal(barrier, inc=1, device_id=up, device_id_type=MESH)

    @pl.when(has_down)
    def _():
        pl.semaphore_signal(barrier, inc=1, device_id=down, device_id_type=MESH)

    wait_small = [load(pairs, pairs_v.at[r]), load(links_in, links), load(counts_in, counts),
                  load(integrals_in, integrals)]

    def load_rows(group):
        sem = lsem.at[len(local)]
        for i in group:
            first = firsts[i]
            for k in range(blocks_b):
                pltpu.make_async_copy(
                    v.at[first // size, pl.ds(first % size, parts[i][0]), pl.ds(k * size, size)],
                    rowbuf[i].at[c * blocks_b + k], sem).start()
        ref = out.at[pl.ds(0, sum(parts[i][0] for i in group))]
        local.append(pltpu.make_async_copy(ref, ref, sem))
        return local[-1].wait

    wait_rows = {group[0]: load_rows(group) for group in ([0], [1], range(2, len(parts)))}
    wait_tab = load(tab, own_tab)
    for j in range(PARTS_A):
        pltpu.make_async_copy(v.at[:, :, pl.ds(j * wide, wide)], colbuf[j].at[pl.ds(r * blocks, blocks)],
                              lsem.at[len(local)]).start()
    local.append(pltpu.make_async_copy(out, out, lsem.at[len(local)]))
    wait_cols = local[-1].wait

    pl.semaphore_wait(barrier, rows - 1 + has_up.astype(jnp.int32) + has_down.astype(jnp.int32))

    for k in range(1, rows):
        send(pairs, pairs_v.at[r], ("pairs", k), ("pairs", k), (lax.rem(r + k, rows), c))
        drain(15.0, pairs_v.at[r], ("pairs", k))

    reach_up = {1: up, -1: down}

    def ends(k):
        return TILE * (chunks[k][3] + chunks[k][2]) / high

    def arrival(t, k, late):
        far = max(cols - 3, 1)
        tiles = max(1, min(t, far)) if late else min(t, far)
        length = TILE * chunks[k][2] / high
        return ends(k) + TILE * tiles + HOP + (length + HOP) * (t if late else max(t - far, 0))

    def line_key(k, way, t):
        return "line", k, way * (1 + t) % cols

    def row_chunk(k, tile):
        part, offset, count, _, _ = chunks[k]
        return rowbuf[part].at[pl.ds(tile * blocks_b, blocks_b), pl.ds(offset, count), :]

    def line_own(k, way, cond):
        helped = chunks[k][4]
        position = c if way == 1 else cols - 1 - c
        limit = cols - 2 if helped else cols - 1
        ref = row_chunk(k, c)
        send(ref, ref, ("line", way, 0, helped), line_key(k, way, 0), reach_up[way], cond & (position < limit))

    def line_arrive(k, way, t, edge, forward):
        helped = chunks[k][4]
        last = cols - 2 if helped else cols - 1
        onward = t + 2 <= last if edge else t + 3 <= last
        if onward != forward or (t + 1 > last if edge else t + 2 > last):
            return
        position = c if way == 1 else cols - 1 - c
        cond = position == t + 1 if edge else (position > t + 1) & (position <= last)
        ref = row_chunk(k, jnp.clip(c - way * (1 + t), 0, cols - 1))
        arrive(ref, line_key(k, way, t), cond)
        if onward:
            send(ref, ref, ("line", way, t + 1, helped), line_key(k, way, t + 1), reach_up[way],
                 cond if edge else cond & (position < last))

    def line_finish(i):
        for k, chunk in enumerate(chunks):
            if chunk[0] == i:
                for way in (1, -1):
                    for t in range(cols - 1):
                        for edge in (False, True):
                            line_arrive(k, way, t, edge, False)

    def table_places(s):
        source = c * spread + s
        source_chip = source // 2
        source_place = jnp.where(
            source_chip < across, source_chip, chips - 1 - (source_chip - across))
        distance = lax.rem(place - source_place + chips, chips)
        return lax.rem(source, 2), (distance, lax.rem(chips - distance, chips))

    ring = (right, left)

    def table_part(h, q):
        return pl.ds((h * PIECES + q) * piece, piece)

    def table_stage(s, h, q, d):
        source_core, hops = table_places(s)
        here = (core == source_core) & (hops[h] == d)
        part = table_part(h, q)
        ref = beta_tab.at[s, part]
        src = ref if d else own_tab.at[part]
        if d:
            arrive(ref, ("table", s // 2, h, q), here)
        if d + 1 < chips:
            send(src, ref, ("table", s, h), ("table", s // 2, h, q), ring[h], here)
        send(src, ref, ("tableP", s), ("tableP", s), partner, here)
        if helps:
            send(src, help_tab.at[s, part], ("help", s), ("help", s // 2, h, q), inward, here & at_end)

    def table_finish():
        for s in range(spread):
            source_core, _ = table_places(s)
            arrive(beta_tab.at[s], ("tableP", s), core != source_core)
            table_loads[s]()

    def help_arrive(s, h, q):
        source_core = table_places(s)[0]
        aided_core = lax.rem(aided * spread + s, 2)
        ref = help_tab.at[s, table_part(h, q)]
        arrive(ref, ("help", s // 2, h, q), helper & (core == aided_core))
        send(ref, ref, ("helpP", s), ("helpP", s), partner, helper & (core == aided_core))

    def help_finish():
        for s in range(spread):
            aided_core = lax.rem(aided * spread + s, 2)
            arrive(help_tab.at[s], ("helpP", s), helper & (core != aided_core))

    def narrow(value):
        return value.astype(jnp.float32).astype(jnp.bfloat16)

    def widen(source, base, target):
        @pl.loop(0, tables)
        def _(index):
            values = narrow(source[index])
            target[base + index] = jnp.concatenate([values, values], axis=1)

    def couple(source, base, target):
        @pl.loop(0, tables // 2)
        def _(index):
            target[base + index] = jnp.concatenate(
                [narrow(source[2 * index]), narrow(source[2 * index + 1])], axis=1)

    def couple_all(source, target):
        for s in range(spread):
            couple(source.at[s], s * (tables // 2), target)

    def tile_half(j, hb, position, k):
        return colbuf[j].at[pl.ds(row_at(position, k) * blocks + hb * half, half)]

    def ring_own(j, hb, way, cond):
        ref = colbuf[j].at[pl.ds(r * blocks + hb * half, half)]
        send(ref, ref, ("ring", way, 0), ("ring", way, j, hb, 0), ring[way], cond)

    def carried(way, hb, t):
        return t < reach - 1 or hb == way

    def ring_arrive(j, hb, way, t):
        ref = tile_half(j, hb, place - 1 - t if way == 0 else place + 1 + t, core)
        arrive(ref, ("ring", way, j, hb, t))
        if t + 1 < reach and carried(way, hb, t + 1):
            send(ref, ref, ("ring", way, t + 1), ("ring", way, j, hb, t + 1), ring[way])
        send(ref, ref, ("ringP", way, t), ("tiles", j), partner)

    def ring_finish(j):
        arrive(colbuf[j].at[pl.ds(0, chips * blocks)], ("tiles", j))

    def coefficients(target, first, count):
        @pl.loop(0, count)
        def _(b):
            block = first + b
            for l in range(link_max):
                pair = pairs_s[lax.div(block, blocks), lax.rem(block, blocks), l]
                norb = integrals.shape[0]
                value = integrals[lax.div(pair, norb), lax.rem(pair, norb)]
                target[b, l] = value * jnp.clip(counts[block] - l, 0, 1).astype(jnp.float32)

    def gather_pairs():
        for wait in wait_small:
            wait()
        for k in range(1, rows):
            arrive(pairs_v.at[lax.rem(r - k + rows, rows)], ("pairs", k))
        copy = pltpu.make_async_copy(pairs_v, pairs_s, lsem.at[0])
        copy.start()
        copy.wait()
        coefficients(alpha_coef, r * blocks, blocks)
        coefficients(beta_coef, c * blocks_b, blocks_b)
        if helps:
            coefficients(help_coef, aided * blocks_b, blocks_b)

    def trips(first, last, body):
        together = max(u for u in (4, 2, 1) if (last - first) % u == 0)

        @pl.loop(0, (last - first) // together)
        def _(trip):
            for turn in range(together):
                body(first + trip * together + turn)

    def alpha_compute(j):
        def body(block):
            total = None
            for l in range(link_max):
                source = links[l, r * blocks + block]
                up_part, low_part = split(colbuf[j][source] * alpha_coef[block, l])
                term = jnp.dot(
                    alpha_signs[block * link_max + l], jnp.concatenate([up_part, low_part], axis=0),
                    preferred_element_type=jnp.float32)
                total = term if total is None else total + term
            where = (pl.ds(pl.multiple_of(block * size, size), size), pl.ds(j * wide, wide))
            out[where] = out[where] + total

        trips(0, blocks, body)

    def beta_compute(group, owner, coef, signs, target, start, add, span=None):
        count = sum(parts[i][0] for i in group)

        def body(block):
            total = None
            for l in range(0, link_max, 2):
                highs, lows = [], []
                for m in (l, l + 1):
                    source = links[m, owner * blocks_b + block]
                    value = jnp.concatenate([rowbuf[i][source] for i in group], axis=0)
                    up_part, low_part = split(value * coef[block, m])
                    highs.append(up_part)
                    lows.append(low_part)
                value = jnp.concatenate(
                    [jnp.concatenate(highs, axis=1), jnp.concatenate(lows, axis=1)], axis=0)
                term = lax.dot_general(
                    value, signs[block * (link_max // 2) + l // 2],
                    (((1,), (1,)), ((), ())), preferred_element_type=jnp.float32)
                total = term if total is None else total + term
            total = total[:count] + total[count:]
            where = (pl.ds(start, count), pl.ds(pl.multiple_of(block * size, size), size))
            if add:
                total = target[where] + total
            target[where] = total

        trips(*(span or (0, blocks_b)), body)

    shared_first = sum(height for height, helped in parts if not helped)

    def own_beta(group, cond, span):
        def action():
            beta_compute(group, c, beta_coef, beta_signs, out, firsts[group[0]], True, span)
        when(cond, action)

    def sums_key(i):
        return line_key(next(k for k, chunk in enumerate(chunks) if chunk[0] == i), 1, 0)

    def help_beta(i):
        @pl.when(helper)
        def _():
            beta_compute([i], aided, help_coef, help_signs, shared, firsts[i] - shared_first, False)

        ref = shared.at[pl.ds(firsts[i] - shared_first, parts[i][0])]
        send(ref, ref, ("sums",), sums_key(i), (r, aided), helper)

    def take_sums(i):
        ref = shared.at[pl.ds(firsts[i] - shared_first, parts[i][0])]
        arrive(ref, sums_key(i), at_end)

        @pl.when(at_end)
        def _():
            where = pl.ds(firsts[i], parts[i][0])
            out[where, :] = out[where, :] + ref[...]

        flush(firsts[i], parts[i][0], at_end)

    held, alphas = [], []

    def flush(first, count, cond):
        if len(alphas) < PARTS_A:
            held.append((first, count, cond))
            return
        where = pl.ds(first, count)
        when(cond, pltpu.make_async_copy(out.at[where], result.at[where], lsem.at[lsem.shape[0] - 1]).start)

    table_loads = []

    def begin():
        always = jnp.bool_(True)
        for k in range(len(chunks)):
            if chunks[k][1] == 0 and chunks[k][0] in wait_rows:
                wait_rows[chunks[k][0]]()
            first = k in early or not helps
            line_own(k, 1, always if first else has_down)
            line_own(k, -1, always if first else has_up)
        wait_tab()

    def begin_tables():
        for s in range(spread):
            source_core, hops = table_places(s)
            table_loads.append(load(tab, beta_tab.at[s], (core == source_core) & (hops[0] == 0)))

    def begin_tiles():
        wait_cols()

    at(-4.0, begin)
    at(-2.0, begin_tables)
    at(-1.5, begin_tiles)

    def rest():
        for k in range(len(early), len(chunks)):
            line_own(k, 1, c == 0)
            line_own(k, -1, c == cols - 1)

    stage_last = START + PIECE * (PIECES - 1 + chips - 1) + HOP * (chips - 1) + 3.5
    if helps:
        at(stage_last + 0.1, rest)

    for k in range(len(chunks)):
        helped = chunks[k][4]
        late_k = helps and k not in early
        for way in (1, -1):
            for t in range(cols - 1):
                for edge in (False, True):
                    late = edge and late_k
                    at(START - LEAD + arrival(t, k, late) + (1.5 if t else 0.0),
                       functools.partial(line_arrive, k, way, t, edge, True))

    for helped in (False, True) if helps else (False,):
        count = sum(height for height, aided_part in parts if aided_part == helped)
        last_k = max(k for k, chunk in enumerate(chunks) if chunk[4] == helped)
        last = cols - 2 if helped else cols - 1
        for way in (1, -1):
            for t in range(last):
                def cond(t=t, way=way, last=last):
                    position = c if way == 1 else cols - 1 - c
                    return (position >= t) & (position < last)

                sent = START + arrival(t, last_k, helps and last_k not in early) + (TILE if t == 0 else 0.0)
                drain(sent + 6.0, out.at[pl.ds(0, count)], ("line", way, t, helped), cond)

    for q in range(PIECES):
        for h in range(2):
            for s in range(spread):
                for d in range(chips):
                    time = -1.0 if d == 0 else START + PIECE * (q + d) + HOP * d + (3.5 if d > 1 else 0.0)
                    at(time, functools.partial(table_stage, s, h, q, d))
    for s in range(spread):
        def mine(s=s):
            return core == table_places(s)[0]

        for h in range(2):
            drain(stage_last + 12.0, beta_tab.at[s, pl.ds(0, tables // 2)], ("table", s, h),
                  lambda s=s, h=h: mine(s) & (table_places(s)[1][h] < chips - 1))
        drain(stage_last + 12.0, beta_tab.at[s], ("tableP", s), mine)
        if helps:
            drain(START + 1.8 * TILE, beta_tab.at[s], ("help", s), lambda s=s: mine(s) & at_end)
            drain(START + 1.8 * TILE, beta_tab.at[s], ("helpP", s),
                  lambda s=s: helper & (core == lax.rem(aided * spread + s, 2)))
    at(stage_last + 4.0, table_finish, 1, 0.1)
    at(stage_last + 4.1, lambda: couple_all(beta_tab, beta_signs), 2, 1.0)

    help_ready = 0.0
    if helps:
        for q in range(PIECES):
            for h in range(2):
                time = START + max(
                    ends(len(early) - 1) + PIECE * (q + PIECES + 1) + HOP, PIECE * (q + chips) + HOP * (chips + 1))
                help_ready = max(help_ready, time + 1.5)
                for s in range(spread):
                    at(time + 0.5, functools.partial(help_arrive, s, h, q))
        at(help_ready, help_finish, 1, 0.1)
        at(help_ready + 0.1, lambda: pl.when(helper)(lambda: couple_all(help_tab, help_signs)), 1, 1.0)
        help_ready += 0.2

    order = [(0, 0), (1, 0), (0, 1), (1, 1), (2, 0), (3, 0), (2, 1), (3, 1)]
    own_place = dict(zip(order, (1, 2, 3, 4, 7, 8, 9, 11)))
    passed_place = (5, 6, 10, 12)
    held_back = {(2, 0): 1, (3, 0): 1, (2, 1): 1, (3, 1): 2}
    step = TILE / (2 * PARTS_A)

    classes = []
    for h in range(2):
        kind = jnp.int32(chips - 1)
        for s in range(spread):
            source_core, hops = table_places(s)
            kind = jnp.where(core == source_core, hops[h], kind)
        classes.append(kind)

    def ring_time(j, second, t):
        place = passed_place[j] if t else own_place[j, second]
        if place == 1:
            return stage_last - PIECE - HOP + 0.2
        if place == 2:
            return START + PIECE * (PIECES + max(chips - 2, 0)) + HOP * chips
        return START + PIECE * PIECES + step * place + 3.0 * HOP + 30.0 * max(t - 1, 0)

    for a, (j, second) in enumerate(order):
        for way in range(2):
            hb = (1 - way) if second else way
            for d in range(chips):
                time = 0.0
                if d < chips - 1 and a >= d + min(d, 1):
                    time = START + PIECE * (PIECES - 1 + d) + HOP * d + (3.55 if d > 1 else 0.05) if d else 0.0
                if (j, second) in held_back:
                    time = ring_time(held_back[j, second], 0, 0) + 0.1
                at(time, functools.partial(ring_own, j, hb, way, classes[way] == d))
            for t in range(reach):
                if carried(way, hb, t):
                    forwards = t + 1 < reach and carried(way, hb, t + 1)
                    at(ring_time(j, second, t) + (0.0 if forwards else 1.0),
                       functools.partial(ring_arrive, j, hb, way, t), 0 if forwards else 1, 0.03)
    for t in range(reach):
        count = high if t < reach - 1 else high // 2
        for way in range(2):
            drain(ring_time(PARTS_A - 1, 1, t) + 4.0, out.at[pl.ds(0, count)], ("ring", way, t))
            drain(ring_time(PARTS_A - 1, 1, t) + 8.0, out.at[pl.ds(0, count)], ("ringP", way, t))

    def own_pass(j):
        ref = colbuf[j].at[pl.ds(r * blocks, blocks)]
        send(ref, ref, ("own",), ("tiles", j), partner)

    def alpha_step(j):
        ring_finish(j)
        alpha_compute(j)
        alphas.append(j)
        if len(alphas) == PARTS_A:
            for entry in held:
                flush(*entry)

    for j in range(PARTS_A):
        at(0.5, functools.partial(own_pass, j))
        done = max(ring_time(j, 0, reach - 1), ring_time(j, 1, max(reach - 2, 0))) + (2.5 if j < 2 else 4.5)
        at(done, functools.partial(alpha_step, j), 4, 0.9)

    drain(25.0, out, ("own",))

    def prepare():
        out[...] = jnp.zeros_like(out)
        gather_pairs()
        widen(own_tab, 0, alpha_signs)

    at(0.6, prepare, 0, 4.0)

    groups = [[0], [1, 2], list(range(3, 10)), list(range(10, 17))]

    def finish_time(i, t):
        k = max(k for k, chunk in enumerate(chunks) if chunk[0] == i)
        return START - LEAD + 1.0 + arrival(t, k, helps and k not in early)

    def help_step(i):
        line_finish(i)
        help_beta(i)

    def own_step(group, finish, cond, turn=0, turns=1):
        if finish and not turn:
            for i in group:
                line_finish(i)
        span = (blocks_b * turn // turns, blocks_b * (turn + 1) // turns)
        own_beta(group, cond, span)
        if turn == turns - 1:
            flush(firsts[group[0]], sum(parts[i][0] for i in group), cond)

    for i, (height, helped) in enumerate(parts):
        if helped:
            ready = max(finish_time(i, max(cols - 3, 0)), help_ready)
            at(ready + 1.5, functools.partial(help_step, i), 2, 0.85)
            at(ready + 11.0, functools.partial(take_sums, i), 5, 0.0)
    if helps:
        drain(help_ready + TILE, shared, ("sums",), lambda: helper)
    for group in groups:
        inside, outside = finish_time(group[-1], max(cols - 3, 0)), finish_time(group[-1], cols - 2)
        if not helps:
            at(outside + 0.1, functools.partial(own_step, group, True, None), 6, 2.6)
            continue
        for turn in range(2):
            at((max(inside, help_ready) + 1.6 if parts[group[0]][1] else inside + 0.1) + 0.01 * turn,
               functools.partial(own_step, group, False, inner, turn, 2), 6, 0.8)
        if not parts[group[0]][1]:
            at(outside + 0.1, functools.partial(own_step, group, True, at_end), 6, 0.0)

    for action in in_order(plan):
        action()
    pltpu.make_async_copy(out, result, lsem.at[lsem.shape[0] - 1]).wait()
    assert len(numbers[0]) == ssem.shape[0] and len(numbers[1]) == rsem.shape[0]
    assert len(local) == lsem.shape[0] - 1


def local(vector, one_electron, links, counts, pairs, signs, rows, cols):
    blocks, link_max = pairs.shape
    size = signs.shape[2]
    high, width = vector.shape
    spread = rows // cols
    tables = blocks * link_max
    parts = row_parts(high, cols)
    helped = sum(height for height, aided in parts if aided)
    reach = rows // 4
    sends = rows - 1 + 2 * (cols - 1) + 4 * reach + 2 + spread * 3
    pieces = 2 * PIECES * ((spread + 1) // 2) + spread
    arrivals = rows - 1 + PARTS_A * (4 * reach - 1) + pieces + len(row_chunks(high, cols)) * (cols - 1)
    if cols >= 4:
        sends += 2 * (cols - 2) + spread * 2
        arrivals += pieces
    scratch = [pltpu.VMEM((rows * blocks, size, width // PARTS_A), jnp.float32)] * PARTS_A
    scratch += [pltpu.VMEM((cols * blocks * spread, height, size), jnp.float32) for height, _ in parts]
    scratch += [
        pltpu.VMEM((tables, size, size), jnp.int32),
        pltpu.VMEM((spread, tables, size, size), jnp.int32),
        pltpu.VMEM((spread, tables, size, size), jnp.int32),
        pltpu.VMEM((tables, size, 2 * size), jnp.bfloat16),
        pltpu.VMEM((spread * tables // 2, size, 2 * size), jnp.bfloat16),
        pltpu.VMEM((spread * tables // 2, size, 2 * size), jnp.bfloat16),
        pltpu.VMEM((max(helped, 8), width), jnp.float32),
        pltpu.VMEM((high, width), jnp.float32),
        pltpu.VMEM((rows, blocks, link_max), jnp.int32),
        pltpu.SMEM((rows, blocks, link_max), jnp.int32),
        pltpu.SMEM((link_max, links.shape[0]), jnp.int32),
        pltpu.SMEM(counts.shape, jnp.int32),
        pltpu.SMEM(one_electron.shape, jnp.float32),
        pltpu.SMEM((blocks, link_max), jnp.float32),
        pltpu.SMEM((blocks * spread, link_max), jnp.float32),
        pltpu.SMEM((blocks * spread, link_max), jnp.float32),
        pltpu.SemaphoreType.DMA((sends,)),
        pltpu.SemaphoreType.DMA((arrivals,)),
        pltpu.SemaphoreType.DMA((10 + spread,)),
    ]
    far = pl.BlockSpec(memory_space=pltpu.HBM)
    operands = (links.T, counts, one_electron, pairs, vector.reshape(blocks, size, width),
                signs.reshape(tables, size, size))
    return pl.pallas_call(
        functools.partial(kernel, rows, cols, blocks, link_max),
        out_shape=jax.ShapeDtypeStruct(vector.shape, jnp.float32),
        in_specs=[far] * 6,
        out_specs=pl.BlockSpec(memory_space=pl.ANY),
        scratch_shapes=scratch,
        compiler_params=pltpu.CompilerParams(
            collective_id=0, has_side_effects=True, vmem_limit_bytes=48 << 20),
    )(*[pltpu.with_memory_space_constraint(value, pltpu.HBM) for value in operands])


def solution(mesh):
    in_specs = (P("row", "col"), P(), P(), P(), P("row", None), P("row", None, None, None))
    out_specs = P("row", "col")
    body = functools.partial(local, rows=mesh.shape["row"], cols=mesh.shape["col"])
    return jax.shard_map(body, mesh=mesh, in_specs=in_specs, out_specs=out_specs, check_vma=False)
```

```python
import functools

import jax
import jax.numpy as jnp
from jax import lax
from jax.experimental import pallas as pl
from jax.experimental.pallas import tpu as pltpu
from jax.sharding import PartitionSpec as P

MESH = pl.DeviceIdType.MESH
PARTS_A = 4
PIECES = 4
START = 4.5
LEAD = 2.5
SLACK = 0.1
TILE = 45.0
HOP = 1.5
PIECE = 5.6


def split(value):
    high = value.astype(jnp.bfloat16)
    low = (value - high.astype(jnp.float32)).astype(jnp.bfloat16)
    return high, low


def row_parts(high, cols):
    helps = cols >= 4
    return [(high // 4, False)] * 2 + [(high // 16, False)] + [(high // 32, helps)] * 14


def row_chunks(high, cols):
    chunks, first = [], 0
    for part, (height, helped) in enumerate(row_parts(high, cols)):
        piece = min(height, high // 16 if part else high // 8)
        for offset in range(0, height, piece):
            chunks.append((part, offset, piece, first + offset, helped))
        first += height
    return chunks


def in_order(plan):
    left = sorted(enumerate(plan), key=lambda entry: (entry[1][0], entry[0]))
    urgent = [entry for entry in left if entry[1][1] <= 2]
    now, result = 0.0, []
    while left:
        ready = [entry for entry in left if entry[1][0] <= now]
        soon = [entry for entry in urgent if entry[1][0] > now][:1]
        if soon:
            room = soon[0][1][0] - now + SLACK
            ready = [entry for entry in ready if entry[1][1] <= 2 or entry[1][2] <= room]
        if not ready:
            now = min(entry[1][0] for entry in (soon or left))
            ready = [entry for entry in left if entry[1][0] <= now and entry[1][1] <= 2] or left[:1]
        chosen = min(ready, key=lambda entry: (entry[1][1], entry[1][0], entry[0]))
        left.remove(chosen)
        if chosen[1][1] <= 2:
            urgent.remove(chosen)
        start, _, length, action = chosen[1]
        now = max(now, start) + length
        result.append(action)
    return result


def kernel(rows, cols, blocks, link_max, links_in, counts_in, integrals_in, pairs, v, tab, result, *scratch):
    size = tab.shape[1]
    high, width = result.shape
    parts = row_parts(high, cols)
    chunks = row_chunks(high, cols)
    firsts = [sum(p[0] for p in parts[:i]) for i in range(len(parts))]
    scratch = list(scratch)
    colbuf = [scratch.pop(0) for _ in range(PARTS_A)]
    rowbuf = [scratch.pop(0) for _ in parts]
    (own_tab, beta_tab, help_tab, alpha_signs, beta_signs, help_signs, shared,
     out, pairs_v, pairs_s, links, counts, integrals, alpha_coef, beta_coef, help_coef,
     ssem, rsem, lsem) = scratch

    wide = width // PARTS_A
    spread = rows // cols
    blocks_b = blocks * spread
    tables = blocks * link_max
    chips = rows // 2
    reach = chips // 2
    across = chips // 2
    half = blocks // 2
    piece = tables // (2 * PIECES)
    helps = cols >= 4
    early = [k for k, chunk in enumerate(chunks) if chunk[0] < 3]

    r = lax.axis_index("row")
    c = lax.axis_index("col")
    core = lax.rem(r, 2)
    chip = r // 2
    other = r + 1 - 2 * core
    place = jnp.where(chip < across, chip, chips - 1 - (chip - across))

    def chip_at(position):
        position = lax.rem(position + 2 * chips, chips)
        return jnp.where(position < across, position, across + (chips - 1 - position))

    def row_at(position, k):
        return 2 * chip_at(position) + k

    right = (row_at(place + 1, core), c)
    left = (row_at(place - 1, core), c)
    partner = (other, c)
    up = (r, jnp.minimum(c + 1, cols - 1))
    down = (r, jnp.maximum(c - 1, 0))
    has_up = c < cols - 1
    has_down = c > 0
    at_end = (c == 0) | (c == cols - 1)
    inner = jnp.logical_not(at_end)
    helper = (c == 1) | (c == cols - 2)
    aided = jnp.where(c == 1, 0, cols - 1)
    inward = (r, jnp.where(c == 0, 1, cols - 2))

    numbers = ({}, {})

    def number(side, key):
        return numbers[side].setdefault(key, len(numbers[side]))

    plan = []

    def at(time, action, rank=0, length=0.0):
        plan.append((time, rank, length, action))

    def describe(src, dst, group, key, device):
        return pltpu.make_async_remote_copy(
            src_ref=src, dst_ref=dst, send_sem=ssem.at[number(0, group)], recv_sem=rsem.at[number(1, key)],
            device_id=device, device_id_type=MESH)

    def when(cond, action):
        if cond is None:
            action()
        else:
            pl.when(cond)(action)

    def send(src, dst, group, key, device, cond=None):
        when(cond, describe(src, dst, group, key, device).start)

    def arrive(ref, key, cond=None):
        when(cond, pltpu.make_async_copy(ref, ref, rsem.at[number(1, key)]).wait)

    def drain(time, ref, group, cond=None):
        def action():
            wait = pltpu.make_async_copy(ref, ref, ssem.at[number(0, group)]).wait
            when(cond() if cond else None, wait)
        at(time, action, 9, 0.02)

    local = []

    def load(src, dst, cond=None):
        copy = pltpu.make_async_copy(src, dst, lsem.at[len(local)])
        local.append(copy)
        when(cond, copy.start)
        return lambda: when(cond, copy.wait)

    barrier = pltpu.get_barrier_semaphore()
    for k in range(1, rows):
        pl.semaphore_signal(barrier, inc=1, device_id=(lax.rem(r + k, rows), c), device_id_type=MESH)

    @pl.when(has_up)
    def _():
        pl.semaphore_signal(barrier, inc=1, device_id=up, device_id_type=MESH)

    @pl.when(has_down)
    def _():
        pl.semaphore_signal(barrier, inc=1, device_id=down, device_id_type=MESH)

    wait_small = [load(pairs, pairs_v.at[r]), load(links_in, links), load(counts_in, counts),
                  load(integrals_in, integrals)]

    def load_rows(group):
        sem = lsem.at[len(local)]
        for i in group:
            first = firsts[i]
            for k in range(blocks_b):
                pltpu.make_async_copy(
                    v.at[first // size, pl.ds(first % size, parts[i][0]), pl.ds(k * size, size)],
                    rowbuf[i].at[c * blocks_b + k], sem).start()
        ref = out.at[pl.ds(0, sum(parts[i][0] for i in group))]
        local.append(pltpu.make_async_copy(ref, ref, sem))
        return local[-1].wait

    wait_rows = {group[0]: load_rows(group) for group in ([0], [1], range(2, len(parts)))}
    wait_tab = load(tab, own_tab)
    for j in range(PARTS_A):
        pltpu.make_async_copy(v.at[:, :, pl.ds(j * wide, wide)], colbuf[j].at[pl.ds(r * blocks, blocks)],
                              lsem.at[len(local)]).start()
    local.append(pltpu.make_async_copy(out, out, lsem.at[len(local)]))
    wait_cols = local[-1].wait

    pl.semaphore_wait(barrier, rows - 1 + has_up.astype(jnp.int32) + has_down.astype(jnp.int32))

    for k in range(1, rows):
        send(pairs, pairs_v.at[r], ("pairs", k), ("pairs", k), (lax.rem(r + k, rows), c))
        drain(15.0, pairs_v.at[r], ("pairs", k))

    reach_up = {1: up, -1: down}

    def ends(k):
        return TILE * (chunks[k][3] + chunks[k][2]) / high

    def arrival(t, k, late):
        far = max(cols - 3, 1)
        tiles = max(1, min(t, far)) if late else min(t, far)
        length = TILE * chunks[k][2] / high
        return ends(k) + TILE * tiles + HOP + (length + HOP) * (t if late else max(t - far, 0))

    def line_key(k, way, t):
        return "line", k, way * (1 + t) % cols

    def row_chunk(k, tile):
        part, offset, count, _, _ = chunks[k]
        return rowbuf[part].at[pl.ds(tile * blocks_b, blocks_b), pl.ds(offset, count), :]

    def line_own(k, way, cond):
        helped = chunks[k][4]
        position = c if way == 1 else cols - 1 - c
        limit = cols - 2 if helped else cols - 1
        ref = row_chunk(k, c)
        send(ref, ref, ("line", way, 0, helped), line_key(k, way, 0), reach_up[way], cond & (position < limit))

    def line_arrive(k, way, t, edge, forward):
        helped = chunks[k][4]
        last = cols - 2 if helped else cols - 1
        onward = t + 2 <= last if edge else t + 3 <= last
        if onward != forward or (t + 1 > last if edge else t + 2 > last):
            return
        position = c if way == 1 else cols - 1 - c
        cond = position == t + 1 if edge else (position > t + 1) & (position <= last)
        ref = row_chunk(k, jnp.clip(c - way * (1 + t), 0, cols - 1))
        arrive(ref, line_key(k, way, t), cond)
        if onward:
            send(ref, ref, ("line", way, t + 1, helped), line_key(k, way, t + 1), reach_up[way],
                 cond if edge else cond & (position < last))

    def line_finish(i):
        for k, chunk in enumerate(chunks):
            if chunk[0] == i:
                for way in (1, -1):
                    for t in range(cols - 1):
                        for edge in (False, True):
                            line_arrive(k, way, t, edge, False)

    def table_places(s):
        source = c * spread + s
        source_chip = source // 2
        source_place = jnp.where(
            source_chip < across, source_chip, chips - 1 - (source_chip - across))
        distance = lax.rem(place - source_place + chips, chips)
        return lax.rem(source, 2), (distance, lax.rem(chips - distance, chips))

    ring = (right, left)

    def table_part(h, q):
        return pl.ds((h * PIECES + q) * piece, piece)

    def table_stage(s, h, q, d):
        source_core, hops = table_places(s)
        here = (core == source_core) & (hops[h] == d)
        part = table_part(h, q)
        ref = beta_tab.at[s, part]
        src = ref if d else own_tab.at[part]
        if d:
            arrive(ref, ("table", s // 2, h, q), here)
        if d + 1 < chips:
            send(src, ref, ("table", s, h), ("table", s // 2, h, q), ring[h], here)
        send(src, ref, ("tableP", s), ("tableP", s), partner, here)
        if helps:
            send(src, help_tab.at[s, part], ("help", s), ("help", s // 2, h, q), inward, here & at_end)

    def table_finish():
        for s in range(spread):
            source_core, _ = table_places(s)
            arrive(beta_tab.at[s], ("tableP", s), core != source_core)
            table_loads[s]()

    def help_arrive(s, h, q):
        source_core = table_places(s)[0]
        aided_core = lax.rem(aided * spread + s, 2)
        ref = help_tab.at[s, table_part(h, q)]
        arrive(ref, ("help", s // 2, h, q), helper & (core == aided_core))
        send(ref, ref, ("helpP", s), ("helpP", s), partner, helper & (core == aided_core))

    def help_finish():
        for s in range(spread):
            aided_core = lax.rem(aided * spread + s, 2)
            arrive(help_tab.at[s], ("helpP", s), helper & (core != aided_core))

    def narrow(value):
        return value.astype(jnp.float32).astype(jnp.bfloat16)

    def widen(source, base, target):
        @pl.loop(0, tables)
        def _(index):
            values = narrow(source[index])
            target[base + index] = jnp.concatenate([values, values], axis=1)

    def couple(source, base, target):
        @pl.loop(0, tables // 2)
        def _(index):
            target[base + index] = jnp.concatenate(
                [narrow(source[2 * index]), narrow(source[2 * index + 1])], axis=1)

    def couple_all(source, target):
        for s in range(spread):
            couple(source.at[s], s * (tables // 2), target)

    def tile_half(j, hb, position, k):
        return colbuf[j].at[pl.ds(row_at(position, k) * blocks + hb * half, half)]

    def ring_own(j, hb, way, cond):
        ref = colbuf[j].at[pl.ds(r * blocks + hb * half, half)]
        send(ref, ref, ("ring", way, 0), ("ring", way, j, hb, 0), ring[way], cond)

    def carried(way, hb, t):
        return t < reach - 1 or hb == way

    def ring_arrive(j, hb, way, t):
        ref = tile_half(j, hb, place - 1 - t if way == 0 else place + 1 + t, core)
        arrive(ref, ("ring", way, j, hb, t))
        if t + 1 < reach and carried(way, hb, t + 1):
            send(ref, ref, ("ring", way, t + 1), ("ring", way, j, hb, t + 1), ring[way])
        send(ref, ref, ("ringP", way, t), ("tiles", j), partner)

    def ring_finish(j):
        arrive(colbuf[j].at[pl.ds(0, chips * blocks)], ("tiles", j))

    def coefficients(target, first, count):
        @pl.loop(0, count)
        def _(b):
            block = first + b
            for l in range(link_max):
                pair = pairs_s[lax.div(block, blocks), lax.rem(block, blocks), l]
                norb = integrals.shape[0]
                value = integrals[lax.div(pair, norb), lax.rem(pair, norb)]
                target[b, l] = value * jnp.clip(counts[block] - l, 0, 1).astype(jnp.float32)

    def gather_pairs():
        for wait in wait_small:
            wait()
        for k in range(1, rows):
            arrive(pairs_v.at[lax.rem(r - k + rows, rows)], ("pairs", k))
        copy = pltpu.make_async_copy(pairs_v, pairs_s, lsem.at[0])
        copy.start()
        copy.wait()
        coefficients(alpha_coef, r * blocks, blocks)
        coefficients(beta_coef, c * blocks_b, blocks_b)
        if helps:
            coefficients(help_coef, aided * blocks_b, blocks_b)

    def trips(first, last, body):
        together = max(u for u in (4, 2, 1) if (last - first) % u == 0)

        @pl.loop(0, (last - first) // together)
        def _(trip):
            for turn in range(together):
                body(first + trip * together + turn)

    def alpha_compute(j):
        def body(block):
            total = None
            for l in range(link_max):
                source = links[l, r * blocks + block]
                up_part, low_part = split(colbuf[j][source] * alpha_coef[block, l])
                term = jnp.dot(
                    alpha_signs[block * link_max + l], jnp.concatenate([up_part, low_part], axis=0),
                    preferred_element_type=jnp.float32)
                total = term if total is None else total + term
            where = (pl.ds(pl.multiple_of(block * size, size), size), pl.ds(j * wide, wide))
            out[where] = out[where] + total

        trips(0, blocks, body)

    def beta_compute(group, owner, coef, signs, target, start, add, span=None):
        count = sum(parts[i][0] for i in group)

        def body(block):
            total = None
            for l in range(0, link_max, 2):
                highs, lows = [], []
                for m in (l, l + 1):
                    source = links[m, owner * blocks_b + block]
                    value = jnp.concatenate([rowbuf[i][source] for i in group], axis=0)
                    up_part, low_part = split(value * coef[block, m])
                    highs.append(up_part)
                    lows.append(low_part)
                value = jnp.concatenate(
                    [jnp.concatenate(highs, axis=1), jnp.concatenate(lows, axis=1)], axis=0)
                term = lax.dot_general(
                    value, signs[block * (link_max // 2) + l // 2],
                    (((1,), (1,)), ((), ())), preferred_element_type=jnp.float32)
                total = term if total is None else total + term
            total = total[:count] + total[count:]
            where = (pl.ds(start, count), pl.ds(pl.multiple_of(block * size, size), size))
            if add:
                total = target[where] + total
            target[where] = total

        trips(*(span or (0, blocks_b)), body)

    shared_first = sum(height for height, helped in parts if not helped)

    def own_beta(group, cond, span):
        def action():
            beta_compute(group, c, beta_coef, beta_signs, out, firsts[group[0]], True, span)
        when(cond, action)

    def sums_key(i):
        return line_key(next(k for k, chunk in enumerate(chunks) if chunk[0] == i), 1, 0)

    def help_beta(i):
        @pl.when(helper)
        def _():
            beta_compute([i], aided, help_coef, help_signs, shared, firsts[i] - shared_first, False)

        ref = shared.at[pl.ds(firsts[i] - shared_first, parts[i][0])]
        send(ref, ref, ("sums",), sums_key(i), (r, aided), helper)

    def take_sums(i):
        ref = shared.at[pl.ds(firsts[i] - shared_first, parts[i][0])]
        arrive(ref, sums_key(i), at_end)

        @pl.when(at_end)
        def _():
            where = pl.ds(firsts[i], parts[i][0])
            out[where, :] = out[where, :] + ref[...]

        flush(firsts[i], parts[i][0], at_end)

    held, alphas = [], []

    def flush(first, count, cond):
        if len(alphas) < PARTS_A:
            held.append((first, count, cond))
            return
        where = pl.ds(first, count)
        when(cond, pltpu.make_async_copy(out.at[where], result.at[where], lsem.at[lsem.shape[0] - 1]).start)

    table_loads = []

    def begin():
        always = jnp.bool_(True)
        for k in range(len(chunks)):
            if chunks[k][1] == 0 and chunks[k][0] in wait_rows:
                wait_rows[chunks[k][0]]()
            first = k in early or not helps
            line_own(k, 1, always if first else has_down)
            line_own(k, -1, always if first else has_up)
        wait_tab()

    def begin_tables():
        for s in range(spread):
            source_core, hops = table_places(s)
            table_loads.append(load(tab, beta_tab.at[s], (core == source_core) & (hops[0] == 0)))

    def begin_tiles():
        wait_cols()

    at(-4.0, begin)
    at(-2.0, begin_tables)
    at(-1.5, begin_tiles)

    def rest():
        for k in range(len(early), len(chunks)):
            line_own(k, 1, c == 0)
            line_own(k, -1, c == cols - 1)

    stage_last = START + PIECE * (PIECES - 1 + chips - 1) + HOP * (chips - 1) + 3.5
    if helps:
        at(stage_last + 0.1, rest)

    for k in range(len(chunks)):
        helped = chunks[k][4]
        late_k = helps and k not in early
        for way in (1, -1):
            for t in range(cols - 1):
                for edge in (False, True):
                    late = edge and late_k
                    at(START - LEAD + arrival(t, k, late) + (1.5 if t else 0.0),
                       functools.partial(line_arrive, k, way, t, edge, True))

    for helped in (False, True) if helps else (False,):
        count = sum(height for height, aided_part in parts if aided_part == helped)
        last_k = max(k for k, chunk in enumerate(chunks) if chunk[4] == helped)
        last = cols - 2 if helped else cols - 1
        for way in (1, -1):
            for t in range(last):
                def cond(t=t, way=way, last=last):
                    position = c if way == 1 else cols - 1 - c
                    return (position >= t) & (position < last)

                sent = START + arrival(t, last_k, helps and last_k not in early) + (TILE if t == 0 else 0.0)
                drain(sent + 6.0, out.at[pl.ds(0, count)], ("line", way, t, helped), cond)

    for q in range(PIECES):
        for h in range(2):
            for s in range(spread):
                for d in range(chips):
                    time = -1.0 if d == 0 else START + PIECE * (q + d) + HOP * d + (3.5 if d > 1 else 0.0)
                    at(time, functools.partial(table_stage, s, h, q, d))
    for s in range(spread):
        def mine(s=s):
            return core == table_places(s)[0]

        for h in range(2):
            drain(stage_last + 12.0, beta_tab.at[s, pl.ds(0, tables // 2)], ("table", s, h),
                  lambda s=s, h=h: mine(s) & (table_places(s)[1][h] < chips - 1))
        drain(stage_last + 12.0, beta_tab.at[s], ("tableP", s), mine)
        if helps:
            drain(START + 1.8 * TILE, beta_tab.at[s], ("help", s), lambda s=s: mine(s) & at_end)
            drain(START + 1.8 * TILE, beta_tab.at[s], ("helpP", s),
                  lambda s=s: helper & (core == lax.rem(aided * spread + s, 2)))
    at(stage_last + 4.0, table_finish, 1, 0.1)
    at(stage_last + 4.1, lambda: couple_all(beta_tab, beta_signs), 2, 1.0)

    help_ready = 0.0
    if helps:
        for q in range(PIECES):
            for h in range(2):
                time = START + max(
                    ends(len(early) - 1) + PIECE * (q + PIECES + 1) + HOP, PIECE * (q + chips) + HOP * (chips + 1))
                help_ready = max(help_ready, time + 1.5)
                for s in range(spread):
                    at(time + 0.5, functools.partial(help_arrive, s, h, q))
        at(help_ready, help_finish, 1, 0.1)
        at(help_ready + 0.1, lambda: pl.when(helper)(lambda: couple_all(help_tab, help_signs)), 1, 1.0)
        help_ready += 0.2

    order = [(0, 0), (1, 0), (0, 1), (1, 1), (2, 0), (3, 0), (2, 1), (3, 1)]
    own_place = dict(zip(order, (1, 2, 3, 4, 7, 8, 9, 11)))
    passed_place = (5, 6, 10, 12)
    held_back = {(2, 0): 1, (3, 0): 1, (2, 1): 1, (3, 1): 2}
    step = TILE / (2 * PARTS_A)

    classes = []
    for h in range(2):
        kind = jnp.int32(chips - 1)
        for s in range(spread):
            source_core, hops = table_places(s)
            kind = jnp.where(core == source_core, hops[h], kind)
        classes.append(kind)

    def ring_time(j, second, t):
        place = passed_place[j] if t else own_place[j, second]
        if place == 1:
            return stage_last - PIECE - HOP + 0.2
        if place == 2:
            return START + PIECE * (PIECES + max(chips - 2, 0)) + HOP * chips
        return START + PIECE * PIECES + step * place + (3.0 if place < 12 else 1.5) * HOP + 30.0 * max(t - 1, 0)

    for a, (j, second) in enumerate(order):
        for way in range(2):
            hb = (1 - way) if second else way
            for d in range(chips):
                time = 0.0
                if d < chips - 1 and a >= d + min(d, 1):
                    time = START + PIECE * (PIECES - 1 + d) + HOP * d + (3.55 if d > 1 else 0.05) if d else 0.0
                if (j, second) in held_back:
                    time = ring_time(held_back[j, second], 0, 0) + 0.1
                at(time, functools.partial(ring_own, j, hb, way, classes[way] == d))
            for t in range(reach):
                if carried(way, hb, t):
                    forwards = t + 1 < reach and carried(way, hb, t + 1)
                    at(ring_time(j, second, t) + (0.0 if forwards else 1.0),
                       functools.partial(ring_arrive, j, hb, way, t), 0 if forwards else 1, 0.03)
    for t in range(reach):
        count = high if t < reach - 1 else high // 2
        for way in range(2):
            drain(ring_time(PARTS_A - 1, 1, t) + 4.0, out.at[pl.ds(0, count)], ("ring", way, t))
            drain(ring_time(PARTS_A - 1, 1, t) + 8.0, out.at[pl.ds(0, count)], ("ringP", way, t))

    def own_pass(j):
        ref = colbuf[j].at[pl.ds(r * blocks, blocks)]
        send(ref, ref, ("own",), ("tiles", j), partner)

    def alpha_step(j):
        ring_finish(j)
        alpha_compute(j)
        alphas.append(j)
        if len(alphas) == PARTS_A:
            for entry in held:
                flush(*entry)

    for j in range(PARTS_A):
        at(0.5, functools.partial(own_pass, j))
        done = max(ring_time(j, 0, reach - 1), ring_time(j, 1, max(reach - 2, 0))) + (2.5 if j < 2 else 4.5)
        at(done, functools.partial(alpha_step, j), 4, 0.9)

    drain(25.0, out, ("own",))

    def prepare():
        out[...] = jnp.zeros_like(out)
        gather_pairs()
        widen(own_tab, 0, alpha_signs)

    at(0.6, prepare, 0, 4.0)

    groups = [[0], [1, 2], list(range(3, 10)), list(range(10, 17))]

    def finish_time(i, t):
        k = max(k for k, chunk in enumerate(chunks) if chunk[0] == i)
        return START - LEAD + 1.0 + arrival(t, k, helps and k not in early)

    def help_step(i):
        line_finish(i)
        help_beta(i)

    def own_step(group, finish, cond, turn=0, turns=1):
        if finish and not turn:
            for i in group:
                line_finish(i)
        span = (blocks_b * turn // turns, blocks_b * (turn + 1) // turns)
        own_beta(group, cond, span)
        if turn == turns - 1:
            flush(firsts[group[0]], sum(parts[i][0] for i in group), cond)

    for i, (height, helped) in enumerate(parts):
        if helped:
            ready = max(finish_time(i, max(cols - 3, 0)), help_ready)
            at(ready + 1.5, functools.partial(help_step, i), 2, 0.85)
            at(ready + 11.0, functools.partial(take_sums, i), 5, 0.0)
    if helps:
        drain(help_ready + TILE, shared, ("sums",), lambda: helper)
    for group in groups:
        inside, outside = finish_time(group[-1], max(cols - 3, 0)), finish_time(group[-1], cols - 2)
        if not helps:
            at(outside + 0.1, functools.partial(own_step, group, True, None), 6, 2.6)
            continue
        for turn in range(2):
            at((max(inside, help_ready) + 1.6 if parts[group[0]][1] else inside + 0.1) + 0.01 * turn,
               functools.partial(own_step, group, False, inner, turn, 2), 6, 0.8)
        if not parts[group[0]][1]:
            at(outside + 0.1, functools.partial(own_step, group, True, at_end), 6, 0.0)

    for action in in_order(plan):
        action()
    pltpu.make_async_copy(out, result, lsem.at[lsem.shape[0] - 1]).wait()
    assert len(numbers[0]) == ssem.shape[0] and len(numbers[1]) == rsem.shape[0]
    assert len(local) == lsem.shape[0] - 1


def local(vector, one_electron, links, counts, pairs, signs, rows, cols):
    blocks, link_max = pairs.shape
    size = signs.shape[2]
    high, width = vector.shape
    spread = rows // cols
    tables = blocks * link_max
    parts = row_parts(high, cols)
    helped = sum(height for height, aided in parts if aided)
    reach = rows // 4
    sends = rows - 1 + 2 * (cols - 1) + 4 * reach + 2 + spread * 3
    pieces = 2 * PIECES * ((spread + 1) // 2) + spread
    arrivals = rows - 1 + PARTS_A * (4 * reach - 1) + pieces + len(row_chunks(high, cols)) * (cols - 1)
    if cols >= 4:
        sends += 2 * (cols - 2) + spread * 2
        arrivals += pieces
    scratch = [pltpu.VMEM((rows * blocks, size, width // PARTS_A), jnp.float32)] * PARTS_A
    scratch += [pltpu.VMEM((cols * blocks * spread, height, size), jnp.float32) for height, _ in parts]
    scratch += [
        pltpu.VMEM((tables, size, size), jnp.int32),
        pltpu.VMEM((spread, tables, size, size), jnp.int32),
        pltpu.VMEM((spread, tables, size, size), jnp.int32),
        pltpu.VMEM((tables, size, 2 * size), jnp.bfloat16),
        pltpu.VMEM((spread * tables // 2, size, 2 * size), jnp.bfloat16),
        pltpu.VMEM((spread * tables // 2, size, 2 * size), jnp.bfloat16),
        pltpu.VMEM((max(helped, 8), width), jnp.float32),
        pltpu.VMEM((high, width), jnp.float32),
        pltpu.VMEM((rows, blocks, link_max), jnp.int32),
        pltpu.SMEM((rows, blocks, link_max), jnp.int32),
        pltpu.SMEM((link_max, links.shape[0]), jnp.int32),
        pltpu.SMEM(counts.shape, jnp.int32),
        pltpu.SMEM(one_electron.shape, jnp.float32),
        pltpu.SMEM((blocks, link_max), jnp.float32),
        pltpu.SMEM((blocks * spread, link_max), jnp.float32),
        pltpu.SMEM((blocks * spread, link_max), jnp.float32),
        pltpu.SemaphoreType.DMA((sends,)),
        pltpu.SemaphoreType.DMA((arrivals,)),
        pltpu.SemaphoreType.DMA((10 + spread,)),
    ]
    far = pl.BlockSpec(memory_space=pltpu.HBM)
    operands = (links.T, counts, one_electron, pairs, vector.reshape(blocks, size, width),
                signs.reshape(tables, size, size))
    return pl.pallas_call(
        functools.partial(kernel, rows, cols, blocks, link_max),
        out_shape=jax.ShapeDtypeStruct(vector.shape, jnp.float32),
        in_specs=[far] * 6,
        out_specs=pl.BlockSpec(memory_space=pl.ANY),
        scratch_shapes=scratch,
        compiler_params=pltpu.CompilerParams(
            collective_id=0, has_side_effects=True, vmem_limit_bytes=48 << 20),
    )(*[pltpu.with_memory_space_constraint(value, pltpu.HBM) for value in operands])


def solution(mesh):
    in_specs = (P("row", "col"), P(), P(), P(), P("row", None), P("row", None, None, None))
    out_specs = P("row", "col")
    body = functools.partial(local, rows=mesh.shape["row"], cols=mesh.shape["col"])
    return jax.shard_map(body, mesh=mesh, in_specs=in_specs, out_specs=out_specs, check_vma=False)
```
